128 devices in a mesh: atoms: 128 (over y, x, z, core).
Axes of the slice: x: 4, y: 4, z: 4, core: 2. Of those that a mesh axis runs over, the one named last changes fastest.
Arguments:
- features: bfloat16 [16384, 9, 128], P('atoms'), may hold values from -6 to 6
- cotangent: bfloat16 [16384, 9, 128], P('atoms'), may hold values from -6 to 6
- wigner: float32 [9, 9, 49152], P(None, None, 'atoms'), may hold values from -1 to 1, as said below
- pair_blocks: int32 [2048, 2], P('atoms'), may hold values from 0 to 127, all different within a row; in each aligned block of 16 rows (0 to 15, 16 to 31, ...) at most 2 rows name the same one
- pair_rows: int32 [2, 6, 2048], P(None, None, 'atoms'), may hold values from 0 to 127
- edge_ends: int32 [2, 49152], P(None, 'atoms'), may hold values from 0 to 5
- first_m0: bfloat16 [768, 512], replicated, may hold values from -0.21875 to 0.21875
- first_m1: bfloat16 [2, 512, 256], replicated, may hold values from -0.1875 to 0.1875
- first_m2: bfloat16 [2, 256, 128], replicated, may hold values from -0.25 to 0.25
- second_m0: bfloat16 [384, 384], replicated, may hold values from -0.3125 to 0.3125
- second_m1: bfloat16 [2, 256, 256], replicated, may hold values from -0.25 to 0.25
- second_m2: bfloat16 [2, 128, 128], replicated, may hold values from -0.375 to 0.375
Outputs:
- messages: bfloat16 [16384, 9, 128], P('atoms')
- grad_features: float32 [16384, 9, 128], P('atoms')
- grad_first_m0: float32 [768, 512], replicated
- grad_first_m1: float32 [2, 512, 256], replicated
- grad_first_m2: float32 [2, 256, 128], replicated
- grad_second_m0: float32 [384, 384], replicated
- grad_second_m1: float32 [2, 256, 256], replicated
- grad_second_m2: float32 [2, 128, 128], replicated
The draws below stay inside these ranges and needn't reach their ends.
Inputs may be any that keep to these rules, and one draw needn't show every extreme that they name: `pair_blocks`: among the 16 pairs of one device no atom block is named more than 2 times; the two blocks of a pair differ. `wigner`: each edge's matrix is orthogonal and block diagonal over degrees 0, 1 and 2.
All inputs are finite; a program needn't handle non-finite values.
Results may differ from the reference program's by a relative error of at most 0.0045.
Values may be sent and summed in bfloat16 or wider, within the bound.
No kernel may reach another device: no remote copies, remote signals or barrier semaphores. Data moves between devices by JAX's collectives and lax.ppermute only.
A program may use at most 128 MiB of HBM per device.

```python
import math
import jax
import jax.numpy as jnp
import numpy as np
from jax import lax

C = 128
COEF = 9
BLK = 128
RPP = 6
EPP = 24
PAIRS_DEV = 16
MOST = 2
ATOMS = 16384
PAIRS = 2048
EDGES = 49152
N_ATOMS = 128


def quad_table():
    table = np.zeros((5, 3, 3), dtype=np.float32)
    root_half = 1.0 / np.sqrt(2.0)
    table[0, 0, 1] = root_half
    table[0, 1, 0] = root_half
    table[1, 1, 2] = root_half
    table[1, 2, 1] = root_half
    table[2, 0, 0] = -1.0 / np.sqrt(6.0)
    table[2, 1, 1] = -1.0 / np.sqrt(6.0)
    table[2, 2, 2] = 2.0 / np.sqrt(6.0)
    table[3, 0, 2] = root_half
    table[3, 2, 0] = root_half
    table[4, 0, 0] = root_half
    table[4, 1, 1] = -root_half
    return table


def draw_wigner(key, part):
    quaternion = jax.random.normal(key, (4, EDGES), jnp.float32)
    quaternion = quaternion / jnp.sqrt(jnp.sum(quaternion * quaternion, axis=0, keepdims=True) + 1e-12)
    qw = quaternion[0]
    qx = quaternion[1]
    qy = quaternion[2]
    qz = quaternion[3]
    rotation = jnp.stack([jnp.stack([1.0 - 2.0 * (qy * qy + qz * qz), 2.0 * (qx * qy - qz * qw), 2.0 * (qx * qz + qy * qw)]), jnp.stack([2.0 * (qx * qy + qz * qw), 1.0 - 2.0 * (qx * qx + qz * qz), 2.0 * (qy * qz - qx * qw)]), jnp.stack([2.0 * (qx * qz - qy * qw), 2.0 * (qy * qz + qx * qw), 1.0 - 2.0 * (qx * qx + qy * qy)])])
    axis_order = jnp.array([1, 2, 0], dtype=jnp.int32)
    first_degree = jnp.take(jnp.take(rotation, axis_order, axis=0), axis_order, axis=1)
    quad_basis = jnp.array(quad_table())
    second_degree = jnp.einsum('aij,jke,bkl,ile->abe', quad_basis, rotation, quad_basis, rotation)
    assembled = jnp.zeros((9, 9, EDGES), jnp.float32)
    assembled = assembled.at[0, 0].set(1.0)
    assembled = assembled.at[1:4, 1:4].set(first_degree)
    assembled = assembled.at[4:9, 4:9].set(second_degree)
    return assembled


def set_ends(result, stream_key, least, largest):
    longest = result.shape.index(max(result.shape))
    spots = []
    for shift in (0, 1):
        where = [jax.random.randint(jax.random.fold_in(stream_key, axis), (), 0, length) for axis, length in enumerate(result.shape)]
        where[longest] = (where[longest] + shift) % result.shape[longest]
        spots.append(tuple(where))
    return result.at[spots[0]].set(least).at[spots[1]].set(largest)


def levels(own_key, extent, pieces, low, high):
    gain = 1.0
    for axis_at, shards_of in pieces:
        draws = jax.random.uniform(jax.random.fold_in(jax.random.fold_in(own_key, 6), axis_at), (shards_of,), jnp.float32, low / len(pieces), high / len(pieces))
        gain = gain * jnp.repeat(jnp.exp(draws), extent[axis_at] // shards_of).reshape((-1,) + (1,) * (len(extent) - 1 - axis_at))
    return gain


def shared_out(own_key, own, number, rows, count, top, reach, slope):
    sequence = jax.random.permutation(own_key, count)
    crowded, common = load_shares(count, rows * top, reach, slope, True), load_shares(count, rows * top, reach, slope, False)
    places = jnp.arange(count)

    def named(sizes, turn):
        used = int((sizes > 0).sum())
        fixed = max(1, used // 4)
        passed = fixed + (places - fixed + turn * (used - fixed)) % max(1, count - fixed)
        return jnp.zeros((count,), jnp.int32).at[sequence[jnp.where(places < fixed, places, passed)]].set(jnp.asarray(sizes, jnp.int32))

    sizes = jnp.where(number % 4 == 0, named(crowded, number // 4), named(common, number - number // 4 - 1))
    mixed = jax.random.permutation(jax.random.fold_in(own, 3), count)
    donor, receiver = mixed[0:count // 2 * 2:2], mixed[1:count // 2 * 2:2]
    slack = jnp.minimum(sizes[donor] - 1, reach - sizes[receiver]) // 2
    slack = jnp.where((donor == sequence[0]) | (receiver == sequence[0]) | (sizes[receiver] == 0), 0, jnp.maximum(slack, 0))
    passed = jax.random.randint(jax.random.fold_in(own, 4), (count // 2,), 0, 1 << 20) % (slack + 1)
    sizes = sizes.at[donor].add(-passed).at[receiver].add(passed)
    members = jnp.searchsorted(jnp.cumsum(sizes), jnp.arange(rows * top), side="right").astype(jnp.int32)
    grid = members.reshape(top, rows).T
    grid = grid[jax.random.permutation(jax.random.fold_in(own, 1), rows)]
    turn = jax.random.randint(jax.random.fold_in(own, 2), (rows, 1), 0, top)
    return jnp.take_along_axis(grid, (jnp.arange(top)[None, :] + turn) % top, axis=1)


def load_shares(count, total, reach, lean, full):
    loads = [(1 << 20) // math.isqrt(grade ** lean) + 1 for grade in range(1, count + 1)]
    largest = reach if full else min(reach, max(-(-total // count), total * loads[0] // sum(loads)))
    least = 1 if total - largest >= count - 1 else 0
    given, rest = [largest] + [least] * (count - 1), total - largest - least * (count - 1)
    while rest > 0:
        free = [i for i in range(1, count) if given[i] < largest] or [i for i in range(1, count) if given[i] < reach]
        whole, remaining = sum([loads[i] for i in free]), rest
        for i in free:
            extra = min(reach - given[i], max(1, remaining * loads[i] // whole), rest)
            given[i] = given[i] + extra
            rest = rest - extra
    return np.array(given)


def noise(own_key, shape, spread, limit, split=(), held_as=jnp.bfloat16):
    level = levels(own_key, shape, split, -0.22, 0.18) if split else 1.0
    result = jax.random.normal(own_key, shape, jnp.float32) * spread * level
    return jnp.minimum(jnp.maximum(result, -limit), limit).astype(held_as)


def setup_inputs(seed: int = 0) -> dict:
    keys = jax.random.split(jax.random.key(seed), 13)
    features = noise(keys[0], (ATOMS, COEF, C), 1.0, 6.0, ((0, 128),))
    cotangent = noise(keys[1], (ATOMS, COEF, C), 1.0, 6.0, ((0, 128),))
    wigner = draw_wigner(jax.random.fold_in(keys[12], 71), 0)
    pair_blocks_keys = jax.random.split(jax.random.fold_in(keys[3], 1), PAIRS // PAIRS_DEV)
    pair_blocks_turns = jax.random.permutation(jax.random.fold_in(keys[3], 3), PAIRS // PAIRS_DEV)
    pair_blocks = jax.vmap(lambda own, number: shared_out(jax.random.fold_in(keys[3], 2), own, number, PAIRS_DEV, N_ATOMS, 2, MOST, 2))(pair_blocks_keys, pair_blocks_turns).reshape((PAIRS, 2))
    pair_rows = set_ends(jax.random.randint(keys[4], (2, RPP, PAIRS), 0, BLK), jax.random.fold_in(keys[4], 1), 0, BLK - 1).astype(jnp.int32)
    edge_ends = set_ends(jax.random.randint(keys[5], (2, EDGES), 0, RPP), jax.random.fold_in(keys[5], 1), 0, RPP - 1).astype(jnp.int32)
    first_m0 = noise(keys[6], (6 * C, 4 * C), (6 * C) ** -0.5, 0.21875)
    first_m1 = noise(keys[7], (2, 4 * C, 2 * C), (8 * C) ** -0.5, 0.1875)
    first_m2 = noise(keys[8], (2, 2 * C, C), (4 * C) ** -0.5, 0.25)
    second_m0 = noise(keys[9], (3 * C, 3 * C), (3 * C) ** -0.5, 0.3125)
    second_m1 = noise(keys[10], (2, 2 * C, 2 * C), (4 * C) ** -0.5, 0.25)
    second_m2 = noise(keys[11], (2, C, C), (2 * C) ** -0.5, 0.375)
    return {"features": features, "cotangent": cotangent, "wigner": wigner, "pair_blocks": pair_blocks, "pair_rows": pair_rows, "edge_ends": edge_ends, "first_m0": first_m0, "first_m1": first_m1, "first_m2": first_m2, "second_m0": second_m0, "second_m1": second_m1, "second_m2": second_m2}


COEF_ORDER = (0, 2, 6, 3, 7, 1, 5, 8, 4)


def rotate(turned, row_block):
    return jnp.einsum("ije,ejc->eic", turned, row_block.astype(jnp.float32), precision=lax.Precision.HIGHEST)


def unrotate(turned, row_block):
    return jnp.einsum("ije,eic->ejc", turned, row_block, precision=lax.Precision.HIGHEST)


def widen_pair(pair_weights):
    upper_half = jnp.concatenate([pair_weights[0], pair_weights[1]], axis=1)
    lower_half = jnp.concatenate([-pair_weights[1], pair_weights[0]], axis=1)
    return jnp.concatenate([upper_half, lower_half], axis=0)


def narrow(gradient):
    half_rows = gradient.shape[0] // 2
    half_cols = gradient.shape[1] // 2
    return jnp.stack([gradient[:half_rows, :half_cols] + gradient[half_rows:, half_cols:],
                      gradient[:half_rows, half_cols:] - gradient[half_rows:, :half_cols]])


def forward_dot(left_rows, weight):
    return jnp.dot(left_rows, weight, preferred_element_type=jnp.float32)


def backward_dot(gradient, weight):
    return lax.dot_general(gradient, weight, (((1,), (1,)), ((), ())), preferred_element_type=jnp.float32)


def weight_dot(left_rows, gradient):
    return lax.dot_general(left_rows, gradient, (((0,), (0,)), ((), ())), preferred_element_type=jnp.float32)


def forward_part(turned, source, target, weights):
    zero_a, big_one_a, big_two_a, zero_b, big_one_b, big_two_b = weights
    row_count = source.shape[0]
    channels = source.shape[2]
    rot_source = rotate(turned, source)
    rot_target = rotate(turned, target)
    lifted = jnp.concatenate([jnp.concatenate([rot_source, rot_target], axis=2),
                              jnp.concatenate([rot_target, rot_source], axis=2)], axis=0)
    lifted = lifted.astype(jnp.bfloat16).reshape(2 * row_count, 18 * channels)
    zero_part = lifted[:, :6 * channels]
    one_part = lifted[:, 6 * channels:14 * channels]
    two_part = lifted[:, 14 * channels:]
    first_out = forward_dot(zero_part, zero_a)
    hidden = jnp.concatenate([first_out[:, :3 * channels], forward_dot(one_part, big_one_a),
                              forward_dot(two_part, big_two_a)], axis=1)
    gate_value = jax.nn.sigmoid(first_out[:, 3 * channels:])
    scalar_part = hidden[:, :channels]
    gated_part = hidden[:, channels:].reshape(2 * row_count, 8, channels)
    activated = jnp.concatenate([jax.nn.silu(scalar_part),
                                 (gated_part * gate_value[:, None, :]).reshape(2 * row_count, 8 * channels)],
                                axis=1).astype(jnp.bfloat16)
    mixed_rows = jnp.concatenate([forward_dot(activated[:, :3 * channels], zero_b),
                                  forward_dot(activated[:, 3 * channels:7 * channels], big_one_b),
                                  forward_dot(activated[:, 7 * channels:], big_two_b)], axis=1)
    mixed_rows = mixed_rows.reshape(2 * row_count, 9, channels)
    stored = (zero_part, one_part, two_part, scalar_part, gated_part, gate_value, activated)
    return unrotate(turned, mixed_rows[:row_count]), unrotate(turned, mixed_rows[row_count:]), stored


def backward_part(turned, stored, grad_target_in, grad_source_in, weights):
    zero_a, big_one_a, big_two_a, zero_b, big_one_b, big_two_b = weights
    zero_part, one_part, two_part, scalar_part, gated_part, gate_value, activated = stored
    row_count = grad_target_in.shape[0]
    channels = grad_target_in.shape[2]
    all_rows = 2 * row_count
    grad_mix = jnp.concatenate([rotate(turned, grad_target_in), rotate(turned, grad_source_in)], axis=0)
    grad_mix = grad_mix.astype(jnp.bfloat16).reshape(all_rows, 9 * channels)
    mix_zero = grad_mix[:, :3 * channels]
    mix_one = grad_mix[:, 3 * channels:7 * channels]
    mix_two = grad_mix[:, 7 * channels:]
    grad_act = jnp.concatenate([backward_dot(mix_zero, zero_b), backward_dot(mix_one, big_one_b),
                                backward_dot(mix_two, big_two_b)], axis=1)
    terms_second = (weight_dot(activated[:, :3 * channels], mix_zero),
                    narrow(weight_dot(activated[:, 3 * channels:7 * channels], mix_one)),
                    narrow(weight_dot(activated[:, 7 * channels:], mix_two)))
    head_gate = jax.nn.sigmoid(scalar_part)
    grad_scalar = grad_act[:, :channels] * head_gate * (1.0 + scalar_part * (1.0 - head_gate))
    grad_gated = grad_act[:, channels:].reshape(all_rows, 8, channels)
    gated_grad = (grad_gated * gate_value[:, None, :]).reshape(all_rows, 8 * channels)
    grad_gate = jnp.sum(grad_gated * gated_part, axis=1) * gate_value * (1.0 - gate_value)
    grad_zero = jnp.concatenate([grad_scalar, gated_grad[:, :2 * channels], grad_gate], axis=1).astype(jnp.bfloat16)
    grad_one = gated_grad[:, 2 * channels:6 * channels].astype(jnp.bfloat16)
    grad_two = gated_grad[:, 6 * channels:].astype(jnp.bfloat16)
    grad_lifted = jnp.concatenate([backward_dot(grad_zero, zero_a), backward_dot(grad_one, big_one_a),
                                   backward_dot(grad_two, big_two_a)], axis=1).reshape(all_rows, 9, 2 * channels)
    terms_first = (weight_dot(zero_part, grad_zero), narrow(weight_dot(one_part, grad_one)),
                   narrow(weight_dot(two_part, grad_two)))
    front_grad = grad_lifted[:row_count]
    back_grad = grad_lifted[row_count:]
    grad_source = unrotate(turned, front_grad[:, :, :channels] + back_grad[:, :, channels:])
    grad_target = unrotate(turned, front_grad[:, :, channels:] + back_grad[:, :, :channels])
    return grad_source, grad_target, terms_first + terms_second


def reference(features, cotangent, wigner, pair_blocks, pair_rows, edge_ends,
              first_m0, first_m1, first_m2, second_m0, second_m1, second_m2):
    channels = features.shape[2]
    coef_count = features.shape[1]
    per_device = PAIRS_DEV * EPP
    weights = (first_m0, widen_pair(first_m1), widen_pair(first_m2),
               second_m0, widen_pair(second_m1), widen_pair(second_m2))
    index_order = jnp.array(COEF_ORDER, dtype=jnp.int32)
    plain_weights = (first_m0, first_m1, first_m2, second_m0, second_m1, second_m2)

    def one_device(running, block_index):
        summed_msgs, summed_grads, totals = running
        pairs_here = lax.dynamic_slice_in_dim(pair_blocks, block_index * PAIRS_DEV, PAIRS_DEV, 0)
        rows_here = lax.dynamic_slice_in_dim(pair_rows, block_index * PAIRS_DEV, PAIRS_DEV, 2)
        ends_here = lax.dynamic_slice_in_dim(edge_ends, block_index * per_device, per_device, 1)
        turned = jnp.take(lax.dynamic_slice_in_dim(wigner, block_index * per_device, per_device, 2),
                          index_order, axis=0)
        pair_of = jnp.arange(per_device, dtype=jnp.int32) // EPP
        target = pairs_here[pair_of, 0] * BLK + rows_here[0, ends_here[0], pair_of]
        source = pairs_here[pair_of, 1] * BLK + rows_here[1, ends_here[1], pair_of]
        to_target, to_source, stored = forward_part(turned, features[source], features[target], weights)
        grad_source, grad_target, grad_terms = backward_part(turned, stored, cotangent[target],
                                                             cotangent[source], weights)
        summed_msgs = summed_msgs.at[target].add(to_target).at[source].add(to_source)
        summed_grads = summed_grads.at[source].add(grad_source).at[target].add(grad_target)
        totals = tuple(left_term + right_term for left_term, right_term in zip(totals, grad_terms))
        return (summed_msgs, summed_grads, totals), None

    initial = (jnp.zeros((BLK * N_ATOMS, coef_count, channels), jnp.float32),
               jnp.zeros((BLK * N_ATOMS, coef_count, channels), jnp.float32),
               tuple(jnp.zeros(weight.shape, jnp.float32) for weight in plain_weights))
    (summed_msgs, summed_grads, totals), unused = lax.scan(one_device, initial,
                                                           jnp.arange(N_ATOMS, dtype=jnp.int32))
    grad_scale = (2.0 * EDGES) ** -0.5
    return (summed_msgs.astype(jnp.bfloat16), summed_grads, totals[0] * grad_scale, totals[1] * grad_scale,
            totals[2] * grad_scale, totals[3] * grad_scale, totals[4] * grad_scale, totals[5] * grad_scale)
```

```python
import jax
import jax.numpy as jnp
import numpy as np
from jax import lax
from jax.experimental import pallas as pl
from jax.experimental.pallas import tpu as pltpu
from jax.sharding import PartitionSpec as P

COEF_ORDER = (0, 2, 6, 3, 7, 1, 5, 8, 4)
F32 = jnp.float32
BF16 = jnp.bfloat16
CH = 112
WROWS = 64
VMEM_LIMIT = 58 * 1024 * 1024


def chunk_maps():
    coef = np.full((CH,), -1)
    row = np.full((CH,), -1)
    for line in range(CH):
        tile, at = divmod(line, 16)
        if at < 12:
            coef[line], row[line] = tile, at
        elif tile < 6:
            coef[line], row[line] = 7 + tile // 3, 4 * (tile % 3) + at - 12
    return coef, row


def spread_tables():
    coef, row = chunk_maps()
    spread = np.zeros((32, 256), np.float32)
    rows = np.full((256,), -1.0, np.float32)
    for half in range(2):
        for line in range(CH):
            if coef[line] >= 0:
                spread[16 * half + coef[line], CH * half + line] = 1.0
                rows[CH * half + line] = row[line]
    return spread, rows


def request_columns():
    cols = np.full((64,), -1)
    cols[:12] = np.arange(12)
    for j in range(3):
        cols[16 * (j + 1) + 12 : 16 * (j + 2)] = 4 * j + np.arange(4)
    return cols


def dot(a, b):
    return jnp.dot(a, b, preferred_element_type=F32)


def dot_nt(a, b):
    return lax.dot_general(a, b, (((1,), (1,)), ((), ())), preferred_element_type=F32)


def dot_tn(a, b):
    return lax.dot_general(a, b, (((0,), (0,)), ((), ())), preferred_element_type=F32)


def whole(shape):
    return pl.BlockSpec(shape, lambda *_: (0,) * len(shape))


VM = pl.BlockSpec(memory_space=pltpu.VMEM)
SM = pl.BlockSpec(memory_space=pltpu.SMEM)


def gather_body(idx_ref, eye_ref, feat_ref, out_ref):
    turned = dot_nt(eye_ref[...], idx_ref[...].astype(F32).astype(BF16))
    lane = lax.broadcasted_iota(jnp.int32, (64, 128), 1).astype(F32)
    picks = []
    for q in range(16):
        col = jnp.broadcast_to(turned[:, q : q + 1], (64, 128))
        picks.append(jnp.where(col == lane, 1.0, 0.0).astype(BF16))
    kinds = [jnp.concatenate([x[16 * v : 16 * v + 16] for x in picks], axis=0) for v in range(4)]
    for j in range(3):
        left = jnp.concatenate([kinds[0], kinds[j + 1]], axis=1)
        right = jnp.concatenate(
            [
                jnp.concatenate([feat_ref[j], feat_ref[j + 3]], axis=1),
                jnp.concatenate([feat_ref[7], feat_ref[8]], axis=1),
            ],
            axis=0,
        )
        got = dot(left, right).astype(BF16)
        out_ref[:, 16 * j : 16 * j + 16, :] = got[:, :128].reshape(16, 16, 128)
        out_ref[:, 16 * (j + 3) : 16 * (j + 4), :] = got[:, 128:].reshape(16, 16, 128)
    last = dot(kinds[0], feat_ref[6]).astype(BF16)
    out_ref[:, 96:112, :] = last.reshape(16, 16, 128)


def pick_rows(idx, eye, feat):
    peers = idx.shape[0]
    return pl.pallas_call(
        gather_body,
        grid=(peers // 16,),
        in_specs=[
            pl.BlockSpec((16, 64), lambda c: (c, 0)),
            whole((64, 64)),
            whole((9, 128, 128)),
        ],
        out_specs=pl.BlockSpec((16, CH, 128), lambda c: (c, 0, 0)),
        out_shape=jax.ShapeDtypeStruct((peers, CH, 128), BF16),
        cost_estimate=pl.CostEstimate(flops=2 * 10**9, transcendentals=0, bytes_accessed=4 * 10**6),
        name="pick_rows",
    )(idx, eye, feat)


def prep_body(ra_ref, rb_ref, sp_ref, spt_ref, rows_ref, rowst_ref, wt_ref, ws_ref, vt_ref, vs_ref):
    a = ra_ref[0]
    a_hi = a.astype(BF16)
    a_lo = (a - a_hi.astype(F32)).astype(BF16)
    lane = lax.broadcasted_iota(jnp.int32, (224, 32), 1)
    a_both = jnp.where(lane < 16, a_hi.astype(F32), a_lo.astype(F32)).astype(BF16)
    x = dot(a_both, sp_ref[...])
    rows = jnp.broadcast_to(rows_ref[0:1, :], (224, 256))
    for at, out in ((9, wt_ref), (10, ws_ref)):
        mine = jnp.broadcast_to(a[:, at : at + 1], (224, 256))
        out[0] = jnp.where(mine == rows, x, 0.0).astype(BF16)
    b = rb_ref[0]
    b_hi = b.astype(BF16)
    b_lo = (b - b_hi.astype(F32)).astype(BF16)
    line = lax.broadcasted_iota(jnp.int32, (32, 256), 0)
    b_both = jnp.where(line < 16, b_hi.astype(F32), b_lo.astype(F32)).astype(BF16)
    y = dot(spt_ref[...], b_both)
    rowst = jnp.broadcast_to(rowst_ref[:, 0:1], (224, 256))
    for at, out in ((9, vt_ref), (10, vs_ref)):
        mine = jnp.broadcast_to(b[at : at + 1, :], (224, 256))
        out[0] = jnp.where(mine == rowst, y, 0.0).astype(BF16)


def build_turns(ra, rb):
    pairs = ra.shape[0]
    spread, rows = spread_tables()
    sp = jnp.asarray(spread, BF16)
    spt = jnp.asarray(spread[:, :224].T, BF16)
    rows8 = jnp.asarray(np.tile(rows[None], (8, 1)), F32)
    rowst = jnp.asarray(np.tile(rows[:224, None], (1, 128)), F32)
    one = jax.ShapeDtypeStruct((pairs, 224, 256), BF16)
    block = pl.BlockSpec((1, 224, 256), lambda p: (p, 0, 0))
    return pl.pallas_call(
        prep_body,
        grid=(pairs,),
        in_specs=[
            pl.BlockSpec((1, 224, 32), lambda p: (p, 0, 0)),
            pl.BlockSpec((1, 32, 256), lambda p: (p, 0, 0)),
            whole((32, 256)),
            whole((224, 32)),
            whole((8, 256)),
            whole((224, 128)),
        ],
        out_specs=[block] * 4,
        out_shape=[one] * 4,
        cost_estimate=pl.CostEstimate(flops=10**9, transcendentals=0, bytes_accessed=10**7),
        name="build_turns",
    )(ra, rb, sp, spt, rows8, rowst)


def turn(w_ref, r_ref, pair, owner):
    chunk = r_ref[owner]
    right = jnp.concatenate([chunk, chunk, jnp.zeros((32, 128), BF16)], axis=0)
    return dot(w_ref[pair], right)


def turn_back(v_ref, pair, src_ref, base):
    parts = [src_ref[pl.ds(base, 24), 128 * k : 128 * k + 128] for k in range(9)]
    x = jnp.concatenate(parts + [jnp.zeros((40, 128), F32)], axis=0)
    hi = x.astype(BF16)
    lo = (x - hi.astype(F32)).astype(BF16)
    y = dot(v_ref[pair], jnp.concatenate([hi, lo], axis=1))
    y = y[:, :128] + y[:, 128:]
    return (y[:CH] + y[CH:]).astype(BF16)


def forward_body(
    own_ref, r_ref, wt_ref, ws_ref, vt_ref, vs_ref, a0_ref, a1_ref, a2_ref, b0_ref, b1_ref, b2_ref,
    out_ref, z_ref, hid_ref, gate_ref, act_ref, mix_ref,
):
    half = z_ref.shape[0] // 2
    pairs = wt_ref.shape[0]

    def lift(d, carry):
        turned = []
        for p in (2 * d, 2 * d + 1):
            turned.append((turn(ws_ref, r_ref, p, own_ref[2 * p + 1]), turn(wt_ref, r_ref, p, own_ref[2 * p])))
        (s0, t0), (s1, t1) = turned
        at = pl.multiple_of(d * 48, 16)
        for k in range(9):
            lines = slice(24 * k, 24 * k + 24)
            s = jnp.concatenate([s0[lines], s1[lines]], axis=0).astype(BF16)
            t = jnp.concatenate([t0[lines], t1[lines]], axis=0).astype(BF16)
            z_ref[pl.ds(at, 48), 256 * k : 256 * k + 128] = s
            z_ref[pl.ds(at, 48), 256 * k + 128 : 256 * k + 256] = t
            z_ref[pl.ds(half + at, 48), 256 * k : 256 * k + 128] = t
            z_ref[pl.ds(half + at, 48), 256 * k + 128 : 256 * k + 256] = s
        return carry

    lax.fori_loop(0, pairs // 2, lift, 0)

    def layer(b, carry):
        at = pl.multiple_of(b * 256, 256)
        here = pl.ds(at, 256)
        o = dot(z_ref[here, 0:768], a0_ref[...])
        gate = jax.nn.sigmoid(o[:, 384:512])
        gate_ref[here, :] = gate
        h0 = o[:, 0:128]
        hid_ref[here, 0:384] = o[:, 0:384]
        act_ref[here, 0:128] = (h0 * jax.nn.sigmoid(h0)).astype(BF16)
        for k in range(1, 3):
            cols = slice(128 * k, 128 * k + 128)
            act_ref[here, cols] = (o[:, cols] * gate).astype(BF16)
        h1 = dot(z_ref[here, 768:1792], a1_ref[...])
        hid_ref[here, 384:896] = h1
        for k in range(4):
            act_ref[here, 384 + 128 * k : 512 + 128 * k] = (h1[:, 128 * k : 128 * k + 128] * gate).astype(BF16)
        h2 = dot(z_ref[here, 1792:2304], a2_ref[...])
        hid_ref[here, 896:1152] = h2
        for k in range(2):
            act_ref[here, 896 + 128 * k : 1024 + 128 * k] = (h2[:, 128 * k : 128 * k + 128] * gate).astype(BF16)
        mix_ref[here, 0:384] = dot(act_ref[here, 0:384], b0_ref[...])
        mix_ref[here, 384:896] = dot(act_ref[here, 384:896], b1_ref[...])
        mix_ref[here, 896:1152] = dot(act_ref[here, 896:1152], b2_ref[...])
        return carry

    lax.fori_loop(0, z_ref.shape[0] // 256, layer, 0)
    out_ref[...] = jnp.zeros(out_ref.shape, BF16)

    def unlift(p, carry):
        at = pl.multiple_of(p * 24, 8)
        t = own_ref[2 * p]
        out_ref[t] = out_ref[t] + turn_back(vt_ref, p, mix_ref, at)
        s = own_ref[2 * p + 1]
        out_ref[s] = out_ref[s] + turn_back(vs_ref, p, mix_ref, half + at)
        return carry

    lax.fori_loop(0, pairs, unlift, 0)


def forward(owners, got, turns, weights, rows):
    peers = got.shape[0]
    return pl.pallas_call(
        forward_body,
        in_specs=[SM] + [VM] * 11,
        out_specs=[VM] * 5,
        out_shape=[
            jax.ShapeDtypeStruct((peers, CH, 128), BF16),
            jax.ShapeDtypeStruct((rows, 2304), BF16),
            jax.ShapeDtypeStruct((rows, 1152), F32),
            jax.ShapeDtypeStruct((rows, 128), F32),
            jax.ShapeDtypeStruct((rows, 1152), BF16),
        ],
        scratch_shapes=[pltpu.VMEM((rows, 1152), F32)],
        compiler_params=pltpu.CompilerParams(vmem_limit_bytes=VMEM_LIMIT),
        cost_estimate=pl.CostEstimate(flops=10**10, transcendentals=10**6, bytes_accessed=3 * 10**7),
        name="forward",
    )(owners, got, *turns, *weights)


def backward_body(
    own_ref, r_ref, wt_ref, ws_ref, vt_ref, vs_ref, a0_ref, a1_ref, a2_ref, b0_ref, b1_ref, b2_ref,
    z_ref, hid_ref, gate_ref, act_ref, out_ref, dmix_ref, dd_ref, gs_ref, gt_ref, *, scale,
):
    half = z_ref.shape[0] // 2
    pairs = wt_ref.shape[0]

    def lift(d, carry):
        turned = []
        for p in (2 * d, 2 * d + 1):
            turned.append((turn(wt_ref, r_ref, p, own_ref[2 * p]), turn(ws_ref, r_ref, p, own_ref[2 * p + 1])))
        (t0, s0), (t1, s1) = turned
        at = pl.multiple_of(d * 48, 16)
        for k in range(9):
            lines = slice(24 * k, 24 * k + 24)
            cols = slice(128 * k, 128 * k + 128)
            dmix_ref[pl.ds(at, 48), cols] = jnp.concatenate([t0[lines], t1[lines]], axis=0).astype(BF16)
            dmix_ref[pl.ds(half + at, 48), cols] = jnp.concatenate([s0[lines], s1[lines]], axis=0).astype(BF16)
        return carry

    lax.fori_loop(0, pairs // 2, lift, 0)

    def layer(b, carry):
        at = pl.multiple_of(b * 128, 128)
        spots = (pl.ds(at, 128), pl.ds(half + at, 128))

        def rows_of(ref, cols):
            return jnp.concatenate([ref[spot, cols] for spot in spots], axis=0)

        def put(col, value):
            value = value.astype(BF16)
            for i, spot in enumerate(spots):
                dd_ref[spot, col : col + 128] = value[128 * i : 128 * i + 128]

        gate = rows_of(gate_ref, slice(0, 128))
        dact0 = dot_nt(rows_of(dmix_ref, slice(0, 384)), b0_ref[...])
        h0 = rows_of(hid_ref, slice(0, 128))
        head = jax.nn.sigmoid(h0)
        put(0, dact0[:, 0:128] * head * (1.0 + h0 * (1.0 - head)))
        total = None

        def gated(k, piece, col):
            put(col, piece * gate)
            return piece * rows_of(hid_ref, slice(128 * k, 128 * k + 128))

        total = gated(1, dact0[:, 128:256], 128) + gated(2, dact0[:, 256:384], 256)
        dact1 = dot_nt(rows_of(dmix_ref, slice(384, 896)), b1_ref[...])
        for k in range(4):
            total = total + gated(3 + k, dact1[:, 128 * k : 128 * k + 128], 512 + 128 * k)
        dact2 = dot_nt(rows_of(dmix_ref, slice(896, 1152)), b2_ref[...])
        for k in range(2):
            total = total + gated(7 + k, dact2[:, 128 * k : 128 * k + 128], 1024 + 128 * k)
        put(384, total * gate * (1.0 - gate))

        first = 0
        for cols, w_ref, count in ((slice(0, 512), a0_ref, 3), (slice(512, 1024), a1_ref, 4), (slice(1024, 1280), a2_ref, 2)):
            dz = dot_nt(rows_of(dd_ref, cols), w_ref[...])
            for k in range(count):
                lo = dz[:, 256 * k : 256 * k + 128]
                hi = dz[:, 256 * k + 128 : 256 * k + 256]
                to = slice(128 * (first + k), 128 * (first + k) + 128)
                gs_ref[spots[0], to] = lo[:128] + hi[128:]
                gt_ref[spots[0], to] = hi[:128] + lo[128:]
            first += count
        return carry

    lax.fori_loop(0, half // 128, layer, 0)
    out_ref[...] = jnp.zeros(out_ref.shape, BF16)

    def unlift(p, carry):
        at = pl.multiple_of(p * 24, 8)
        s = own_ref[2 * p + 1]
        out_ref[s, 0:CH] = out_ref[s, 0:CH] + turn_back(vs_ref, p, gs_ref, at)
        t = own_ref[2 * p]
        out_ref[t, 0:CH] = out_ref[t, 0:CH] + turn_back(vt_ref, p, gt_ref, at)
        return carry

    lax.fori_loop(0, pairs, unlift, 0)

    def put_rows(row, value):
        value = (value * scale).astype(BF16)
        count = value.shape[0] // WROWS
        q = row // WROWS
        out_ref[q : q + count, CH : CH + WROWS, :] = value.reshape(count, WROWS, 128)

    def plain(left_ref, left_at, height, right_ref, right_cols, row):
        for c in range(height // 128):
            g = dot_tn(left_ref[:, left_at + 128 * c : left_at + 128 * c + 128], right_ref[:, right_cols])
            for n in range(g.shape[1] // 128):
                put_rows(row + n * height + 128 * c, g[:, 128 * n : 128 * n + 128])

    def folded(left_ref, left_at, height, right_ref, right_cols, row):
        width = (right_cols.stop - right_cols.start) // 2
        blocks = width // 128
        for c in range(height // 128):
            low = left_at + 128 * c
            top = dot_tn(left_ref[:, low : low + 128], right_ref[:, right_cols])
            bot = dot_tn(left_ref[:, low + height : low + height + 128], right_ref[:, right_cols])
            same = top[:, :width] + bot[:, width:]
            cross = top[:, width:] - bot[:, :width]
            for n in range(blocks):
                cols = slice(128 * n, 128 * n + 128)
                put_rows(row + n * height + 128 * c, same[:, cols])
                put_rows(row + (blocks + n) * height + 128 * c, cross[:, cols])

    plain(z_ref, 0, 768, dd_ref, slice(0, 512), 0)
    folded(z_ref, 768, 512, dd_ref, slice(512, 1024), 3072)
    folded(z_ref, 1792, 256, dd_ref, slice(1024, 1280), 5120)
    plain(act_ref, 0, 384, dmix_ref, slice(0, 384), 5632)
    folded(act_ref, 384, 256, dmix_ref, slice(384, 896), 6784)
    folded(act_ref, 896, 128, dmix_ref, slice(896, 1152), 7808)


def backward(owners, got, turns, weights, kept, scale):
    peers = got.shape[0]
    rows = kept[0].shape[0]

    def body(*refs):
        backward_body(*refs, scale=scale)

    return pl.pallas_call(
        body,
        in_specs=[SM] + [VM] * 15,
        out_specs=VM,
        out_shape=jax.ShapeDtypeStruct((peers, CH + WROWS, 128), BF16),
        scratch_shapes=[
            pltpu.VMEM((rows, 1152), BF16),
            pltpu.VMEM((rows, 1280), BF16),
            pltpu.VMEM((rows // 2, 1152), F32),
            pltpu.VMEM((rows // 2, 1152), F32),
        ],
        compiler_params=pltpu.CompilerParams(vmem_limit_bytes=VMEM_LIMIT),
        cost_estimate=pl.CostEstimate(flops=2 * 10**10, transcendentals=10**6, bytes_accessed=3 * 10**7),
        name="backward",
    )(owners, got, *turns, *weights, *kept)


def scatter_body(idx_ref, got_ref, out_ref, *rest, with_weights):
    acc_ref, last_ref = rest[-2:]

    @pl.when(pl.program_id(0) == 0)
    def _():
        acc_ref[...] = jnp.zeros(acc_ref.shape, F32)
        last_ref[...] = jnp.zeros(last_ref.shape, F32)
        if with_weights:
            rest[0][...] = jnp.zeros(rest[0].shape, F32)

    atom = lax.broadcasted_iota(jnp.int32, (128, 256), 0)
    kinds = [
        jnp.where(jnp.broadcast_to(idx_ref[v : v + 1, :], (128, 256)) == atom, 1.0, 0.0).astype(BF16)
        for v in range(4)
    ]
    tiles = [got_ref[:, 16 * t : 16 * t + 16, :].reshape(256, 128) for t in range(7)]
    acc_ref[...] += dot(kinds[0], jnp.concatenate(tiles, axis=1))
    spare = jnp.concatenate([jnp.concatenate([tiles[j], tiles[j + 3]], axis=1) for j in range(3)], axis=0)
    last_ref[...] += dot(jnp.concatenate(kinds[1:], axis=1), spare)
    if with_weights:
        rest[0][...] += jnp.sum(got_ref[:, CH : CH + WROWS, :].astype(F32), axis=0)

    @pl.when(pl.program_id(0) == pl.num_programs(0) - 1)
    def _():
        for k in range(7):
            out_ref[k] = acc_ref[:, 128 * k : 128 * k + 128].astype(out_ref.dtype)
        for k in range(2):
            out_ref[7 + k] = last_ref[:, 128 * k : 128 * k + 128].astype(out_ref.dtype)


def add_rows(idx_rows, got, dtype, with_weights):
    peers, lines, _ = got.shape

    def body(*refs):
        scatter_body(*refs, with_weights=with_weights)

    out_specs = [whole((9, 128, 128))]
    out_shape = [jax.ShapeDtypeStruct((9, 128, 128), dtype)]
    if with_weights:
        out_specs.append(whole((WROWS, 128)))
        out_shape.append(jax.ShapeDtypeStruct((WROWS, 128), F32))
    return pl.pallas_call(
        body,
        grid=(peers // 16,),
        in_specs=[
            pl.BlockSpec((8, 256), lambda c: (0, c)),
            pl.BlockSpec((16, lines, 128), lambda c: (c, 0, 0)),
        ],
        out_specs=out_specs,
        out_shape=out_shape,
        scratch_shapes=[pltpu.VMEM((128, 896), F32), pltpu.VMEM((128, 256), F32)],
        cost_estimate=pl.CostEstimate(flops=10**9, transcendentals=0, bytes_accessed=6 * 10**6),
        name="add_rows_w" if with_weights else "add_rows",
    )(idx_rows, got)


def widen_pair(w):
    upper = jnp.concatenate([w[0], w[1]], axis=1)
    lower = jnp.concatenate([-w[1], w[0]], axis=1)
    return jnp.concatenate([upper, lower], axis=0)


def exchange(x):
    return lax.all_to_all(x, "atoms", split_axis=0, concat_axis=0, tiled=True)


def local(
    features, cotangent, wigner, pair_blocks, pair_rows, edge_ends,
    first_m0, first_m1, first_m2, second_m0, second_m1, second_m2,
):
    peers = lax.axis_size("atoms")
    pairs = pair_blocks.shape[0]
    edges = edge_ends.shape[1]
    each = edges // pairs
    owners = pair_blocks.reshape(2 * pairs)
    ends = jnp.arange(2 * pairs, dtype=jnp.int32)
    slots = jnp.sum(
        jnp.logical_and(owners[:, None] == owners[None, :], ends[:, None] > ends[None, :]), axis=1
    ).astype(jnp.int32)

    end_rows = jnp.transpose(pair_rows, (2, 0, 1)).reshape(2 * pairs, 6)
    cols = request_columns()
    row_cols = jnp.concatenate([end_rows[:, max(c, 0) % 6 : max(c, 0) % 6 + 1] for c in cols], axis=1)
    col_slot = jnp.asarray(np.where(cols < 0, -1, cols // 6), jnp.int32)
    peer = jnp.arange(peers, dtype=jnp.int32)
    hit = jnp.logical_and(
        owners[None, :, None] == peer[:, None, None], slots[None, :, None] == col_slot[None, None, :]
    )
    request = jnp.sum(jnp.where(hit, row_cols[None] + 1, 0), axis=1) - 1
    asked = exchange(request)
    asked_rows = jnp.transpose(asked.reshape(peers, 4, 16), (1, 0, 2)).reshape(4, peers * 16)
    asked_rows = jnp.concatenate([asked_rows, asked_rows], axis=0)
    eye = jnp.eye(64, dtype=BF16)

    got_f = exchange(pick_rows(asked, eye, jnp.transpose(features, (1, 0, 2))))
    got_c = exchange(pick_rows(asked, eye, jnp.transpose(cotangent, (1, 0, 2))))

    turned = jnp.stack([wigner[i] for i in COEF_ORDER]).reshape(9, 9, pairs, each)
    pos = jnp.stack(
        [
            (slots.reshape(pairs, 2)[:, side, None] * 6 + edge_ends[side].reshape(pairs, each)).astype(F32)
            for side in range(2)
        ],
        axis=0,
    )
    pos = jnp.broadcast_to(pos[:, None], (2, 9, pairs, each))
    by_j = jnp.transpose(turned, (1, 0, 2, 3))
    gap5 = jnp.zeros((5, 9, pairs, each), F32)
    gap7 = jnp.zeros((7, 9, pairs, each), F32)
    table = jnp.concatenate([by_j, pos, gap5, by_j, gap7], axis=0)
    ra = jnp.transpose(table, (2, 1, 3, 0)).reshape(pairs, 9 * each, 32)
    ra = jnp.pad(ra, ((0, 0), (0, 224 - 9 * each), (0, 0)))
    rb = jnp.transpose(table, (2, 0, 1, 3)).reshape(pairs, 32, 9 * each)
    rb = jnp.pad(rb, ((0, 0), (0, 0), (0, 256 - 9 * each)))
    turns = build_turns(ra, rb)

    weights = (
        first_m0, widen_pair(first_m1), widen_pair(first_m2),
        second_m0, widen_pair(second_m1), widen_pair(second_m2),
    )
    back_m, *kept = forward(owners, got_f, turns, weights, 2 * edges)
    got_m = exchange(back_m)
    scale = float((2.0 * edges * peers) ** (-0.5))
    back_g = backward(owners, got_c, turns, weights, kept, scale)
    back_g, got_m = lax.optimization_barrier((back_g, got_m))
    got_g = exchange(back_g)
    (messages,) = add_rows(asked_rows, got_m, BF16, False)
    grad_features, w_sum = add_rows(asked_rows, got_g, F32, True)
    messages = jnp.transpose(messages, (1, 0, 2))
    grad_features = jnp.transpose(grad_features, (1, 0, 2))

    w_all = exchange(jnp.broadcast_to(w_sum.astype(BF16)[None], (peers, WROWS, 128)))
    w_all = w_all.reshape(peers * WROWS, 128).astype(F32)

    def unpack(row, parts, height, blocks):
        x = w_all[row : row + parts * blocks * height].reshape(parts, blocks, height, 128)
        return jnp.transpose(x, (0, 2, 1, 3)).reshape(parts, height, blocks * 128)

    return (
        messages,
        grad_features,
        unpack(0, 1, 768, 4)[0],
        unpack(3072, 2, 512, 2),
        unpack(5120, 2, 256, 1),
        unpack(5632, 1, 384, 3)[0],
        unpack(6784, 2, 256, 2),
        unpack(7808, 2, 128, 1),
    )


def solution(mesh):
    rows = P("atoms", None, None)
    in_specs = (
        rows, rows, P(None, None, "atoms"), P("atoms", None), P(None, None, "atoms"), P(None, "atoms"),
        P(), P(), P(), P(), P(), P(),
    )
    out_specs = (rows, rows, P(), P(), P(), P(), P(), P())
    return jax.shard_map(local, mesh=mesh, in_specs=in_specs, out_specs=out_specs, check_vma=False)
```

```python
import jax
import jax.numpy as jnp
import numpy as np
from jax import lax
from jax.experimental import pallas as pl
from jax.experimental.pallas import tpu as pltpu
from jax.sharding import PartitionSpec as P

COEF_ORDER = (0, 2, 6, 3, 7, 1, 5, 8, 4)
F32 = jnp.float32
BF16 = jnp.bfloat16
CH = 112
WEIGHT_ROWS = 8192
VMEM_LIMIT = 58 * 1024 * 1024


def chunk_maps():
    coef = np.full((CH,), -1)
    row = np.full((CH,), -1)
    for line in range(CH):
        tile, at = divmod(line, 16)
        if at < 12:
            coef[line], row[line] = tile, at
        elif tile < 6:
            coef[line], row[line] = 7 + tile // 3, 4 * (tile % 3) + at - 12
    return coef, row


def spread_tables():
    coef, row = chunk_maps()
    spread = np.zeros((32, 256), np.float32)
    rows = np.full((256,), -1.0, np.float32)
    for half in range(2):
        for line in range(CH):
            if coef[line] >= 0:
                spread[16 * half + coef[line], CH * half + line] = 1.0
                rows[CH * half + line] = row[line]
    return spread, rows


def request_columns():
    cols = np.full((64,), -1)
    cols[:12] = np.arange(12)
    for j in range(3):
        cols[16 * (j + 1) + 12 : 16 * (j + 2)] = 4 * j + np.arange(4)
    return cols


def dot(a, b):
    return jnp.dot(a, b, preferred_element_type=F32)


def dot_nt(a, b):
    return lax.dot_general(a, b, (((1,), (1,)), ((), ())), preferred_element_type=F32)


def dot_tn(a, b):
    return lax.dot_general(a, b, (((0,), (0,)), ((), ())), preferred_element_type=F32)


def whole(shape):
    return pl.BlockSpec(shape, lambda *_: (0,) * len(shape))


VM = pl.BlockSpec(memory_space=pltpu.VMEM)
SM = pl.BlockSpec(memory_space=pltpu.SMEM)


def gather_body(idx_ref, eye_ref, feat_ref, out_ref):
    turned = dot_nt(eye_ref[...], idx_ref[...].astype(F32).astype(BF16))
    lane = lax.broadcasted_iota(jnp.int32, (64, 128), 1).astype(F32)
    picks = []
    for q in range(16):
        col = jnp.broadcast_to(turned[:, q : q + 1], (64, 128))
        picks.append(jnp.where(col == lane, 1.0, 0.0).astype(BF16))
    kinds = [jnp.concatenate([x[16 * v : 16 * v + 16] for x in picks], axis=0) for v in range(4)]
    for j in range(3):
        left = jnp.concatenate([kinds[0], kinds[j + 1]], axis=1)
        right = jnp.concatenate(
            [
                jnp.concatenate([feat_ref[j], feat_ref[j + 3]], axis=1),
                jnp.concatenate([feat_ref[7], feat_ref[8]], axis=1),
            ],
            axis=0,
        )
        got = dot(left, right).astype(BF16)
        out_ref[:, 16 * j : 16 * j + 16, :] = got[:, :128].reshape(16, 16, 128)
        out_ref[:, 16 * (j + 3) : 16 * (j + 4), :] = got[:, 128:].reshape(16, 16, 128)
    last = dot(kinds[0], feat_ref[6]).astype(BF16)
    out_ref[:, 96:112, :] = last.reshape(16, 16, 128)


def pick_rows(idx, eye, feat):
    peers = idx.shape[0]
    return pl.pallas_call(
        gather_body,
        grid=(peers // 16,),
        in_specs=[
            pl.BlockSpec((16, 64), lambda c: (c, 0)),
            whole((64, 64)),
            whole((9, 128, 128)),
        ],
        out_specs=pl.BlockSpec((16, CH, 128), lambda c: (c, 0, 0)),
        out_shape=jax.ShapeDtypeStruct((peers, CH, 128), BF16),
        cost_estimate=pl.CostEstimate(flops=2 * 10**9, transcendentals=0, bytes_accessed=4 * 10**6),
        name="pick_rows",
    )(idx, eye, feat)


def prep_body(ra_ref, rb_ref, sp_ref, spt_ref, rows_ref, rowst_ref, wt_ref, ws_ref, vt_ref, vs_ref):
    a = ra_ref[0]
    a_hi = a.astype(BF16)
    a_lo = (a - a_hi.astype(F32)).astype(BF16)
    lane = lax.broadcasted_iota(jnp.int32, (224, 32), 1)
    a_both = jnp.where(lane < 16, a_hi.astype(F32), a_lo.astype(F32)).astype(BF16)
    x = dot(a_both, sp_ref[...])
    rows = jnp.broadcast_to(rows_ref[0:1, :], (224, 256))
    for at, out in ((9, wt_ref), (10, ws_ref)):
        mine = jnp.broadcast_to(a[:, at : at + 1], (224, 256))
        out[0] = jnp.where(mine == rows, x, 0.0).astype(BF16)
    b = rb_ref[0]
    b_hi = b.astype(BF16)
    b_lo = (b - b_hi.astype(F32)).astype(BF16)
    line = lax.broadcasted_iota(jnp.int32, (32, 256), 0)
    b_both = jnp.where(line < 16, b_hi.astype(F32), b_lo.astype(F32)).astype(BF16)
    y = dot(spt_ref[...], b_both)
    rowst = jnp.broadcast_to(rowst_ref[:, 0:1], (224, 256))
    for at, out in ((9, vt_ref), (10, vs_ref)):
        mine = jnp.broadcast_to(b[at : at + 1, :], (224, 256))
        out[0] = jnp.where(mine == rowst, y, 0.0).astype(BF16)


def build_turns(ra, rb):
    pairs = ra.shape[0]
    spread, rows = spread_tables()
    sp = jnp.asarray(spread, BF16)
    spt = jnp.asarray(spread[:, :224].T, BF16)
    rows8 = jnp.asarray(np.tile(rows[None], (8, 1)), F32)
    rowst = jnp.asarray(np.tile(rows[:224, None], (1, 128)), F32)
    one = jax.ShapeDtypeStruct((pairs, 224, 256), BF16)
    block = pl.BlockSpec((1, 224, 256), lambda p: (p, 0, 0))
    return pl.pallas_call(
        prep_body,
        grid=(pairs,),
        in_specs=[
            pl.BlockSpec((1, 224, 32), lambda p: (p, 0, 0)),
            pl.BlockSpec((1, 32, 256), lambda p: (p, 0, 0)),
            whole((32, 256)),
            whole((224, 32)),
            whole((8, 256)),
            whole((224, 128)),
        ],
        out_specs=[block] * 4,
        out_shape=[one] * 4,
        cost_estimate=pl.CostEstimate(flops=10**9, transcendentals=0, bytes_accessed=10**7),
        name="build_turns",
    )(ra, rb, sp, spt, rows8, rowst)


def turn(w_ref, r_ref, pair, owner):
    chunk = r_ref[owner]
    right = jnp.concatenate([chunk, chunk, jnp.zeros((32, 128), BF16)], axis=0)
    return dot(w_ref[pair], right)


def turn_back(v_ref, pair, src_ref, base):
    parts = [src_ref[pl.ds(base, 24), 128 * k : 128 * k + 128] for k in range(9)]
    x = jnp.concatenate(parts + [jnp.zeros((40, 128), F32)], axis=0)
    hi = x.astype(BF16)
    lo = (x - hi.astype(F32)).astype(BF16)
    y = dot(v_ref[pair], jnp.concatenate([hi, lo], axis=1))
    y = y[:, :128] + y[:, 128:]
    return (y[:CH] + y[CH:]).astype(BF16)


def forward_body(
    own_ref, r_ref, wt_ref, ws_ref, vt_ref, vs_ref, a0_ref, a1_ref, a2_ref, b0_ref, b1_ref, b2_ref,
    out_ref, z_ref, hid_ref, gate_ref, act_ref, mix_ref,
):
    half = z_ref.shape[0] // 2
    pairs = wt_ref.shape[0]

    def lift(d, carry):
        turned = []
        for p in (2 * d, 2 * d + 1):
            turned.append((turn(ws_ref, r_ref, p, own_ref[2 * p + 1]), turn(wt_ref, r_ref, p, own_ref[2 * p])))
        (s0, t0), (s1, t1) = turned
        at = pl.multiple_of(d * 48, 16)
        for k in range(9):
            lines = slice(24 * k, 24 * k + 24)
            s = jnp.concatenate([s0[lines], s1[lines]], axis=0).astype(BF16)
            t = jnp.concatenate([t0[lines], t1[lines]], axis=0).astype(BF16)
            z_ref[pl.ds(at, 48), 256 * k : 256 * k + 128] = s
            z_ref[pl.ds(at, 48), 256 * k + 128 : 256 * k + 256] = t
            z_ref[pl.ds(half + at, 48), 256 * k : 256 * k + 128] = t
            z_ref[pl.ds(half + at, 48), 256 * k + 128 : 256 * k + 256] = s
        return carry

    lax.fori_loop(0, pairs // 2, lift, 0)

    def layer(b, carry):
        at = pl.multiple_of(b * 256, 256)
        here = pl.ds(at, 256)
        o = dot(z_ref[here, 0:768], a0_ref[...])
        gate = jax.nn.sigmoid(o[:, 384:512])
        gate_ref[here, :] = gate
        h0 = o[:, 0:128]
        hid_ref[here, 0:384] = o[:, 0:384]
        act_ref[here, 0:128] = (h0 * jax.nn.sigmoid(h0)).astype(BF16)
        for k in range(1, 3):
            cols = slice(128 * k, 128 * k + 128)
            act_ref[here, cols] = (o[:, cols] * gate).astype(BF16)
        h1 = dot(z_ref[here, 768:1792], a1_ref[...])
        hid_ref[here, 384:896] = h1
        for k in range(4):
            act_ref[here, 384 + 128 * k : 512 + 128 * k] = (h1[:, 128 * k : 128 * k + 128] * gate).astype(BF16)
        h2 = dot(z_ref[here, 1792:2304], a2_ref[...])
        hid_ref[here, 896:1152] = h2
        for k in range(2):
            act_ref[here, 896 + 128 * k : 1024 + 128 * k] = (h2[:, 128 * k : 128 * k + 128] * gate).astype(BF16)
        mix_ref[here, 0:384] = dot(act_ref[here, 0:384], b0_ref[...])
        mix_ref[here, 384:896] = dot(act_ref[here, 384:896], b1_ref[...])
        mix_ref[here, 896:1152] = dot(act_ref[here, 896:1152], b2_ref[...])
        return carry

    lax.fori_loop(0, z_ref.shape[0] // 256, layer, 0)
    out_ref[...] = jnp.zeros(out_ref.shape, BF16)

    def unlift(p, carry):
        at = pl.multiple_of(p * 24, 8)
        t = own_ref[2 * p]
        out_ref[t] = out_ref[t] + turn_back(vt_ref, p, mix_ref, at)
        s = own_ref[2 * p + 1]
        out_ref[s] = out_ref[s] + turn_back(vs_ref, p, mix_ref, half + at)
        return carry

    lax.fori_loop(0, pairs, unlift, 0)


def forward(owners, got, turns, weights, rows):
    peers = got.shape[0]
    return pl.pallas_call(
        forward_body,
        in_specs=[SM] + [VM] * 11,
        out_specs=[VM] * 5,
        out_shape=[
            jax.ShapeDtypeStruct((peers, CH, 128), BF16),
            jax.ShapeDtypeStruct((rows, 2304), BF16),
            jax.ShapeDtypeStruct((rows, 1152), F32),
            jax.ShapeDtypeStruct((rows, 128), F32),
            jax.ShapeDtypeStruct((rows, 1152), BF16),
        ],
        scratch_shapes=[pltpu.VMEM((rows, 1152), F32)],
        compiler_params=pltpu.CompilerParams(vmem_limit_bytes=VMEM_LIMIT),
        cost_estimate=pl.CostEstimate(flops=10**10, transcendentals=10**6, bytes_accessed=3 * 10**7),
        name="forward",
    )(owners, got, *turns, *weights)


def backward_body(
    own_ref, r_ref, wt_ref, ws_ref, vt_ref, vs_ref, a0_ref, a1_ref, a2_ref, b0_ref, b1_ref, b2_ref,
    z_ref, hid_ref, gate_ref, act_ref, out_ref, wg_ref, dmix_ref, dd_ref, gs_ref, gt_ref, *, scale,
):
    half = z_ref.shape[0] // 2
    pairs = wt_ref.shape[0]

    def lift(d, carry):
        turned = []
        for p in (2 * d, 2 * d + 1):
            turned.append((turn(wt_ref, r_ref, p, own_ref[2 * p]), turn(ws_ref, r_ref, p, own_ref[2 * p + 1])))
        (t0, s0), (t1, s1) = turned
        at = pl.multiple_of(d * 48, 16)
        for k in range(9):
            lines = slice(24 * k, 24 * k + 24)
            cols = slice(128 * k, 128 * k + 128)
            dmix_ref[pl.ds(at, 48), cols] = jnp.concatenate([t0[lines], t1[lines]], axis=0).astype(BF16)
            dmix_ref[pl.ds(half + at, 48), cols] = jnp.concatenate([s0[lines], s1[lines]], axis=0).astype(BF16)
        return carry

    lax.fori_loop(0, pairs // 2, lift, 0)

    def layer(b, carry):
        at = pl.multiple_of(b * 128, 128)
        spots = (pl.ds(at, 128), pl.ds(half + at, 128))

        def rows_of(ref, cols):
            return jnp.concatenate([ref[spot, cols] for spot in spots], axis=0)

        def put(col, value):
            value = value.astype(BF16)
            for i, spot in enumerate(spots):
                dd_ref[spot, col : col + 128] = value[128 * i : 128 * i + 128]

        gate = rows_of(gate_ref, slice(0, 128))
        dact0 = dot_nt(rows_of(dmix_ref, slice(0, 384)), b0_ref[...])
        h0 = rows_of(hid_ref, slice(0, 128))
        head = jax.nn.sigmoid(h0)
        put(0, dact0[:, 0:128] * head * (1.0 + h0 * (1.0 - head)))
        total = None

        def gated(k, piece, col):
            put(col, piece * gate)
            return piece * rows_of(hid_ref, slice(128 * k, 128 * k + 128))

        total = gated(1, dact0[:, 128:256], 128) + gated(2, dact0[:, 256:384], 256)
        dact1 = dot_nt(rows_of(dmix_ref, slice(384, 896)), b1_ref[...])
        for k in range(4):
            total = total + gated(3 + k, dact1[:, 128 * k : 128 * k + 128], 512 + 128 * k)
        dact2 = dot_nt(rows_of(dmix_ref, slice(896, 1152)), b2_ref[...])
        for k in range(2):
            total = total + gated(7 + k, dact2[:, 128 * k : 128 * k + 128], 1024 + 128 * k)
        put(384, total * gate * (1.0 - gate))

        first = 0
        for cols, w_ref, count in ((slice(0, 512), a0_ref, 3), (slice(512, 1024), a1_ref, 4), (slice(1024, 1280), a2_ref, 2)):
            dz = dot_nt(rows_of(dd_ref, cols), w_ref[...])
            for k in range(count):
                lo = dz[:, 256 * k : 256 * k + 128]
                hi = dz[:, 256 * k + 128 : 256 * k + 256]
                to = slice(128 * (first + k), 128 * (first + k) + 128)
                gs_ref[spots[0], to] = lo[:128] + hi[128:]
                gt_ref[spots[0], to] = hi[:128] + lo[128:]
            first += count
        return carry

    lax.fori_loop(0, half // 128, layer, 0)
    out_ref[...] = jnp.zeros(out_ref.shape, BF16)

    def unlift(p, carry):
        at = pl.multiple_of(p * 24, 8)
        s = own_ref[2 * p + 1]
        out_ref[s] = out_ref[s] + turn_back(vs_ref, p, gs_ref, at)
        t = own_ref[2 * p]
        out_ref[t] = out_ref[t] + turn_back(vt_ref, p, gt_ref, at)
        return carry

    lax.fori_loop(0, pairs, unlift, 0)

    def put_rows(row, value):
        wg_ref[row : row + value.shape[0], :] = (value * scale).astype(BF16)

    wg_ref[8064:8192, :] = jnp.zeros((128, 128), BF16)

    def plain(left_ref, left_at, height, right_ref, right_cols, row):
        for c in range(height // 128):
            g = dot_tn(left_ref[:, left_at + 128 * c : left_at + 128 * c + 128], right_ref[:, right_cols])
            for n in range(g.shape[1] // 128):
                put_rows(row + n * height + 128 * c, g[:, 128 * n : 128 * n + 128])

    def folded(left_ref, left_at, height, right_ref, right_cols, row):
        width = (right_cols.stop - right_cols.start) // 2
        blocks = width // 128
        for c in range(height // 128):
            low = left_at + 128 * c
            top = dot_tn(left_ref[:, low : low + 128], right_ref[:, right_cols])
            bot = dot_tn(left_ref[:, low + height : low + height + 128], right_ref[:, right_cols])
            same = top[:, :width] + bot[:, width:]
            cross = top[:, width:] - bot[:, :width]
            for n in range(blocks):
                cols = slice(128 * n, 128 * n + 128)
                put_rows(row + n * height + 128 * c, same[:, cols])
                put_rows(row + (blocks + n) * height + 128 * c, cross[:, cols])

    plain(z_ref, 0, 768, dd_ref, slice(0, 512), 0)
    folded(z_ref, 768, 512, dd_ref, slice(512, 1024), 3072)
    folded(z_ref, 1792, 256, dd_ref, slice(1024, 1280), 5120)
    plain(act_ref, 0, 384, dmix_ref, slice(0, 384), 5632)
    folded(act_ref, 384, 256, dmix_ref, slice(384, 896), 6784)
    folded(act_ref, 896, 128, dmix_ref, slice(896, 1152), 7808)


def backward(owners, got, turns, weights, kept, scale):
    peers = got.shape[0]
    rows = kept[0].shape[0]

    def body(*refs):
        backward_body(*refs, scale=scale)

    return pl.pallas_call(
        body,
        in_specs=[SM] + [VM] * 15,
        out_specs=[VM, VM],
        out_shape=[
            jax.ShapeDtypeStruct((peers, CH, 128), BF16),
            jax.ShapeDtypeStruct((WEIGHT_ROWS, 128), BF16),
        ],
        scratch_shapes=[
            pltpu.VMEM((rows, 1152), BF16),
            pltpu.VMEM((rows, 1280), BF16),
            pltpu.VMEM((rows // 2, 1152), F32),
            pltpu.VMEM((rows // 2, 1152), F32),
        ],
        compiler_params=pltpu.CompilerParams(vmem_limit_bytes=VMEM_LIMIT),
        cost_estimate=pl.CostEstimate(flops=2 * 10**10, transcendentals=10**6, bytes_accessed=3 * 10**7),
        name="backward",
    )(owners, got, *turns, *weights, *kept)


def scatter_body(idx_ref, got_ref, out_ref, acc_ref, last_ref):
    @pl.when(pl.program_id(0) == 0)
    def _():
        acc_ref[...] = jnp.zeros(acc_ref.shape, F32)
        last_ref[...] = jnp.zeros(last_ref.shape, F32)

    atom = lax.broadcasted_iota(jnp.int32, (128, 256), 0)
    kinds = [
        jnp.where(jnp.broadcast_to(idx_ref[v : v + 1, :], (128, 256)) == atom, 1.0, 0.0).astype(BF16)
        for v in range(4)
    ]
    tiles = [got_ref[:, 16 * t : 16 * t + 16, :].reshape(256, 128) for t in range(7)]
    acc_ref[...] += dot(kinds[0], jnp.concatenate(tiles, axis=1))
    spare = jnp.concatenate([jnp.concatenate([tiles[j], tiles[j + 3]], axis=1) for j in range(3)], axis=0)
    last_ref[...] += dot(jnp.concatenate(kinds[1:], axis=1), spare)

    @pl.when(pl.program_id(0) == pl.num_programs(0) - 1)
    def _():
        for k in range(7):
            out_ref[k] = acc_ref[:, 128 * k : 128 * k + 128].astype(out_ref.dtype)
        for k in range(2):
            out_ref[7 + k] = last_ref[:, 128 * k : 128 * k + 128].astype(out_ref.dtype)


def add_rows(idx_rows, got, dtype):
    peers = got.shape[0]
    return pl.pallas_call(
        scatter_body,
        grid=(peers // 16,),
        in_specs=[
            pl.BlockSpec((8, 256), lambda c: (0, c)),
            pl.BlockSpec((16, CH, 128), lambda c: (c, 0, 0)),
        ],
        out_specs=whole((9, 128, 128)),
        out_shape=jax.ShapeDtypeStruct((9, 128, 128), dtype),
        scratch_shapes=[pltpu.VMEM((128, 896), F32), pltpu.VMEM((128, 256), F32)],
        cost_estimate=pl.CostEstimate(flops=10**9, transcendentals=0, bytes_accessed=6 * 10**6),
        name="add_rows",
    )(idx_rows, got)


def moved(x, stride, step):
    count = lax.axis_size("atoms")
    plan = []
    for i in range(count):
        digit = (i // stride) % 4
        plan.append((i, i + ((digit + step) % 4 - digit) * stride))
    return lax.ppermute(x, "atoms", plan)


def swapped(x):
    return lax.ppermute(x, "atoms", [(i, i ^ 1) for i in range(lax.axis_size("atoms"))])


def add_and_split(place, pieces, base, scale_rows):
    rows = pieces[-1].shape[0] // 4

    def body(place_ref, *refs):
        ins, outs = refs[: len(pieces)], refs[len(pieces) :]
        for d in range(4):
            at = pl.multiple_of(((place_ref[0] + d) % 4) * rows, 8)
            total = None
            for n, ref in enumerate(ins):
                skip = place_ref[1] * scale_rows if (n == 0 and base) else 0
                value = ref[pl.ds(pl.multiple_of(skip + at, 8), rows), :].astype(F32)
                total = value if total is None else total + value
            outs[d][...] = total

    return pl.pallas_call(
        body,
        in_specs=[SM] + [VM] * len(pieces),
        out_specs=[VM] * 4,
        out_shape=[jax.ShapeDtypeStruct((rows, 128), F32)] * 4,
        cost_estimate=pl.CostEstimate(flops=10**6, transcendentals=0, bytes_accessed=3 * 10**6),
        name="add_and_split",
    )(place, *pieces)


def add_last(pieces):
    def body(*refs):
        total = refs[0][...]
        for ref in refs[1:-1]:
            total = total + ref[...]
        refs[-1][...] = total.astype(BF16)

    return pl.pallas_call(
        body,
        in_specs=[VM] * len(pieces),
        out_specs=VM,
        out_shape=jax.ShapeDtypeStruct(pieces[0].shape, BF16),
        name="add_last",
    )(*pieces)


def join(place, pieces):
    rows = pieces[0].shape[0]

    def body(place_ref, *refs):
        for d in range(4):
            at = pl.multiple_of(((place_ref[0] + 4 - d) % 4) * rows, 16)
            refs[4][pl.ds(at, rows), :] = refs[d][...]

    return pl.pallas_call(
        body,
        in_specs=[SM] + [VM] * 4,
        out_specs=VM,
        out_shape=jax.ShapeDtypeStruct((4 * rows, 128), BF16),
        name="join",
    )(place, *pieces)


WEIGHT_PARTS = (
    (0, 1, 768, 4), (3072, 2, 512, 2), (5120, 2, 256, 1), (5632, 1, 384, 3), (6784, 2, 256, 2), (7808, 2, 128, 1),
)


def unpack(core, mine, other):
    half = mine.shape[0]

    def body(core_ref, mine_ref, other_ref, *refs):
        outs, all_ref = refs[:-1], refs[-1]
        all_ref[pl.ds(pl.multiple_of(core_ref[0] * half, 16), half), :] = mine_ref[...]
        all_ref[pl.ds(pl.multiple_of((1 - core_ref[0]) * half, 16), half), :] = other_ref[...]
        for out, (row, parts, height, blocks) in zip(outs, WEIGHT_PARTS):
            for p in range(parts):
                for n in range(blocks):
                    low = row + (p * blocks + n) * height
                    out[p, :, 128 * n : 128 * n + 128] = all_ref[low : low + height, :].astype(F32)

    return pl.pallas_call(
        body,
        in_specs=[SM, VM, VM],
        out_specs=[VM] * 6,
        out_shape=[jax.ShapeDtypeStruct((parts, height, 128 * blocks), F32) for _, parts, height, blocks in WEIGHT_PARTS],
        scratch_shapes=[pltpu.VMEM((2 * half, 128), BF16)],
        compiler_params=pltpu.CompilerParams(vmem_limit_bytes=VMEM_LIMIT // 2),
        name="unpack",
    )(core, mine, other)


def sum_weights(grads):
    me = lax.axis_index("atoms").astype(jnp.int32)
    core = me % 2
    places = {stride: jnp.stack([(me // stride) % 4, core]) for stride in (32, 8, 2)}
    half = WEIGHT_ROWS // 2
    sent = lax.dynamic_slice_in_dim(grads, (1 - core) * half, half, axis=0)
    pieces = [grads, swapped(sent)]
    for stride in (32, 8, 2):
        parts = add_and_split(places[stride], pieces, stride == 32, half)
        pieces = [parts[0]] + [moved(parts[d], stride, d) for d in (1, 2, 3)]
    value = add_last(pieces)
    for stride in (2, 8, 32):
        value = join(places[stride], [value] + [moved(value, stride, d) for d in (1, 2, 3)])
    return unpack(jnp.stack([core, core]), value, swapped(value))


def widen_pair(w):
    upper = jnp.concatenate([w[0], w[1]], axis=1)
    lower = jnp.concatenate([-w[1], w[0]], axis=1)
    return jnp.concatenate([upper, lower], axis=0)


def exchange(x):
    return lax.all_to_all(x, "atoms", split_axis=0, concat_axis=0, tiled=True)


def local(
    features, cotangent, wigner, pair_blocks, pair_rows, edge_ends,
    first_m0, first_m1, first_m2, second_m0, second_m1, second_m2,
):
    peers = lax.axis_size("atoms")
    pairs = pair_blocks.shape[0]
    edges = edge_ends.shape[1]
    each = edges // pairs
    owners = pair_blocks.reshape(2 * pairs)
    ends = jnp.arange(2 * pairs, dtype=jnp.int32)
    slots = jnp.sum(
        jnp.logical_and(owners[:, None] == owners[None, :], ends[:, None] > ends[None, :]), axis=1
    ).astype(jnp.int32)

    end_rows = jnp.transpose(pair_rows, (2, 0, 1)).reshape(2 * pairs, 6)
    cols = request_columns()
    row_cols = jnp.concatenate([end_rows[:, max(c, 0) % 6 : max(c, 0) % 6 + 1] for c in cols], axis=1)
    col_slot = jnp.asarray(np.where(cols < 0, -1, cols // 6), jnp.int32)
    peer = jnp.arange(peers, dtype=jnp.int32)
    hit = jnp.logical_and(
        owners[None, :, None] == peer[:, None, None], slots[None, :, None] == col_slot[None, None, :]
    )
    request = jnp.sum(jnp.where(hit, row_cols[None] + 1, 0), axis=1) - 1
    asked = exchange(request)
    asked_rows = jnp.transpose(asked.reshape(peers, 4, 16), (1, 0, 2)).reshape(4, peers * 16)
    asked_rows = jnp.concatenate([asked_rows, asked_rows], axis=0)
    eye = jnp.eye(64, dtype=BF16)

    got_f = exchange(pick_rows(asked, eye, jnp.transpose(features, (1, 0, 2))))
    got_c = exchange(pick_rows(asked, eye, jnp.transpose(cotangent, (1, 0, 2))))

    turned = jnp.stack([wigner[i] for i in COEF_ORDER]).reshape(9, 9, pairs, each)
    pos = jnp.stack(
        [
            (slots.reshape(pairs, 2)[:, side, None] * 6 + edge_ends[side].reshape(pairs, each)).astype(F32)
            for side in range(2)
        ],
        axis=0,
    )
    pos = jnp.broadcast_to(pos[:, None], (2, 9, pairs, each))
    by_j = jnp.transpose(turned, (1, 0, 2, 3))
    gap5 = jnp.zeros((5, 9, pairs, each), F32)
    gap7 = jnp.zeros((7, 9, pairs, each), F32)
    table = jnp.concatenate([by_j, pos, gap5, by_j, gap7], axis=0)
    ra = jnp.transpose(table, (2, 1, 3, 0)).reshape(pairs, 9 * each, 32)
    ra = jnp.pad(ra, ((0, 0), (0, 224 - 9 * each), (0, 0)))
    rb = jnp.transpose(table, (2, 0, 1, 3)).reshape(pairs, 32, 9 * each)
    rb = jnp.pad(rb, ((0, 0), (0, 0), (0, 256 - 9 * each)))
    turns = build_turns(ra, rb)

    weights = (
        first_m0, widen_pair(first_m1), widen_pair(first_m2),
        second_m0, widen_pair(second_m1), widen_pair(second_m2),
    )
    back_m, *kept = forward(owners, got_f, turns, weights, 2 * edges)
    got_m = exchange(back_m)
    scale = float((2.0 * edges * peers) ** (-0.5))
    back_g, grads = backward(owners, got_c, turns, weights, kept, scale)
    back_g, got_m = lax.optimization_barrier((back_g, got_m))
    got_g = exchange(back_g)
    messages = jnp.transpose(add_rows(asked_rows, got_m, BF16), (1, 0, 2))
    w = sum_weights(grads)
    grad_features = jnp.transpose(add_rows(asked_rows, got_g, F32), (1, 0, 2))
    return (messages, grad_features, w[0][0], w[1], w[2], w[3][0], w[4], w[5])


def solution(mesh):
    rows = P("atoms", None, None)
    in_specs = (
        rows, rows, P(None, None, "atoms"), P("atoms", None), P(None, None, "atoms"), P(None, "atoms"),
        P(), P(), P(), P(), P(), P(),
    )
    out_specs = (rows, rows, P(), P(), P(), P(), P(), P())
    return jax.shard_map(local, mesh=mesh, in_specs=in_specs, out_specs=out_specs, check_vma=False)
```

```python
import jax
import jax.numpy as jnp
import numpy as np
from jax import lax
from jax.experimental import pallas as pl
from jax.experimental.pallas import tpu as pltpu
from jax.sharding import PartitionSpec as P

COEF_ORDER = (0, 2, 6, 3, 7, 1, 5, 8, 4)
F32 = jnp.float32
BF16 = jnp.bfloat16
CH = 112
WEIGHT_ROWS = 8192
WR = 32
VMEM_LIMIT = 58 * 1024 * 1024


def chunk_maps():
    coef = np.full((CH,), -1)
    row = np.full((CH,), -1)
    for line in range(CH):
        tile, at = divmod(line, 16)
        if at < 12:
            coef[line], row[line] = tile, at
        elif tile < 6:
            coef[line], row[line] = 7 + tile // 3, 4 * (tile % 3) + at - 12
    return coef, row


def spread_tables():
    coef, row = chunk_maps()
    spread = np.zeros((32, 256), np.float32)
    rows = np.full((256,), -1.0, np.float32)
    for half in range(2):
        for line in range(CH):
            if coef[line] >= 0:
                spread[16 * half + coef[line], CH * half + line] = 1.0
                rows[CH * half + line] = row[line]
    return spread, rows


def request_columns():
    cols = np.full((64,), -1)
    cols[:12] = np.arange(12)
    for j in range(3):
        cols[16 * (j + 1) + 12 : 16 * (j + 2)] = 4 * j + np.arange(4)
    return cols


def dot(a, b):
    return jnp.dot(a, b, preferred_element_type=F32)


def dot_nt(a, b):
    return lax.dot_general(a, b, (((1,), (1,)), ((), ())), preferred_element_type=F32)


def dot_tn(a, b):
    return lax.dot_general(a, b, (((0,), (0,)), ((), ())), preferred_element_type=F32)


def whole(shape):
    return pl.BlockSpec(shape, lambda *_: (0,) * len(shape))


VM = pl.BlockSpec(memory_space=pltpu.VMEM)
SM = pl.BlockSpec(memory_space=pltpu.SMEM)


def gather_body(idx_ref, eye_ref, feat_ref, out_ref):
    turned = dot_nt(eye_ref[...], idx_ref[...].astype(F32).astype(BF16))
    lane = lax.broadcasted_iota(jnp.int32, (64, 128), 1).astype(F32)
    picks = []
    for q in range(16):
        col = jnp.broadcast_to(turned[:, q : q + 1], (64, 128))
        picks.append(jnp.where(col == lane, 1.0, 0.0).astype(BF16))
    kinds = [jnp.concatenate([x[16 * v : 16 * v + 16] for x in picks], axis=0) for v in range(4)]
    for j in range(3):
        left = jnp.concatenate([kinds[0], kinds[j + 1]], axis=1)
        right = jnp.concatenate(
            [
                jnp.concatenate([feat_ref[j], feat_ref[j + 3]], axis=1),
                jnp.concatenate([feat_ref[7], feat_ref[8]], axis=1),
            ],
            axis=0,
        )
        got = dot(left, right).astype(BF16)
        out_ref[:, 16 * j : 16 * j + 16, :] = got[:, :128].reshape(16, 16, 128)
        out_ref[:, 16 * (j + 3) : 16 * (j + 4), :] = got[:, 128:].reshape(16, 16, 128)
    last = dot(kinds[0], feat_ref[6]).astype(BF16)
    out_ref[:, 96:112, :] = last.reshape(16, 16, 128)


def pick_rows(idx, eye, feat):
    peers = idx.shape[0]
    return pl.pallas_call(
        gather_body,
        grid=(peers // 16,),
        in_specs=[
            pl.BlockSpec((16, 64), lambda c: (c, 0)),
            whole((64, 64)),
            whole((9, 128, 128)),
        ],
        out_specs=pl.BlockSpec((16, CH, 128), lambda c: (c, 0, 0)),
        out_shape=jax.ShapeDtypeStruct((peers, CH, 128), BF16),
        cost_estimate=pl.CostEstimate(flops=2 * 10**9, transcendentals=0, bytes_accessed=4 * 10**6),
        name="pick_rows",
    )(idx, eye, feat)


def prep_body(ra_ref, rb_ref, sp_ref, spt_ref, rows_ref, rowst_ref, wt_ref, ws_ref, vt_ref, vs_ref):
    a = ra_ref[0]
    a_hi = a.astype(BF16)
    a_lo = (a - a_hi.astype(F32)).astype(BF16)
    lane = lax.broadcasted_iota(jnp.int32, (224, 32), 1)
    a_both = jnp.where(lane < 16, a_hi.astype(F32), a_lo.astype(F32)).astype(BF16)
    x = dot(a_both, sp_ref[...])
    rows = jnp.broadcast_to(rows_ref[0:1, :], (224, 256))
    for at, out in ((9, wt_ref), (10, ws_ref)):
        mine = jnp.broadcast_to(a[:, at : at + 1], (224, 256))
        out[0] = jnp.where(mine == rows, x, 0.0).astype(BF16)
    b = rb_ref[0]
    b_hi = b.astype(BF16)
    b_lo = (b - b_hi.astype(F32)).astype(BF16)
    line = lax.broadcasted_iota(jnp.int32, (32, 256), 0)
    b_both = jnp.where(line < 16, b_hi.astype(F32), b_lo.astype(F32)).astype(BF16)
    y = dot(spt_ref[...], b_both)
    rowst = jnp.broadcast_to(rowst_ref[:, 0:1], (224, 256))
    for at, out in ((9, vt_ref), (10, vs_ref)):
        mine = jnp.broadcast_to(b[at : at + 1, :], (224, 256))
        out[0] = jnp.where(mine == rowst, y, 0.0).astype(BF16)


def build_turns(ra, rb):
    pairs = ra.shape[0]
    spread, rows = spread_tables()
    sp = jnp.asarray(spread, BF16)
    spt = jnp.asarray(spread[:, :224].T, BF16)
    rows8 = jnp.asarray(np.tile(rows[None], (8, 1)), F32)
    rowst = jnp.asarray(np.tile(rows[:224, None], (1, 128)), F32)
    one = jax.ShapeDtypeStruct((pairs, 224, 256), BF16)
    block = pl.BlockSpec((1, 224, 256), lambda p: (p, 0, 0))
    return pl.pallas_call(
        prep_body,
        grid=(pairs,),
        in_specs=[
            pl.BlockSpec((1, 224, 32), lambda p: (p, 0, 0)),
            pl.BlockSpec((1, 32, 256), lambda p: (p, 0, 0)),
            whole((32, 256)),
            whole((224, 32)),
            whole((8, 256)),
            whole((224, 128)),
        ],
        out_specs=[block] * 4,
        out_shape=[one] * 4,
        cost_estimate=pl.CostEstimate(flops=10**9, transcendentals=0, bytes_accessed=10**7),
        name="build_turns",
    )(ra, rb, sp, spt, rows8, rowst)


def turn(w_ref, r_ref, pair, owner):
    chunk = r_ref[owner]
    right = jnp.concatenate([chunk, chunk, jnp.zeros((32, 128), BF16)], axis=0)
    return dot(w_ref[pair], right)


def turn_back(v_ref, pair, src_ref, base):
    parts = [src_ref[pl.ds(base, 24), 128 * k : 128 * k + 128] for k in range(9)]
    x = jnp.concatenate(parts + [jnp.zeros((40, 128), F32)], axis=0)
    hi = x.astype(BF16)
    lo = (x - hi.astype(F32)).astype(BF16)
    y = dot(v_ref[pair], jnp.concatenate([hi, lo], axis=1))
    y = y[:, :128] + y[:, 128:]
    return (y[:CH] + y[CH:]).astype(BF16)


def forward_body(
    own_ref, r_ref, wt_ref, ws_ref, vt_ref, vs_ref, a0_ref, a1_ref, a2_ref, b0_ref, b1_ref, b2_ref,
    out_ref, z_ref, hid_ref, gate_ref, act_ref, mix_ref,
):
    half = z_ref.shape[0] // 2
    pairs = wt_ref.shape[0]

    def lift(d, carry):
        turned = []
        for p in (2 * d, 2 * d + 1):
            turned.append((turn(ws_ref, r_ref, p, own_ref[2 * p + 1]), turn(wt_ref, r_ref, p, own_ref[2 * p])))
        (s0, t0), (s1, t1) = turned
        at = pl.multiple_of(d * 48, 16)
        for k in range(9):
            lines = slice(24 * k, 24 * k + 24)
            s = jnp.concatenate([s0[lines], s1[lines]], axis=0).astype(BF16)
            t = jnp.concatenate([t0[lines], t1[lines]], axis=0).astype(BF16)
            z_ref[pl.ds(at, 48), 256 * k : 256 * k + 128] = s
            z_ref[pl.ds(at, 48), 256 * k + 128 : 256 * k + 256] = t
            z_ref[pl.ds(half + at, 48), 256 * k : 256 * k + 128] = t
            z_ref[pl.ds(half + at, 48), 256 * k + 128 : 256 * k + 256] = s
        return carry

    lax.fori_loop(0, pairs // 2, lift, 0)

    def layer(b, carry):
        at = pl.multiple_of(b * 256, 256)
        here = pl.ds(at, 256)
        o = dot(z_ref[here, 0:768], a0_ref[...])
        gate = jax.nn.sigmoid(o[:, 384:512])
        gate_ref[here, :] = gate
        h0 = o[:, 0:128]
        hid_ref[here, 0:384] = o[:, 0:384]
        act_ref[here, 0:128] = (h0 * jax.nn.sigmoid(h0)).astype(BF16)
        for k in range(1, 3):
            cols = slice(128 * k, 128 * k + 128)
            act_ref[here, cols] = (o[:, cols] * gate).astype(BF16)
        h1 = dot(z_ref[here, 768:1792], a1_ref[...])
        hid_ref[here, 384:896] = h1
        for k in range(4):
            act_ref[here, 384 + 128 * k : 512 + 128 * k] = (h1[:, 128 * k : 128 * k + 128] * gate).astype(BF16)
        h2 = dot(z_ref[here, 1792:2304], a2_ref[...])
        hid_ref[here, 896:1152] = h2
        for k in range(2):
            act_ref[here, 896 + 128 * k : 1024 + 128 * k] = (h2[:, 128 * k : 128 * k + 128] * gate).astype(BF16)
        mix_ref[here, 0:384] = dot(act_ref[here, 0:384], b0_ref[...])
        mix_ref[here, 384:896] = dot(act_ref[here, 384:896], b1_ref[...])
        mix_ref[here, 896:1152] = dot(act_ref[here, 896:1152], b2_ref[...])
        return carry

    lax.fori_loop(0, z_ref.shape[0] // 256, layer, 0)
    out_ref[...] = jnp.zeros(out_ref.shape, BF16)

    def unlift(p, carry):
        at = pl.multiple_of(p * 24, 8)
        t = own_ref[2 * p]
        out_ref[t] = out_ref[t] + turn_back(vt_ref, p, mix_ref, at)
        s = own_ref[2 * p + 1]
        out_ref[s] = out_ref[s] + turn_back(vs_ref, p, mix_ref, half + at)
        return carry

    lax.fori_loop(0, pairs, unlift, 0)


def forward(owners, got, turns, weights, rows):
    peers = got.shape[0]
    return pl.pallas_call(
        forward_body,
        in_specs=[SM] + [VM] * 11,
        out_specs=[VM] * 5,
        out_shape=[
            jax.ShapeDtypeStruct((peers, CH, 128), BF16),
            jax.ShapeDtypeStruct((rows, 2304), BF16),
            jax.ShapeDtypeStruct((rows, 1152), F32),
            jax.ShapeDtypeStruct((rows, 128), F32),
            jax.ShapeDtypeStruct((rows, 1152), BF16),
        ],
        scratch_shapes=[pltpu.VMEM((rows, 1152), F32)],
        compiler_params=pltpu.CompilerParams(vmem_limit_bytes=VMEM_LIMIT),
        cost_estimate=pl.CostEstimate(flops=10**10, transcendentals=10**6, bytes_accessed=3 * 10**7),
        name="forward",
    )(owners, got, *turns, *weights)


def backward_body(
    own_ref, r_ref, wt_ref, ws_ref, vt_ref, vs_ref, a0_ref, a1_ref, a2_ref, b0_ref, b1_ref, b2_ref,
    z_ref, hid_ref, gate_ref, act_ref, out_ref, wg_ref, dmix_ref, dd_ref, gs_ref, gt_ref, *, scale,
):
    half = z_ref.shape[0] // 2
    pairs = wt_ref.shape[0]

    def lift(d, carry):
        turned = []
        for p in (2 * d, 2 * d + 1):
            turned.append((turn(wt_ref, r_ref, p, own_ref[2 * p]), turn(ws_ref, r_ref, p, own_ref[2 * p + 1])))
        (t0, s0), (t1, s1) = turned
        at = pl.multiple_of(d * 48, 16)
        for k in range(9):
            lines = slice(24 * k, 24 * k + 24)
            cols = slice(128 * k, 128 * k + 128)
            dmix_ref[pl.ds(at, 48), cols] = jnp.concatenate([t0[lines], t1[lines]], axis=0).astype(BF16)
            dmix_ref[pl.ds(half + at, 48), cols] = jnp.concatenate([s0[lines], s1[lines]], axis=0).astype(BF16)
        return carry

    lax.fori_loop(0, pairs // 2, lift, 0)

    def layer(b, carry):
        at = pl.multiple_of(b * 128, 128)
        spots = (pl.ds(at, 128), pl.ds(half + at, 128))

        def rows_of(ref, cols):
            return jnp.concatenate([ref[spot, cols] for spot in spots], axis=0)

        def put(col, value):
            value = value.astype(BF16)
            for i, spot in enumerate(spots):
                dd_ref[spot, col : col + 128] = value[128 * i : 128 * i + 128]

        gate = rows_of(gate_ref, slice(0, 128))
        dact0 = dot_nt(rows_of(dmix_ref, slice(0, 384)), b0_ref[...])
        h0 = rows_of(hid_ref, slice(0, 128))
        head = jax.nn.sigmoid(h0)
        put(0, dact0[:, 0:128] * head * (1.0 + h0 * (1.0 - head)))
        total = None

        def gated(k, piece, col):
            put(col, piece * gate)
            return piece * rows_of(hid_ref, slice(128 * k, 128 * k + 128))

        total = gated(1, dact0[:, 128:256], 128) + gated(2, dact0[:, 256:384], 256)
        dact1 = dot_nt(rows_of(dmix_ref, slice(384, 896)), b1_ref[...])
        for k in range(4):
            total = total + gated(3 + k, dact1[:, 128 * k : 128 * k + 128], 512 + 128 * k)
        dact2 = dot_nt(rows_of(dmix_ref, slice(896, 1152)), b2_ref[...])
        for k in range(2):
            total = total + gated(7 + k, dact2[:, 128 * k : 128 * k + 128], 1024 + 128 * k)
        put(384, total * gate * (1.0 - gate))

        first = 0
        for cols, w_ref, count in ((slice(0, 512), a0_ref, 3), (slice(512, 1024), a1_ref, 4), (slice(1024, 1280), a2_ref, 2)):
            dz = dot_nt(rows_of(dd_ref, cols), w_ref[...])
            for k in range(count):
                lo = dz[:, 256 * k : 256 * k + 128]
                hi = dz[:, 256 * k + 128 : 256 * k + 256]
                to = slice(128 * (first + k), 128 * (first + k) + 128)
                gs_ref[spots[0], to] = lo[:128] + hi[128:]
                gt_ref[spots[0], to] = hi[:128] + lo[128:]
            first += count
        return carry

    lax.fori_loop(0, half // 128, layer, 0)
    out_ref[...] = jnp.zeros(out_ref.shape, BF16)

    def unlift(p, carry):
        at = pl.multiple_of(p * 24, 8)
        s = own_ref[2 * p + 1]
        out_ref[s] = out_ref[s] + turn_back(vs_ref, p, gs_ref, at)
        t = own_ref[2 * p]
        out_ref[t] = out_ref[t] + turn_back(vt_ref, p, gt_ref, at)
        return carry

    lax.fori_loop(0, pairs, unlift, 0)

    def put_rows(row, value):
        wg_ref[row : row + value.shape[0], :] = (value * scale).astype(BF16)

    wg_ref[8064:8192, :] = jnp.zeros((128, 128), BF16)

    def plain(left_ref, left_at, height, right_ref, right_cols, row):
        for c in range(height // 128):
            g = dot_tn(left_ref[:, left_at + 128 * c : left_at + 128 * c + 128], right_ref[:, right_cols])
            for n in range(g.shape[1] // 128):
                put_rows(row + n * height + 128 * c, g[:, 128 * n : 128 * n + 128])

    def folded(left_ref, left_at, height, right_ref, right_cols, row):
        width = (right_cols.stop - right_cols.start) // 2
        blocks = width // 128
        for c in range(height // 128):
            low = left_at + 128 * c
            top = dot_tn(left_ref[:, low : low + 128], right_ref[:, right_cols])
            bot = dot_tn(left_ref[:, low + height : low + height + 128], right_ref[:, right_cols])
            same = top[:, :width] + bot[:, width:]
            cross = top[:, width:] - bot[:, :width]
            for n in range(blocks):
                cols = slice(128 * n, 128 * n + 128)
                put_rows(row + n * height + 128 * c, same[:, cols])
                put_rows(row + (blocks + n) * height + 128 * c, cross[:, cols])

    plain(z_ref, 0, 768, dd_ref, slice(0, 512), 0)
    folded(z_ref, 768, 512, dd_ref, slice(512, 1024), 3072)
    folded(z_ref, 1792, 256, dd_ref, slice(1024, 1280), 5120)
    plain(act_ref, 0, 384, dmix_ref, slice(0, 384), 5632)
    folded(act_ref, 384, 256, dmix_ref, slice(384, 896), 6784)
    folded(act_ref, 896, 128, dmix_ref, slice(896, 1152), 7808)


def backward(owners, got, turns, weights, kept, scale):
    peers = got.shape[0]
    rows = kept[0].shape[0]

    def body(*refs):
        backward_body(*refs, scale=scale)

    return pl.pallas_call(
        body,
        in_specs=[SM] + [VM] * 15,
        out_specs=[VM, VM],
        out_shape=[
            jax.ShapeDtypeStruct((peers, CH, 128), BF16),
            jax.ShapeDtypeStruct((WEIGHT_ROWS, 128), BF16),
        ],
        scratch_shapes=[
            pltpu.VMEM((rows, 1152), BF16),
            pltpu.VMEM((rows, 1280), BF16),
            pltpu.VMEM((rows // 2, 1152), F32),
            pltpu.VMEM((rows // 2, 1152), F32),
        ],
        compiler_params=pltpu.CompilerParams(vmem_limit_bytes=VMEM_LIMIT),
        cost_estimate=pl.CostEstimate(flops=2 * 10**10, transcendentals=10**6, bytes_accessed=3 * 10**7),
        name="backward",
    )(owners, got, *turns, *weights, *kept)


def scatter_body(idx_ref, got_ref, out_ref, acc_ref, last_ref):
    @pl.when(pl.program_id(0) == 0)
    def _():
        acc_ref[...] = jnp.zeros(acc_ref.shape, F32)
        last_ref[...] = jnp.zeros(last_ref.shape, F32)

    atom = lax.broadcasted_iota(jnp.int32, (128, 256), 0)
    kinds = [
        jnp.where(jnp.broadcast_to(idx_ref[v : v + 1, :], (128, 256)) == atom, 1.0, 0.0).astype(BF16)
        for v in range(4)
    ]
    tiles = [got_ref[:, 16 * t : 16 * t + 16, :].reshape(256, 128) for t in range(7)]
    acc_ref[...] += dot(kinds[0], jnp.concatenate(tiles, axis=1))
    spare = jnp.concatenate([jnp.concatenate([tiles[j], tiles[j + 3]], axis=1) for j in range(3)], axis=0)
    last_ref[...] += dot(jnp.concatenate(kinds[1:], axis=1), spare)

    @pl.when(pl.program_id(0) == pl.num_programs(0) - 1)
    def _():
        for k in range(7):
            out_ref[k] = acc_ref[:, 128 * k : 128 * k + 128].astype(out_ref.dtype)
        for k in range(2):
            out_ref[7 + k] = last_ref[:, 128 * k : 128 * k + 128].astype(out_ref.dtype)


def add_rows(idx_rows, got, dtype):
    peers = got.shape[0]
    return pl.pallas_call(
        scatter_body,
        grid=(peers // 16,),
        in_specs=[
            pl.BlockSpec((8, 256), lambda c: (0, c)),
            pl.BlockSpec((16, CH, 128), lambda c: (c, 0, 0)),
        ],
        out_specs=whole((9, 128, 128)),
        out_shape=jax.ShapeDtypeStruct((9, 128, 128), dtype),
        scratch_shapes=[pltpu.VMEM((128, 896), F32), pltpu.VMEM((128, 256), F32)],
        cost_estimate=pl.CostEstimate(flops=10**9, transcendentals=0, bytes_accessed=6 * 10**6),
        name="add_rows",
    )(idx_rows, got)


def swapped(x):
    return lax.ppermute(x, "atoms", [(i, i ^ 1) for i in range(lax.axis_size("atoms"))])


def add_pair(core, grads, other):
    half = other.shape[0]

    def body(core_ref, grads_ref, other_ref, out_ref):
        mine = grads_ref[pl.ds(pl.multiple_of(core_ref[0] * half, 16), half), :]
        total = mine.astype(F32) + other_ref[...].astype(F32)
        out_ref[...] = total.astype(BF16).reshape(half // WR, WR, 128)

    return pl.pallas_call(
        body,
        in_specs=[SM, VM, VM],
        out_specs=VM,
        out_shape=jax.ShapeDtypeStruct((half // WR, WR, 128), BF16),
        cost_estimate=pl.CostEstimate(flops=10**6, transcendentals=0, bytes_accessed=4 * 10**6),
        name="add_pair",
    )(core, grads, other)


def add_peers(got):
    peers = got.shape[0]
    chips = peers // 2

    def body(got_ref, out_ref):
        x = got_ref[...].astype(F32).reshape(chips, 2, 16, 128)
        total = jnp.sum(x, axis=0).astype(BF16)
        out_ref[...] = jnp.broadcast_to(total[None], (chips, 2, 16, 128))

    return pl.pallas_call(
        body,
        grid=(WR // 16,),
        in_specs=[pl.BlockSpec((peers, 16, 128), lambda i: (0, CH // 16 + i, 0))],
        out_specs=pl.BlockSpec((chips, 2, 16, 128), lambda i: (0, 0, i, 0)),
        out_shape=jax.ShapeDtypeStruct((chips, 2, WR, 128), BF16),
        cost_estimate=pl.CostEstimate(flops=10**6, transcendentals=0, bytes_accessed=3 * 10**6),
        name="add_peers",
    )(got)


WEIGHT_PARTS = (
    (0, 1, 768, 4), (3072, 2, 512, 2), (5120, 2, 256, 1), (5632, 1, 384, 3), (6784, 2, 256, 2), (7808, 2, 128, 1),
)


def unpack(core, mine, other):
    chips = mine.shape[0]

    def body(core_ref, mine_ref, other_ref, *refs):
        outs, all_ref = refs[:-1], refs[-1]

        def place(chip, carry):
            for half in range(2):
                at = half * 2 * chips + 2 * chip
                all_ref[at + core_ref[0]] = mine_ref[chip, half]
                all_ref[at + 1 - core_ref[0]] = other_ref[chip, half]
            return carry

        lax.fori_loop(0, chips, place, 0, unroll=4)
        for out, (row, parts, height, blocks) in zip(outs, WEIGHT_PARTS):
            for p in range(parts):
                for n in range(blocks):
                    low = (row + (p * blocks + n) * height) // WR
                    value = all_ref[low : low + height // WR].reshape(height, 128)
                    out[p, :, 128 * n : 128 * n + 128] = value.astype(F32)

    return pl.pallas_call(
        body,
        in_specs=[SM, VM, VM],
        out_specs=[VM] * 6,
        out_shape=[jax.ShapeDtypeStruct((parts, height, 128 * blocks), F32) for _, parts, height, blocks in WEIGHT_PARTS],
        scratch_shapes=[pltpu.VMEM((4 * chips, WR, 128), BF16)],
        compiler_params=pltpu.CompilerParams(vmem_limit_bytes=VMEM_LIMIT // 2),
        cost_estimate=pl.CostEstimate(flops=10**6, transcendentals=0, bytes_accessed=6 * 10**6),
        name="unpack",
    )(core, mine, other)


def widen_pair(w):
    upper = jnp.concatenate([w[0], w[1]], axis=1)
    lower = jnp.concatenate([-w[1], w[0]], axis=1)
    return jnp.concatenate([upper, lower], axis=0)


def exchange(x):
    return lax.all_to_all(x, "atoms", split_axis=0, concat_axis=0, tiled=True)


def local(
    features, cotangent, wigner, pair_blocks, pair_rows, edge_ends,
    first_m0, first_m1, first_m2, second_m0, second_m1, second_m2,
):
    peers = lax.axis_size("atoms")
    pairs = pair_blocks.shape[0]
    edges = edge_ends.shape[1]
    each = edges // pairs
    owners = pair_blocks.reshape(2 * pairs)
    ends = jnp.arange(2 * pairs, dtype=jnp.int32)
    slots = jnp.sum(
        jnp.logical_and(owners[:, None] == owners[None, :], ends[:, None] > ends[None, :]), axis=1
    ).astype(jnp.int32)

    end_rows = jnp.transpose(pair_rows, (2, 0, 1)).reshape(2 * pairs, 6)
    cols = request_columns()
    row_cols = jnp.concatenate([end_rows[:, max(c, 0) % 6 : max(c, 0) % 6 + 1] for c in cols], axis=1)
    col_slot = jnp.asarray(np.where(cols < 0, -1, cols // 6), jnp.int32)
    peer = jnp.arange(peers, dtype=jnp.int32)
    hit = jnp.logical_and(
        owners[None, :, None] == peer[:, None, None], slots[None, :, None] == col_slot[None, None, :]
    )
    request = jnp.sum(jnp.where(hit, row_cols[None] + 1, 0), axis=1) - 1
    asked = exchange(request)
    asked_rows = jnp.transpose(asked.reshape(peers, 4, 16), (1, 0, 2)).reshape(4, peers * 16)
    asked_rows = jnp.concatenate([asked_rows, asked_rows], axis=0)
    eye = jnp.eye(64, dtype=BF16)

    got_f = exchange(pick_rows(asked, eye, jnp.transpose(features, (1, 0, 2))))
    got_c = exchange(pick_rows(asked, eye, jnp.transpose(cotangent, (1, 0, 2))))

    turned = jnp.stack([wigner[i] for i in COEF_ORDER]).reshape(9, 9, pairs, each)
    pos = jnp.stack(
        [
            (slots.reshape(pairs, 2)[:, side, None] * 6 + edge_ends[side].reshape(pairs, each)).astype(F32)
            for side in range(2)
        ],
        axis=0,
    )
    pos = jnp.broadcast_to(pos[:, None], (2, 9, pairs, each))
    by_j = jnp.transpose(turned, (1, 0, 2, 3))
    gap5 = jnp.zeros((5, 9, pairs, each), F32)
    gap7 = jnp.zeros((7, 9, pairs, each), F32)
    table = jnp.concatenate([by_j, pos, gap5, by_j, gap7], axis=0)
    ra = jnp.transpose(table, (2, 1, 3, 0)).reshape(pairs, 9 * each, 32)
    ra = jnp.pad(ra, ((0, 0), (0, 224 - 9 * each), (0, 0)))
    rb = jnp.transpose(table, (2, 0, 1, 3)).reshape(pairs, 32, 9 * each)
    rb = jnp.pad(rb, ((0, 0), (0, 0), (0, 256 - 9 * each)))
    turns = build_turns(ra, rb)

    weights = (
        first_m0, widen_pair(first_m1), widen_pair(first_m2),
        second_m0, widen_pair(second_m1), widen_pair(second_m2),
    )
    back_m, *kept = forward(owners, got_f, turns, weights, 2 * edges)
    got_m = exchange(back_m)
    scale = float((2.0 * edges * peers) ** (-0.5))
    back_g, grads = backward(owners, got_c, turns, weights, kept, scale)
    core = (lax.axis_index("atoms") % 2).astype(jnp.int32)
    cores = jnp.stack([core, core])
    half = WEIGHT_ROWS // 2
    sent = lax.dynamic_slice_in_dim(grads, (1 - core) * half, half, axis=0)
    w_rows = add_pair(cores, grads, swapped(sent))
    both = jnp.concatenate([back_g, w_rows], axis=1)
    both, got_m = lax.optimization_barrier((both, got_m))
    messages = add_rows(asked_rows, got_m, BF16)
    got_g, messages = lax.optimization_barrier((exchange(both), messages))
    same_core = [list(range(c, peers, 2)) for c in range(2)]
    w_mine = lax.all_to_all(
        add_peers(got_g).reshape(peers // 2, 2 * WR, 128), "atoms",
        split_axis=0, concat_axis=0, tiled=True, axis_index_groups=same_core,
    ).reshape(peers // 2, 2, WR, 128)
    grad_features = add_rows(asked_rows, got_g, F32)
    w_mine, grad_features = lax.optimization_barrier((w_mine, grad_features))
    messages = jnp.transpose(messages, (1, 0, 2))
    grad_features = jnp.transpose(grad_features, (1, 0, 2))
    w = unpack(cores, w_mine, swapped(w_mine))
    return (messages, grad_features, w[0][0], w[1], w[2], w[3][0], w[4], w[5])


def solution(mesh):
    rows = P("atoms", None, None)
    in_specs = (
        rows, rows, P(None, None, "atoms"), P("atoms", None), P(None, None, "atoms"), P(None, "atoms"),
        P(), P(), P(), P(), P(), P(),
    )
    out_specs = (rows, rows, P(), P(), P(), P(), P(), P())
    return jax.shard_map(local, mesh=mesh, in_specs=in_specs, out_specs=out_specs, check_vma=False)
```

```python
import jax
import jax.numpy as jnp
import numpy as np
from jax import lax
from jax.experimental import pallas as pl
from jax.experimental.pallas import tpu as pltpu
from jax.sharding import PartitionSpec as P

COEF_ORDER = (0, 2, 6, 3, 7, 1, 5, 8, 4)
F32 = jnp.float32
BF16 = jnp.bfloat16
CH = 112
WEIGHT_ROWS = 8192
WR = 32
PICK = 64
VMEM_LIMIT = 58 * 1024 * 1024


def chunk_maps():
    coef = np.full((CH,), -1)
    row = np.full((CH,), -1)
    for line in range(CH):
        tile, at = divmod(line, 16)
        if at < 12:
            coef[line], row[line] = tile, at
        elif tile < 6:
            coef[line], row[line] = 7 + tile // 3, 4 * (tile % 3) + at - 12
    return coef, row


def spread_tables():
    coef, row = chunk_maps()
    spread = np.zeros((32, 256), np.float32)
    rows = np.full((256,), -1.0, np.float32)
    for half in range(2):
        for line in range(CH):
            if coef[line] >= 0:
                spread[16 * half + coef[line], CH * half + line] = 1.0
                rows[CH * half + line] = row[line]
    return spread, rows


def request_columns():
    cols = np.full((64,), -1)
    cols[:12] = np.arange(12)
    for j in range(3):
        cols[16 * (j + 1) + 12 : 16 * (j + 2)] = 4 * j + np.arange(4)
    return cols


def dot(a, b):
    return jnp.dot(a, b, preferred_element_type=F32)


def dot_nt(a, b):
    return lax.dot_general(a, b, (((1,), (1,)), ((), ())), preferred_element_type=F32)


def dot_tn(a, b):
    return lax.dot_general(a, b, (((0,), (0,)), ((), ())), preferred_element_type=F32)


def whole(shape):
    return pl.BlockSpec(shape, lambda *_: (0,) * len(shape))


VM = pl.BlockSpec(memory_space=pltpu.VMEM)
SM = pl.BlockSpec(memory_space=pltpu.SMEM)


def gather_body(idx_ref, eye_ref, feat_ref, out_ref):
    turned = dot_nt(eye_ref[...], idx_ref[...].astype(F32).astype(BF16))
    lane = lax.broadcasted_iota(jnp.int32, (64, 128), 1).astype(F32)
    picks = []
    for q in range(PICK):
        col = jnp.broadcast_to(turned[:, q : q + 1], (64, 128))
        picks.append(jnp.where(col == lane, 1.0, 0.0).astype(BF16))
    kinds = [jnp.concatenate([x[16 * v : 16 * v + 16] for x in picks], axis=0) for v in range(4)]
    for j in range(3):
        left = jnp.concatenate([kinds[0], kinds[j + 1]], axis=1)
        right = jnp.concatenate(
            [
                jnp.concatenate([feat_ref[j], feat_ref[j + 3]], axis=1),
                jnp.concatenate([feat_ref[7], feat_ref[8]], axis=1),
            ],
            axis=0,
        )
        got = dot(left, right).astype(BF16)
        out_ref[:, 16 * j : 16 * j + 16, :] = got[:, :128].reshape(PICK, 16, 128)
        out_ref[:, 16 * (j + 3) : 16 * (j + 4), :] = got[:, 128:].reshape(PICK, 16, 128)
    last = dot(kinds[0], feat_ref[6]).astype(BF16)
    out_ref[:, 96:112, :] = last.reshape(PICK, 16, 128)


def pick_rows(idx, eye, feat):
    peers = idx.shape[0]
    return pl.pallas_call(
        gather_body,
        grid=(peers // PICK,),
        in_specs=[
            pl.BlockSpec((PICK, 64), lambda c: (c, 0)),
            whole((64, 64)),
            whole((9, 128, 128)),
        ],
        out_specs=pl.BlockSpec((PICK, CH, 128), lambda c: (c, 0, 0)),
        out_shape=jax.ShapeDtypeStruct((peers, CH, 128), BF16),
        compiler_params=pltpu.CompilerParams(vmem_limit_bytes=VMEM_LIMIT // 2),
        cost_estimate=pl.CostEstimate(flops=2 * 10**9, transcendentals=0, bytes_accessed=4 * 10**6),
        name="pick_rows",
    )(idx, eye, feat)


def prep_body(ra_ref, rb_ref, sp_ref, spt_ref, rows_ref, rowst_ref, wt_ref, ws_ref, vt_ref, vs_ref):
    a = ra_ref[0]
    a_hi = a.astype(BF16)
    a_lo = (a - a_hi.astype(F32)).astype(BF16)
    lane = lax.broadcasted_iota(jnp.int32, (224, 32), 1)
    a_both = jnp.where(lane < 16, a_hi.astype(F32), a_lo.astype(F32)).astype(BF16)
    x = dot(a_both, sp_ref[...])
    rows = jnp.broadcast_to(rows_ref[0:1, :], (224, 256))
    for at, out in ((9, wt_ref), (10, ws_ref)):
        mine = jnp.broadcast_to(a[:, at : at + 1], (224, 256))
        out[0] = jnp.where(mine == rows, x, 0.0).astype(BF16)
    b = rb_ref[0]
    b_hi = b.astype(BF16)
    b_lo = (b - b_hi.astype(F32)).astype(BF16)
    line = lax.broadcasted_iota(jnp.int32, (32, 256), 0)
    b_both = jnp.where(line < 16, b_hi.astype(F32), b_lo.astype(F32)).astype(BF16)
    y = dot(spt_ref[...], b_both)
    rowst = jnp.broadcast_to(rowst_ref[:, 0:1], (224, 256))
    for at, out in ((9, vt_ref), (10, vs_ref)):
        mine = jnp.broadcast_to(b[at : at + 1, :], (224, 256))
        out[0] = jnp.where(mine == rowst, y, 0.0).astype(BF16)


def build_turns(ra, rb):
    pairs = ra.shape[0]
    spread, rows = spread_tables()
    sp = jnp.asarray(spread, BF16)
    spt = jnp.asarray(spread[:, :224].T, BF16)
    rows8 = jnp.asarray(np.tile(rows[None], (8, 1)), F32)
    rowst = jnp.asarray(np.tile(rows[:224, None], (1, 128)), F32)
    one = jax.ShapeDtypeStruct((pairs, 224, 256), BF16)
    block = pl.BlockSpec((1, 224, 256), lambda p: (p, 0, 0))
    return pl.pallas_call(
        prep_body,
        grid=(pairs,),
        in_specs=[
            pl.BlockSpec((1, 224, 32), lambda p: (p, 0, 0)),
            pl.BlockSpec((1, 32, 256), lambda p: (p, 0, 0)),
            whole((32, 256)),
            whole((224, 32)),
            whole((8, 256)),
            whole((224, 128)),
        ],
        out_specs=[block] * 4,
        out_shape=[one] * 4,
        cost_estimate=pl.CostEstimate(flops=10**9, transcendentals=0, bytes_accessed=10**7),
        name="build_turns",
    )(ra, rb, sp, spt, rows8, rowst)


def turn(w_ref, r_ref, pair, owner):
    chunk = r_ref[owner]
    right = jnp.concatenate([chunk, chunk, jnp.zeros((32, 128), BF16)], axis=0)
    return dot(w_ref[pair], right)


def turn_back(v_ref, pair, src_ref, base):
    parts = [src_ref[pl.ds(base, 24), 128 * k : 128 * k + 128] for k in range(9)]
    x = jnp.concatenate(parts + [jnp.zeros((40, 128), F32)], axis=0)
    hi = x.astype(BF16)
    lo = (x - hi.astype(F32)).astype(BF16)
    y = dot(v_ref[pair], jnp.concatenate([hi, lo], axis=1))
    y = y[:, :128] + y[:, 128:]
    return (y[:CH] + y[CH:]).astype(BF16)


def forward_body(
    own_ref, r_ref, wt_ref, ws_ref, vt_ref, vs_ref, a0_ref, a1_ref, a2_ref, b0_ref, b1_ref, b2_ref,
    out_ref, z_ref, hid_ref, gate_ref, act_ref, mix_ref,
):
    half = z_ref.shape[0] // 2
    pairs = wt_ref.shape[0]

    def lift(d, carry):
        turned = []
        for p in (2 * d, 2 * d + 1):
            turned.append((turn(ws_ref, r_ref, p, own_ref[2 * p + 1]), turn(wt_ref, r_ref, p, own_ref[2 * p])))
        (s0, t0), (s1, t1) = turned
        at = pl.multiple_of(d * 48, 16)
        for k in range(9):
            lines = slice(24 * k, 24 * k + 24)
            s = jnp.concatenate([s0[lines], s1[lines]], axis=0).astype(BF16)
            t = jnp.concatenate([t0[lines], t1[lines]], axis=0).astype(BF16)
            z_ref[pl.ds(at, 48), 256 * k : 256 * k + 128] = s
            z_ref[pl.ds(at, 48), 256 * k + 128 : 256 * k + 256] = t
            z_ref[pl.ds(half + at, 48), 256 * k : 256 * k + 128] = t
            z_ref[pl.ds(half + at, 48), 256 * k + 128 : 256 * k + 256] = s
        return carry

    lax.fori_loop(0, pairs // 2, lift, 0)

    def layer(b, carry):
        at = pl.multiple_of(b * 256, 256)
        here = pl.ds(at, 256)
        o = dot(z_ref[here, 0:768], a0_ref[...])
        gate = jax.nn.sigmoid(o[:, 384:512])
        gate_ref[here, :] = gate
        h0 = o[:, 0:128]
        hid_ref[here, 0:384] = o[:, 0:384]
        act_ref[here, 0:128] = (h0 * jax.nn.sigmoid(h0)).astype(BF16)
        for k in range(1, 3):
            cols = slice(128 * k, 128 * k + 128)
            act_ref[here, cols] = (o[:, cols] * gate).astype(BF16)
        h1 = dot(z_ref[here, 768:1792], a1_ref[...])
        hid_ref[here, 384:896] = h1
        for k in range(4):
            act_ref[here, 384 + 128 * k : 512 + 128 * k] = (h1[:, 128 * k : 128 * k + 128] * gate).astype(BF16)
        h2 = dot(z_ref[here, 1792:2304], a2_ref[...])
        hid_ref[here, 896:1152] = h2
        for k in range(2):
            act_ref[here, 896 + 128 * k : 1024 + 128 * k] = (h2[:, 128 * k : 128 * k + 128] * gate).astype(BF16)
        mix_ref[here, 0:384] = dot(act_ref[here, 0:384], b0_ref[...])
        mix_ref[here, 384:896] = dot(act_ref[here, 384:896], b1_ref[...])
        mix_ref[here, 896:1152] = dot(act_ref[here, 896:1152], b2_ref[...])
        return carry

    lax.fori_loop(0, z_ref.shape[0] // 256, layer, 0)
    out_ref[...] = jnp.zeros(out_ref.shape, BF16)

    def unlift(p, carry):
        at = pl.multiple_of(p * 24, 8)
        t = own_ref[2 * p]
        out_ref[t] = out_ref[t] + turn_back(vt_ref, p, mix_ref, at)
        s = own_ref[2 * p + 1]
        out_ref[s] = out_ref[s] + turn_back(vs_ref, p, mix_ref, half + at)
        return carry

    lax.fori_loop(0, pairs, unlift, 0)


def forward(owners, got, turns, weights, rows):
    peers = got.shape[0]
    return pl.pallas_call(
        forward_body,
        in_specs=[SM] + [VM] * 11,
        out_specs=[VM] * 5,
        out_shape=[
            jax.ShapeDtypeStruct((peers, CH, 128), BF16),
            jax.ShapeDtypeStruct((rows, 2304), BF16),
            jax.ShapeDtypeStruct((rows, 1152), F32),
            jax.ShapeDtypeStruct((rows, 128), F32),
            jax.ShapeDtypeStruct((rows, 1152), BF16),
        ],
        scratch_shapes=[pltpu.VMEM((rows, 1152), F32)],
        compiler_params=pltpu.CompilerParams(vmem_limit_bytes=VMEM_LIMIT),
        cost_estimate=pl.CostEstimate(flops=10**10, transcendentals=10**6, bytes_accessed=3 * 10**7),
        name="forward",
    )(owners, got, *turns, *weights)


def backward_body(
    own_ref, r_ref, wt_ref, ws_ref, vt_ref, vs_ref, a0_ref, a1_ref, a2_ref, b0_ref, b1_ref, b2_ref,
    z_ref, hid_ref, gate_ref, act_ref, out_ref, wg_ref, dmix_ref, dd_ref, gs_ref, gt_ref, *, scale,
):
    half = z_ref.shape[0] // 2
    pairs = wt_ref.shape[0]

    def lift(d, carry):
        turned = []
        for p in (2 * d, 2 * d + 1):
            turned.append((turn(wt_ref, r_ref, p, own_ref[2 * p]), turn(ws_ref, r_ref, p, own_ref[2 * p + 1])))
        (t0, s0), (t1, s1) = turned
        at = pl.multiple_of(d * 48, 16)
        for k in range(9):
            lines = slice(24 * k, 24 * k + 24)
            cols = slice(128 * k, 128 * k + 128)
            dmix_ref[pl.ds(at, 48), cols] = jnp.concatenate([t0[lines], t1[lines]], axis=0).astype(BF16)
            dmix_ref[pl.ds(half + at, 48), cols] = jnp.concatenate([s0[lines], s1[lines]], axis=0).astype(BF16)
        return carry

    lax.fori_loop(0, pairs // 2, lift, 0)

    def layer(b, carry):
        at = pl.multiple_of(b * 128, 128)
        spots = (pl.ds(at, 128), pl.ds(half + at, 128))

        def rows_of(ref, cols):
            return jnp.concatenate([ref[spot, cols] for spot in spots], axis=0)

        def put(col, value):
            value = value.astype(BF16)
            for i, spot in enumerate(spots):
                dd_ref[spot, col : col + 128] = value[128 * i : 128 * i + 128]

        gate = rows_of(gate_ref, slice(0, 128))
        dact0 = dot_nt(rows_of(dmix_ref, slice(0, 384)), b0_ref[...])
        h0 = rows_of(hid_ref, slice(0, 128))
        head = jax.nn.sigmoid(h0)
        put(0, dact0[:, 0:128] * head * (1.0 + h0 * (1.0 - head)))
        total = None

        def gated(k, piece, col):
            put(col, piece * gate)
            return piece * rows_of(hid_ref, slice(128 * k, 128 * k + 128))

        total = gated(1, dact0[:, 128:256], 128) + gated(2, dact0[:, 256:384], 256)
        dact1 = dot_nt(rows_of(dmix_ref, slice(384, 896)), b1_ref[...])
        for k in range(4):
            total = total + gated(3 + k, dact1[:, 128 * k : 128 * k + 128], 512 + 128 * k)
        dact2 = dot_nt(rows_of(dmix_ref, slice(896, 1152)), b2_ref[...])
        for k in range(2):
            total = total + gated(7 + k, dact2[:, 128 * k : 128 * k + 128], 1024 + 128 * k)
        put(384, total * gate * (1.0 - gate))

        first = 0
        for cols, w_ref, count in ((slice(0, 512), a0_ref, 3), (slice(512, 1024), a1_ref, 4), (slice(1024, 1280), a2_ref, 2)):
            dz = dot_nt(rows_of(dd_ref, cols), w_ref[...])
            for k in range(count):
                lo = dz[:, 256 * k : 256 * k + 128]
                hi = dz[:, 256 * k + 128 : 256 * k + 256]
                to = slice(128 * (first + k), 128 * (first + k) + 128)
                gs_ref[spots[0], to] = lo[:128] + hi[128:]
                gt_ref[spots[0], to] = hi[:128] + lo[128:]
            first += count
        return carry

    lax.fori_loop(0, half // 128, layer, 0)
    out_ref[...] = jnp.zeros(out_ref.shape, BF16)

    def unlift(p, carry):
        at = pl.multiple_of(p * 24, 8)
        s = own_ref[2 * p + 1]
        out_ref[s] = out_ref[s] + turn_back(vs_ref, p, gs_ref, at)
        t = own_ref[2 * p]
        out_ref[t] = out_ref[t] + turn_back(vt_ref, p, gt_ref, at)
        return carry

    lax.fori_loop(0, pairs, unlift, 0)

    def put_rows(row, value):
        wg_ref[row : row + value.shape[0], :] = (value * scale).astype(BF16)

    wg_ref[8064:8192, :] = jnp.zeros((128, 128), BF16)

    def plain(left_ref, left_at, height, right_ref, right_cols, row):
        for c in range(height // 128):
            g = dot_tn(left_ref[:, left_at + 128 * c : left_at + 128 * c + 128], right_ref[:, right_cols])
            for n in range(g.shape[1] // 128):
                put_rows(row + n * height + 128 * c, g[:, 128 * n : 128 * n + 128])

    def folded(left_ref, left_at, height, right_ref, right_cols, row):
        width = (right_cols.stop - right_cols.start) // 2
        blocks = width // 128
        for c in range(height // 128):
            low = left_at + 128 * c
            top = dot_tn(left_ref[:, low : low + 128], right_ref[:, right_cols])
            bot = dot_tn(left_ref[:, low + height : low + height + 128], right_ref[:, right_cols])
            same = top[:, :width] + bot[:, width:]
            cross = top[:, width:] - bot[:, :width]
            for n in range(blocks):
                cols = slice(128 * n, 128 * n + 128)
                put_rows(row + n * height + 128 * c, same[:, cols])
                put_rows(row + (blocks + n) * height + 128 * c, cross[:, cols])

    plain(z_ref, 0, 768, dd_ref, slice(0, 512), 0)
    folded(z_ref, 768, 512, dd_ref, slice(512, 1024), 3072)
    folded(z_ref, 1792, 256, dd_ref, slice(1024, 1280), 5120)
    plain(act_ref, 0, 384, dmix_ref, slice(0, 384), 5632)
    folded(act_ref, 384, 256, dmix_ref, slice(384, 896), 6784)
    folded(act_ref, 896, 128, dmix_ref, slice(896, 1152), 7808)


def backward(owners, got, turns, weights, kept, scale):
    peers = got.shape[0]
    rows = kept[0].shape[0]

    def body(*refs):
        backward_body(*refs, scale=scale)

    return pl.pallas_call(
        body,
        in_specs=[SM] + [VM] * 15,
        out_specs=[VM, VM],
        out_shape=[
            jax.ShapeDtypeStruct((peers, CH, 128), BF16),
            jax.ShapeDtypeStruct((WEIGHT_ROWS, 128), BF16),
        ],
        scratch_shapes=[
            pltpu.VMEM((rows, 1152), BF16),
            pltpu.VMEM((rows, 1280), BF16),
            pltpu.VMEM((rows // 2, 1152), F32),
            pltpu.VMEM((rows // 2, 1152), F32),
        ],
        compiler_params=pltpu.CompilerParams(vmem_limit_bytes=VMEM_LIMIT),
        cost_estimate=pl.CostEstimate(flops=2 * 10**10, transcendentals=10**6, bytes_accessed=3 * 10**7),
        name="backward",
    )(owners, got, *turns, *weights, *kept)


def scatter_body(idx_ref, got_ref, out_ref, acc_ref, last_ref):
    @pl.when(pl.program_id(0) == 0)
    def _():
        acc_ref[...] = jnp.zeros(acc_ref.shape, F32)
        last_ref[...] = jnp.zeros(last_ref.shape, F32)

    atom = lax.broadcasted_iota(jnp.int32, (128, 256), 0)
    kinds = [
        jnp.where(jnp.broadcast_to(idx_ref[v : v + 1, :], (128, 256)) == atom, 1.0, 0.0).astype(BF16)
        for v in range(4)
    ]
    tiles = [got_ref[:, 16 * t : 16 * t + 16, :].reshape(256, 128) for t in range(7)]
    acc_ref[...] += dot(kinds[0], jnp.concatenate(tiles, axis=1))
    spare = jnp.concatenate([jnp.concatenate([tiles[j], tiles[j + 3]], axis=1) for j in range(3)], axis=0)
    last_ref[...] += dot(jnp.concatenate(kinds[1:], axis=1), spare)

    @pl.when(pl.program_id(0) == pl.num_programs(0) - 1)
    def _():
        for k in range(7):
            out_ref[k] = acc_ref[:, 128 * k : 128 * k + 128].astype(out_ref.dtype)
        for k in range(2):
            out_ref[7 + k] = last_ref[:, 128 * k : 128 * k + 128].astype(out_ref.dtype)


def add_rows(idx_rows, got, dtype):
    peers = got.shape[0]
    return pl.pallas_call(
        scatter_body,
        grid=(peers // 16,),
        in_specs=[
            pl.BlockSpec((8, 256), lambda c: (0, c)),
            pl.BlockSpec((16, CH, 128), lambda c: (c, 0, 0)),
        ],
        out_specs=whole((9, 128, 128)),
        out_shape=jax.ShapeDtypeStruct((9, 128, 128), dtype),
        scratch_shapes=[pltpu.VMEM((128, 896), F32), pltpu.VMEM((128, 256), F32)],
        cost_estimate=pl.CostEstimate(flops=10**9, transcendentals=0, bytes_accessed=6 * 10**6),
        name="add_rows",
    )(idx_rows, got)


def swapped(x):
    return lax.ppermute(x, "atoms", [(i, i ^ 1) for i in range(lax.axis_size("atoms"))])


def add_pair(core, grads, other):
    half = other.shape[0]

    def body(core_ref, grads_ref, other_ref, out_ref):
        mine = grads_ref[pl.ds(pl.multiple_of(core_ref[0] * half, 16), half), :]
        total = mine.astype(F32) + other_ref[...].astype(F32)
        out_ref[...] = total.astype(BF16).reshape(half // WR, WR, 128)

    return pl.pallas_call(
        body,
        in_specs=[SM, VM, VM],
        out_specs=VM,
        out_shape=jax.ShapeDtypeStruct((half // WR, WR, 128), BF16),
        cost_estimate=pl.CostEstimate(flops=10**6, transcendentals=0, bytes_accessed=4 * 10**6),
        name="add_pair",
    )(core, grads, other)


def add_peers(got):
    peers = got.shape[0]
    chips = peers // 2

    def body(got_ref, out_ref):
        x = got_ref[...].astype(F32).reshape(chips, 2, 16, 128)
        total = jnp.sum(x, axis=0).astype(BF16)
        out_ref[...] = jnp.broadcast_to(total[None], (chips, 2, 16, 128))

    return pl.pallas_call(
        body,
        grid=(WR // 16,),
        in_specs=[pl.BlockSpec((peers, 16, 128), lambda i: (0, CH // 16 + i, 0))],
        out_specs=pl.BlockSpec((chips, 2, 16, 128), lambda i: (0, 0, i, 0)),
        out_shape=jax.ShapeDtypeStruct((chips, 2, WR, 128), BF16),
        cost_estimate=pl.CostEstimate(flops=10**6, transcendentals=0, bytes_accessed=3 * 10**6),
        name="add_peers",
    )(got)


WEIGHT_PARTS = (
    (0, 1, 768, 4), (3072, 2, 512, 2), (5120, 2, 256, 1), (5632, 1, 384, 3), (6784, 2, 256, 2), (7808, 2, 128, 1),
)


def unpack(core, mine, other):
    chips = mine.shape[0]

    def body(core_ref, mine_ref, other_ref, *refs):
        outs, all_ref = refs[:-1], refs[-1]

        def place(chip, carry):
            for half in range(2):
                at = half * 2 * chips + 2 * chip
                all_ref[at + core_ref[0]] = mine_ref[chip, half]
                all_ref[at + 1 - core_ref[0]] = other_ref[chip, half]
            return carry

        lax.fori_loop(0, chips, place, 0, unroll=4)
        for out, (row, parts, height, blocks) in zip(outs, WEIGHT_PARTS):
            for p in range(parts):
                for n in range(blocks):
                    low = (row + (p * blocks + n) * height) // WR
                    value = all_ref[low : low + height // WR].reshape(height, 128)
                    out[p, :, 128 * n : 128 * n + 128] = value.astype(F32)

    return pl.pallas_call(
        body,
        in_specs=[SM, VM, VM],
        out_specs=[VM] * 6,
        out_shape=[jax.ShapeDtypeStruct((parts, height, 128 * blocks), F32) for _, parts, height, blocks in WEIGHT_PARTS],
        scratch_shapes=[pltpu.VMEM((4 * chips, WR, 128), BF16)],
        compiler_params=pltpu.CompilerParams(vmem_limit_bytes=VMEM_LIMIT // 2),
        cost_estimate=pl.CostEstimate(flops=10**6, transcendentals=0, bytes_accessed=6 * 10**6),
        name="unpack",
    )(core, mine, other)


def widen_pair(w):
    upper = jnp.concatenate([w[0], w[1]], axis=1)
    lower = jnp.concatenate([-w[1], w[0]], axis=1)
    return jnp.concatenate([upper, lower], axis=0)


def exchange(x):
    return lax.all_to_all(x, "atoms", split_axis=0, concat_axis=0, tiled=True)


def local(
    features, cotangent, wigner, pair_blocks, pair_rows, edge_ends,
    first_m0, first_m1, first_m2, second_m0, second_m1, second_m2,
):
    peers = lax.axis_size("atoms")
    pairs = pair_blocks.shape[0]
    edges = edge_ends.shape[1]
    each = edges // pairs
    owners = pair_blocks.reshape(2 * pairs)
    ends = jnp.arange(2 * pairs, dtype=jnp.int32)
    slots = jnp.sum(
        jnp.logical_and(owners[:, None] == owners[None, :], ends[:, None] > ends[None, :]), axis=1
    ).astype(jnp.int32)

    end_rows = jnp.transpose(pair_rows, (2, 0, 1)).reshape(2 * pairs, 6)
    cols = request_columns()
    row_cols = jnp.concatenate([end_rows[:, max(c, 0) % 6 : max(c, 0) % 6 + 1] for c in cols], axis=1)
    col_slot = jnp.asarray(np.where(cols < 0, -1, cols // 6), jnp.int32)
    peer = jnp.arange(peers, dtype=jnp.int32)
    hit = jnp.logical_and(
        owners[None, :, None] == peer[:, None, None], slots[None, :, None] == col_slot[None, None, :]
    )
    request = jnp.sum(jnp.where(hit, row_cols[None] + 1, 0), axis=1) - 1
    asked = exchange(request)
    asked_rows = jnp.transpose(asked.reshape(peers, 4, 16), (1, 0, 2)).reshape(4, peers * 16)
    asked_rows = jnp.concatenate([asked_rows, asked_rows], axis=0)
    eye = jnp.eye(64, dtype=BF16)

    got_f = exchange(pick_rows(asked, eye, jnp.transpose(features, (1, 0, 2))))

    turned = jnp.stack([wigner[i] for i in COEF_ORDER]).reshape(9, 9, pairs, each)
    pos = jnp.stack(
        [
            (slots.reshape(pairs, 2)[:, side, None] * 6 + edge_ends[side].reshape(pairs, each)).astype(F32)
            for side in range(2)
        ],
        axis=0,
    )
    pos = jnp.broadcast_to(pos[:, None], (2, 9, pairs, each))
    by_j = jnp.transpose(turned, (1, 0, 2, 3))
    gap5 = jnp.zeros((5, 9, pairs, each), F32)
    gap7 = jnp.zeros((7, 9, pairs, each), F32)
    table = jnp.concatenate([by_j, pos, gap5, by_j, gap7], axis=0)
    ra = jnp.transpose(table, (2, 1, 3, 0)).reshape(pairs, 9 * each, 32)
    ra = jnp.pad(ra, ((0, 0), (0, 224 - 9 * each), (0, 0)))
    rb = jnp.transpose(table, (2, 0, 1, 3)).reshape(pairs, 32, 9 * each)
    rb = jnp.pad(rb, ((0, 0), (0, 0), (0, 256 - 9 * each)))
    turns = build_turns(ra, rb)

    weights = (
        first_m0, widen_pair(first_m1), widen_pair(first_m2),
        second_m0, widen_pair(second_m1), widen_pair(second_m2),
    )
    picked_c = pick_rows(asked, eye, jnp.transpose(cotangent, (1, 0, 2)))
    picked_c, turns, weights = lax.optimization_barrier((picked_c, turns, weights))
    got_c = exchange(picked_c)
    back_m, *kept = forward(owners, got_f, turns, weights, 2 * edges)
    got_m = exchange(back_m)
    scale = float((2.0 * edges * peers) ** (-0.5))
    back_g, grads = backward(owners, got_c, turns, weights, kept, scale)
    core = (lax.axis_index("atoms") % 2).astype(jnp.int32)
    cores = jnp.stack([core, core])
    half = WEIGHT_ROWS // 2
    sent = lax.dynamic_slice_in_dim(grads, (1 - core) * half, half, axis=0)
    w_rows = add_pair(cores, grads, swapped(sent))
    both = jnp.concatenate([back_g, w_rows], axis=1)
    both, got_m = lax.optimization_barrier((both, got_m))
    messages = add_rows(asked_rows, got_m, BF16)
    got_g, messages = lax.optimization_barrier((exchange(both), messages))
    same_core = [list(range(c, peers, 2)) for c in range(2)]
    w_mine = lax.all_to_all(
        add_peers(got_g).reshape(peers // 2, 2 * WR, 128), "atoms",
        split_axis=0, concat_axis=0, tiled=True, axis_index_groups=same_core,
    ).reshape(peers // 2, 2, WR, 128)
    grad_features = add_rows(asked_rows, got_g, F32)
    w_mine, grad_features = lax.optimization_barrier((w_mine, grad_features))
    messages = jnp.transpose(messages, (1, 0, 2))
    grad_features = jnp.transpose(grad_features, (1, 0, 2))
    w = unpack(cores, w_mine, swapped(w_mine))
    return (messages, grad_features, w[0][0], w[1], w[2], w[3][0], w[4], w[5])


def solution(mesh):
    rows = P("atoms", None, None)
    in_specs = (
        rows, rows, P(None, None, "atoms"), P("atoms", None), P(None, None, "atoms"), P(None, "atoms"),
        P(), P(), P(), P(), P(), P(),
    )
    out_specs = (rows, rows, P(), P(), P(), P(), P(), P())
    return jax.shard_map(local, mesh=mesh, in_specs=in_specs, out_specs=out_specs, check_vma=False)
```

```python
import jax
import jax.numpy as jnp
import numpy as np
from jax import lax
from jax.experimental import pallas as pl
from jax.experimental.pallas import tpu as pltpu
from jax.sharding import PartitionSpec as P

COEF_ORDER = (0, 2, 6, 3, 7, 1, 5, 8, 4)
F32 = jnp.float32
BF16 = jnp.bfloat16
CH = 112
GROUPS = 27
WEIGHT_ROWS = 8192
WR = 32
PICK = 64
VMEM_LIMIT = 58 * 1024 * 1024


def chunk_maps():
    coef = np.full((CH,), -1)
    row = np.full((CH,), -1)
    for line in range(CH):
        tile, at = divmod(line, 16)
        if at < 12:
            coef[line], row[line] = tile, at
        elif tile < 6:
            coef[line], row[line] = 7 + tile // 3, 4 * (tile % 3) + at - 12
    return coef, row


def spread_tables():
    coef, row = chunk_maps()
    spread = np.zeros((32, 256), np.float32)
    rows = np.full((256,), -1.0, np.float32)
    for half in range(2):
        for line in range(CH):
            if coef[line] >= 0:
                spread[16 * half + coef[line], CH * half + line] = 1.0
                rows[CH * half + line] = row[line]
    return spread, rows


def request_columns():
    cols = np.full((64,), -1)
    cols[:12] = np.arange(12)
    for j in range(3):
        cols[16 * (j + 1) + 12 : 16 * (j + 2)] = 4 * j + np.arange(4)
    return cols


def dot(a, b):
    return jnp.dot(a, b, preferred_element_type=F32)


def dot_nt(a, b):
    return lax.dot_general(a, b, (((1,), (1,)), ((), ())), preferred_element_type=F32)


def dot_tn(a, b):
    return lax.dot_general(a, b, (((0,), (0,)), ((), ())), preferred_element_type=F32)


def whole(shape):
    return pl.BlockSpec(shape, lambda *_: (0,) * len(shape))


VM = pl.BlockSpec(memory_space=pltpu.VMEM)
SM = pl.BlockSpec(memory_space=pltpu.SMEM)


def gather_body(idx_ref, eye_ref, feat_ref, out_ref):
    turned = dot_nt(eye_ref[...], idx_ref[...].astype(F32).astype(BF16))
    lane = lax.broadcasted_iota(jnp.int32, (64, 128), 1).astype(F32)
    picks = []
    for q in range(PICK):
        col = jnp.broadcast_to(turned[:, q : q + 1], (64, 128))
        picks.append(jnp.where(col == lane, 1.0, 0.0).astype(BF16))
    kinds = [jnp.concatenate([x[16 * v : 16 * v + 16] for x in picks], axis=0) for v in range(4)]
    for j in range(3):
        left = jnp.concatenate([kinds[0], kinds[j + 1]], axis=1)
        right = jnp.concatenate(
            [
                jnp.concatenate([feat_ref[j], feat_ref[j + 3]], axis=1),
                jnp.concatenate([feat_ref[7], feat_ref[8]], axis=1),
            ],
            axis=0,
        )
        got = dot(left, right).astype(BF16)
        out_ref[:, 4 * j : 4 * j + 4] = got[:, :128].reshape(PICK, 4, 4, 128)
        out_ref[:, 4 * (j + 3) : 4 * (j + 4)] = got[:, 128:].reshape(PICK, 4, 4, 128)
    last = dot(kinds[0], feat_ref[6]).astype(BF16)
    out_ref[:, 24:27] = last.reshape(PICK, 4, 4, 128)[:, :3]


def pick_rows(idx, eye, feat):
    peers = idx.shape[0]
    return pl.pallas_call(
        gather_body,
        grid=(peers // PICK,),
        in_specs=[
            pl.BlockSpec((PICK, 64), lambda c: (c, 0)),
            whole((64, 64)),
            whole((9, 128, 128)),
        ],
        out_specs=pl.BlockSpec((PICK, GROUPS, 4, 128), lambda c: (c, 0, 0, 0)),
        out_shape=jax.ShapeDtypeStruct((peers, GROUPS, 4, 128), BF16),
        compiler_params=pltpu.CompilerParams(vmem_limit_bytes=VMEM_LIMIT // 2),
        cost_estimate=pl.CostEstimate(flops=2 * 10**9, transcendentals=0, bytes_accessed=4 * 10**6),
        name="pick_rows",
    )(idx, eye, feat)


def prep_body(ra_ref, rb_ref, sp_ref, spt_ref, rows_ref, rowst_ref, wt_ref, ws_ref, vt_ref, vs_ref):
    a = ra_ref[0]
    a_hi = a.astype(BF16)
    a_lo = (a - a_hi.astype(F32)).astype(BF16)
    lane = lax.broadcasted_iota(jnp.int32, (224, 32), 1)
    a_both = jnp.where(lane < 16, a_hi.astype(F32), a_lo.astype(F32)).astype(BF16)
    x = dot(a_both, sp_ref[...])
    rows = jnp.broadcast_to(rows_ref[0:1, :], (224, 256))
    for at, out in ((9, wt_ref), (10, ws_ref)):
        mine = jnp.broadcast_to(a[:, at : at + 1], (224, 256))
        out[0] = jnp.where(mine == rows, x, 0.0).astype(BF16)
    b = rb_ref[0]
    b_hi = b.astype(BF16)
    b_lo = (b - b_hi.astype(F32)).astype(BF16)
    line = lax.broadcasted_iota(jnp.int32, (32, 256), 0)
    b_both = jnp.where(line < 16, b_hi.astype(F32), b_lo.astype(F32)).astype(BF16)
    y = dot(spt_ref[...], b_both)
    rowst = jnp.broadcast_to(rowst_ref[:, 0:1], (224, 256))
    for at, out in ((9, vt_ref), (10, vs_ref)):
        mine = jnp.broadcast_to(b[at : at + 1, :], (224, 256))
        out[0] = jnp.where(mine == rowst, y, 0.0).astype(BF16)


def build_turns(ra, rb):
    pairs = ra.shape[0]
    spread, rows = spread_tables()
    sp = jnp.asarray(spread, BF16)
    spt = jnp.asarray(spread[:, :224].T, BF16)
    rows8 = jnp.asarray(np.tile(rows[None], (8, 1)), F32)
    rowst = jnp.asarray(np.tile(rows[:224, None], (1, 128)), F32)
    one = jax.ShapeDtypeStruct((pairs, 224, 256), BF16)
    block = pl.BlockSpec((1, 224, 256), lambda p: (p, 0, 0))
    return pl.pallas_call(
        prep_body,
        grid=(pairs,),
        in_specs=[
            pl.BlockSpec((1, 224, 32), lambda p: (p, 0, 0)),
            pl.BlockSpec((1, 32, 256), lambda p: (p, 0, 0)),
            whole((32, 256)),
            whole((224, 32)),
            whole((8, 256)),
            whole((224, 128)),
        ],
        out_specs=[block] * 4,
        out_shape=[one] * 4,
        cost_estimate=pl.CostEstimate(flops=10**9, transcendentals=0, bytes_accessed=10**7),
        name="build_turns",
    )(ra, rb, sp, spt, rows8, rowst)


def turn(w_ref, r_ref, pair, owner):
    groups = r_ref[owner]
    last = jnp.concatenate([groups[24:27], jnp.zeros((1, 4, 128), BF16)], axis=0).reshape(16, 128)
    chunk = jnp.concatenate([groups[:24].reshape(96, 128), last], axis=0)
    right = jnp.concatenate([chunk, chunk, jnp.zeros((32, 128), BF16)], axis=0)
    return dot(w_ref[pair], right)


def turn_back(v_ref, pair, src_ref, base):
    parts = [src_ref[pl.ds(base, 24), 128 * k : 128 * k + 128] for k in range(9)]
    x = jnp.concatenate(parts + [jnp.zeros((40, 128), F32)], axis=0)
    hi = x.astype(BF16)
    lo = (x - hi.astype(F32)).astype(BF16)
    y = dot(v_ref[pair], jnp.concatenate([hi, lo], axis=1))
    y = y[:, :128] + y[:, 128:]
    y = (y[:CH] + y[CH:]).astype(BF16)
    return y.reshape(GROUPS + 1, 4, 128)[:GROUPS]


def forward_body(
    own_ref, r_ref, wt_ref, ws_ref, vt_ref, vs_ref, a0_ref, a1_ref, a2_ref, b0_ref, b1_ref, b2_ref,
    out_ref, z_ref, hid_ref, gate_ref, act_ref, mix_ref,
):
    half = z_ref.shape[0] // 2
    pairs = wt_ref.shape[0]

    def lift(d, carry):
        turned = []
        for p in (2 * d, 2 * d + 1):
            turned.append((turn(ws_ref, r_ref, p, own_ref[2 * p + 1]), turn(wt_ref, r_ref, p, own_ref[2 * p])))
        (s0, t0), (s1, t1) = turned
        at = pl.multiple_of(d * 48, 16)
        for k in range(9):
            lines = slice(24 * k, 24 * k + 24)
            s = jnp.concatenate([s0[lines], s1[lines]], axis=0).astype(BF16)
            t = jnp.concatenate([t0[lines], t1[lines]], axis=0).astype(BF16)
            z_ref[pl.ds(at, 48), 256 * k : 256 * k + 128] = s
            z_ref[pl.ds(at, 48), 256 * k + 128 : 256 * k + 256] = t
            z_ref[pl.ds(half + at, 48), 256 * k : 256 * k + 128] = t
            z_ref[pl.ds(half + at, 48), 256 * k + 128 : 256 * k + 256] = s
        return carry

    lax.fori_loop(0, pairs // 2, lift, 0)

    def layer(b, carry):
        at = pl.multiple_of(b * 256, 256)
        here = pl.ds(at, 256)
        o = dot(z_ref[here, 0:768], a0_ref[...])
        gate = jax.nn.sigmoid(o[:, 384:512])
        gate_ref[here, :] = gate
        h0 = o[:, 0:128]
        hid_ref[here, 0:384] = o[:, 0:384]
        act_ref[here, 0:128] = (h0 * jax.nn.sigmoid(h0)).astype(BF16)
        for k in range(1, 3):
            cols = slice(128 * k, 128 * k + 128)
            act_ref[here, cols] = (o[:, cols] * gate).astype(BF16)
        h1 = dot(z_ref[here, 768:1792], a1_ref[...])
        hid_ref[here, 384:896] = h1
        for k in range(4):
            act_ref[here, 384 + 128 * k : 512 + 128 * k] = (h1[:, 128 * k : 128 * k + 128] * gate).astype(BF16)
        h2 = dot(z_ref[here, 1792:2304], a2_ref[...])
        hid_ref[here, 896:1152] = h2
        for k in range(2):
            act_ref[here, 896 + 128 * k : 1024 + 128 * k] = (h2[:, 128 * k : 128 * k + 128] * gate).astype(BF16)
        mix_ref[here, 0:384] = dot(act_ref[here, 0:384], b0_ref[...])
        mix_ref[here, 384:896] = dot(act_ref[here, 384:896], b1_ref[...])
        mix_ref[here, 896:1152] = dot(act_ref[here, 896:1152], b2_ref[...])
        return carry

    lax.fori_loop(0, z_ref.shape[0] // 256, layer, 0)
    out_ref[...] = jnp.zeros(out_ref.shape, BF16)

    def unlift(p, carry):
        at = pl.multiple_of(p * 24, 8)
        t = own_ref[2 * p]
        out_ref[t] = out_ref[t] + turn_back(vt_ref, p, mix_ref, at)
        s = own_ref[2 * p + 1]
        out_ref[s] = out_ref[s] + turn_back(vs_ref, p, mix_ref, half + at)
        return carry

    lax.fori_loop(0, pairs, unlift, 0)


def forward(owners, got, turns, weights, rows):
    peers = got.shape[0]
    return pl.pallas_call(
        forward_body,
        in_specs=[SM] + [VM] * 11,
        out_specs=[VM] * 5,
        out_shape=[
            jax.ShapeDtypeStruct((peers, GROUPS, 4, 128), BF16),
            jax.ShapeDtypeStruct((rows, 2304), BF16),
            jax.ShapeDtypeStruct((rows, 1152), F32),
            jax.ShapeDtypeStruct((rows, 128), F32),
            jax.ShapeDtypeStruct((rows, 1152), BF16),
        ],
        scratch_shapes=[pltpu.VMEM((rows, 1152), F32)],
        compiler_params=pltpu.CompilerParams(vmem_limit_bytes=VMEM_LIMIT),
        cost_estimate=pl.CostEstimate(flops=10**10, transcendentals=10**6, bytes_accessed=3 * 10**7),
        name="forward",
    )(owners, got, *turns, *weights)


def backward_body(
    own_ref, r_ref, wt_ref, ws_ref, vt_ref, vs_ref, a0_ref, a1_ref, a2_ref, b0_ref, b1_ref, b2_ref,
    z_ref, hid_ref, gate_ref, act_ref, out_ref, wg_ref, dmix_ref, dd_ref, gs_ref, gt_ref, *, scale,
):
    half = z_ref.shape[0] // 2
    pairs = wt_ref.shape[0]

    def lift(d, carry):
        turned = []
        for p in (2 * d, 2 * d + 1):
            turned.append((turn(wt_ref, r_ref, p, own_ref[2 * p]), turn(ws_ref, r_ref, p, own_ref[2 * p + 1])))
        (t0, s0), (t1, s1) = turned
        at = pl.multiple_of(d * 48, 16)
        for k in range(9):
            lines = slice(24 * k, 24 * k + 24)
            cols = slice(128 * k, 128 * k + 128)
            dmix_ref[pl.ds(at, 48), cols] = jnp.concatenate([t0[lines], t1[lines]], axis=0).astype(BF16)
            dmix_ref[pl.ds(half + at, 48), cols] = jnp.concatenate([s0[lines], s1[lines]], axis=0).astype(BF16)
        return carry

    lax.fori_loop(0, pairs // 2, lift, 0)

    def layer(b, carry):
        at = pl.multiple_of(b * 128, 128)
        spots = (pl.ds(at, 128), pl.ds(half + at, 128))

        def rows_of(ref, cols):
            return jnp.concatenate([ref[spot, cols] for spot in spots], axis=0)

        def put(col, value):
            value = value.astype(BF16)
            for i, spot in enumerate(spots):
                dd_ref[spot, col : col + 128] = value[128 * i : 128 * i + 128]

        gate = rows_of(gate_ref, slice(0, 128))
        dact0 = dot_nt(rows_of(dmix_ref, slice(0, 384)), b0_ref[...])
        h0 = rows_of(hid_ref, slice(0, 128))
        head = jax.nn.sigmoid(h0)
        put(0, dact0[:, 0:128] * head * (1.0 + h0 * (1.0 - head)))
        total = None

        def gated(k, piece, col):
            put(col, piece * gate)
            return piece * rows_of(hid_ref, slice(128 * k, 128 * k + 128))

        total = gated(1, dact0[:, 128:256], 128) + gated(2, dact0[:, 256:384], 256)
        dact1 = dot_nt(rows_of(dmix_ref, slice(384, 896)), b1_ref[...])
        for k in range(4):
            total = total + gated(3 + k, dact1[:, 128 * k : 128 * k + 128], 512 + 128 * k)
        dact2 = dot_nt(rows_of(dmix_ref, slice(896, 1152)), b2_ref[...])
        for k in range(2):
            total = total + gated(7 + k, dact2[:, 128 * k : 128 * k + 128], 1024 + 128 * k)
        put(384, total * gate * (1.0 - gate))

        first = 0
        for cols, w_ref, count in ((slice(0, 512), a0_ref, 3), (slice(512, 1024), a1_ref, 4), (slice(1024, 1280), a2_ref, 2)):
            dz = dot_nt(rows_of(dd_ref, cols), w_ref[...])
            for k in range(count):
                lo = dz[:, 256 * k : 256 * k + 128]
                hi = dz[:, 256 * k + 128 : 256 * k + 256]
                to = slice(128 * (first + k), 128 * (first + k) + 128)
                gs_ref[spots[0], to] = lo[:128] + hi[128:]
                gt_ref[spots[0], to] = hi[:128] + lo[128:]
            first += count
        return carry

    lax.fori_loop(0, half // 128, layer, 0)
    out_ref[...] = jnp.zeros(out_ref.shape, BF16)

    def unlift(p, carry):
        at = pl.multiple_of(p * 24, 8)
        s = own_ref[2 * p + 1]
        out_ref[s] = out_ref[s] + turn_back(vs_ref, p, gs_ref, at)
        t = own_ref[2 * p]
        out_ref[t] = out_ref[t] + turn_back(vt_ref, p, gt_ref, at)
        return carry

    lax.fori_loop(0, pairs, unlift, 0)

    def put_rows(row, value):
        wg_ref[row : row + value.shape[0], :] = (value * scale).astype(BF16)

    wg_ref[8064:8192, :] = jnp.zeros((128, 128), BF16)

    def plain(left_ref, left_at, height, right_ref, right_cols, row):
        for c in range(height // 128):
            g = dot_tn(left_ref[:, left_at + 128 * c : left_at + 128 * c + 128], right_ref[:, right_cols])
            for n in range(g.shape[1] // 128):
                put_rows(row + n * height + 128 * c, g[:, 128 * n : 128 * n + 128])

    def folded(left_ref, left_at, height, right_ref, right_cols, row):
        width = (right_cols.stop - right_cols.start) // 2
        blocks = width // 128
        for c in range(height // 128):
            low = left_at + 128 * c
            top = dot_tn(left_ref[:, low : low + 128], right_ref[:, right_cols])
            bot = dot_tn(left_ref[:, low + height : low + height + 128], right_ref[:, right_cols])
            same = top[:, :width] + bot[:, width:]
            cross = top[:, width:] - bot[:, :width]
            for n in range(blocks):
                cols = slice(128 * n, 128 * n + 128)
                put_rows(row + n * height + 128 * c, same[:, cols])
                put_rows(row + (blocks + n) * height + 128 * c, cross[:, cols])

    plain(z_ref, 0, 768, dd_ref, slice(0, 512), 0)
    folded(z_ref, 768, 512, dd_ref, slice(512, 1024), 3072)
    folded(z_ref, 1792, 256, dd_ref, slice(1024, 1280), 5120)
    plain(act_ref, 0, 384, dmix_ref, slice(0, 384), 5632)
    folded(act_ref, 384, 256, dmix_ref, slice(384, 896), 6784)
    folded(act_ref, 896, 128, dmix_ref, slice(896, 1152), 7808)


def backward(owners, got, turns, weights, kept, scale):
    peers = got.shape[0]
    rows = kept[0].shape[0]

    def body(*refs):
        backward_body(*refs, scale=scale)

    return pl.pallas_call(
        body,
        in_specs=[SM] + [VM] * 15,
        out_specs=[VM, VM],
        out_shape=[
            jax.ShapeDtypeStruct((peers, GROUPS, 4, 128), BF16),
            jax.ShapeDtypeStruct((WEIGHT_ROWS, 128), BF16),
        ],
        scratch_shapes=[
            pltpu.VMEM((rows, 1152), BF16),
            pltpu.VMEM((rows, 1280), BF16),
            pltpu.VMEM((rows // 2, 1152), F32),
            pltpu.VMEM((rows // 2, 1152), F32),
        ],
        compiler_params=pltpu.CompilerParams(vmem_limit_bytes=VMEM_LIMIT),
        cost_estimate=pl.CostEstimate(flops=2 * 10**10, transcendentals=10**6, bytes_accessed=3 * 10**7),
        name="backward",
    )(owners, got, *turns, *weights, *kept)


def scatter_body(idx_ref, got_ref, out_ref, acc_ref, last_ref, *, first):
    @pl.when(pl.program_id(0) == 0)
    def _():
        acc_ref[...] = jnp.zeros(acc_ref.shape, F32)
        last_ref[...] = jnp.zeros(last_ref.shape, F32)

    atom = lax.broadcasted_iota(jnp.int32, (128, 256), 0)
    kinds = [
        jnp.where(jnp.broadcast_to(idx_ref[v : v + 1, :], (128, 256)) == atom, 1.0, 0.0).astype(BF16)
        for v in range(4)
    ]
    tiles = [got_ref[:, first + 4 * t : first + 4 * t + 4].reshape(256, 128) for t in range(6)]
    last = got_ref[:, first + 24 : first + 27]
    tiles.append(jnp.concatenate([last, jnp.zeros((16, 1, 4, 128), BF16)], axis=1).reshape(256, 128))
    acc_ref[...] += dot(kinds[0], jnp.concatenate(tiles, axis=1))
    spare = jnp.concatenate([jnp.concatenate([tiles[j], tiles[j + 3]], axis=1) for j in range(3)], axis=0)
    last_ref[...] += dot(jnp.concatenate(kinds[1:], axis=1), spare)

    @pl.when(pl.program_id(0) == pl.num_programs(0) - 1)
    def _():
        for k in range(7):
            out_ref[k] = acc_ref[:, 128 * k : 128 * k + 128].astype(out_ref.dtype)
        for k in range(2):
            out_ref[7 + k] = last_ref[:, 128 * k : 128 * k + 128].astype(out_ref.dtype)


def add_rows(idx_rows, got, dtype):
    peers, groups = got.shape[:2]

    def body(*refs):
        scatter_body(*refs, first=groups - GROUPS)

    return pl.pallas_call(
        body,
        grid=(peers // 16,),
        in_specs=[
            pl.BlockSpec((8, 256), lambda c: (0, c)),
            pl.BlockSpec((16, groups, 4, 128), lambda c: (c, 0, 0, 0)),
        ],
        out_specs=whole((9, 128, 128)),
        out_shape=jax.ShapeDtypeStruct((9, 128, 128), dtype),
        scratch_shapes=[pltpu.VMEM((128, 896), F32), pltpu.VMEM((128, 256), F32)],
        cost_estimate=pl.CostEstimate(flops=10**9, transcendentals=0, bytes_accessed=6 * 10**6),
        name="add_rows",
    )(idx_rows, got)


def swapped(x):
    return lax.ppermute(x, "atoms", [(i, i ^ 1) for i in range(lax.axis_size("atoms"))])


def add_pair(core, grads, other):
    half = other.shape[0]

    def body(core_ref, grads_ref, other_ref, out_ref):
        mine = grads_ref[pl.ds(pl.multiple_of(core_ref[0] * half, 16), half), :]
        total = mine.astype(F32) + other_ref[...].astype(F32)
        out_ref[...] = total.astype(BF16).reshape(half // WR, WR // 4, 4, 128)

    return pl.pallas_call(
        body,
        in_specs=[SM, VM, VM],
        out_specs=VM,
        out_shape=jax.ShapeDtypeStruct((half // WR, WR // 4, 4, 128), BF16),
        cost_estimate=pl.CostEstimate(flops=10**6, transcendentals=0, bytes_accessed=4 * 10**6),
        name="add_pair",
    )(core, grads, other)


def add_peers(got):
    peers = got.shape[0]
    chips = peers // 2

    def body(got_ref, out_ref):
        x = got_ref[...].reshape(peers, WR, 128).astype(F32).reshape(chips, 2, WR, 128)
        total = jnp.sum(x, axis=0).astype(BF16)
        out_ref[...] = jnp.broadcast_to(total[None], (chips, 2, WR, 128))

    return pl.pallas_call(
        body,
        grid=(1,),
        in_specs=[pl.BlockSpec((peers, WR // 4, 4, 128), lambda i: (0, 0, 0, 0))],
        out_specs=whole((chips, 2, WR, 128)),
        out_shape=jax.ShapeDtypeStruct((chips, 2, WR, 128), BF16),
        compiler_params=pltpu.CompilerParams(vmem_limit_bytes=VMEM_LIMIT // 2),
        cost_estimate=pl.CostEstimate(flops=10**6, transcendentals=0, bytes_accessed=3 * 10**6),
        name="add_peers",
    )(got)


WEIGHT_PARTS = (
    (0, 1, 768, 4), (3072, 2, 512, 2), (5120, 2, 256, 1), (5632, 1, 384, 3), (6784, 2, 256, 2), (7808, 2, 128, 1),
)


def unpack(core, mine, other):
    chips = mine.shape[0]

    def body(core_ref, mine_ref, other_ref, *refs):
        outs, all_ref = refs[:-1], refs[-1]

        def place(chip, carry):
            for half in range(2):
                at = half * 2 * chips + 2 * chip
                all_ref[at + core_ref[0]] = mine_ref[chip, half]
                all_ref[at + 1 - core_ref[0]] = other_ref[chip, half]
            return carry

        lax.fori_loop(0, chips, place, 0, unroll=4)
        for out, (row, parts, height, blocks) in zip(outs, WEIGHT_PARTS):
            for p in range(parts):
                for n in range(blocks):
                    low = (row + (p * blocks + n) * height) // WR
                    value = all_ref[low : low + height // WR].reshape(height, 128)
                    out[p, :, 128 * n : 128 * n + 128] = value.astype(F32)

    return pl.pallas_call(
        body,
        in_specs=[SM, VM, VM],
        out_specs=[VM] * 6,
        out_shape=[jax.ShapeDtypeStruct((parts, height, 128 * blocks), F32) for _, parts, height, blocks in WEIGHT_PARTS],
        scratch_shapes=[pltpu.VMEM((4 * chips, WR, 128), BF16)],
        compiler_params=pltpu.CompilerParams(vmem_limit_bytes=VMEM_LIMIT // 2),
        cost_estimate=pl.CostEstimate(flops=10**6, transcendentals=0, bytes_accessed=6 * 10**6),
        name="unpack",
    )(core, mine, other)


def widen_pair(w):
    upper = jnp.concatenate([w[0], w[1]], axis=1)
    lower = jnp.concatenate([-w[1], w[0]], axis=1)
    return jnp.concatenate([upper, lower], axis=0)


def exchange(x):
    return lax.all_to_all(x, "atoms", split_axis=0, concat_axis=0, tiled=True)


def local(
    features, cotangent, wigner, pair_blocks, pair_rows, edge_ends,
    first_m0, first_m1, first_m2, second_m0, second_m1, second_m2,
):
    peers = lax.axis_size("atoms")
    pairs = pair_blocks.shape[0]
    edges = edge_ends.shape[1]
    each = edges // pairs
    owners = pair_blocks.reshape(2 * pairs)
    ends = jnp.arange(2 * pairs, dtype=jnp.int32)
    slots = jnp.sum(
        jnp.logical_and(owners[:, None] == owners[None, :], ends[:, None] > ends[None, :]), axis=1
    ).astype(jnp.int32)

    end_rows = jnp.transpose(pair_rows, (2, 0, 1)).reshape(2 * pairs, 6)
    cols = request_columns()
    row_cols = jnp.concatenate([end_rows[:, max(c, 0) % 6 : max(c, 0) % 6 + 1] for c in cols], axis=1)
    col_slot = jnp.asarray(np.where(cols < 0, -1, cols // 6), jnp.int32)
    peer = jnp.arange(peers, dtype=jnp.int32)
    hit = jnp.logical_and(
        owners[None, :, None] == peer[:, None, None], slots[None, :, None] == col_slot[None, None, :]
    )
    request = jnp.sum(jnp.where(hit, row_cols[None] + 1, 0), axis=1) - 1
    asked = exchange(request)
    asked_rows = jnp.transpose(asked.reshape(peers, 4, 16), (1, 0, 2)).reshape(4, peers * 16)
    asked_rows = jnp.concatenate([asked_rows, asked_rows], axis=0)
    eye = jnp.eye(64, dtype=BF16)

    got_f = exchange(pick_rows(asked, eye, jnp.transpose(features, (1, 0, 2))))

    turned = jnp.stack([wigner[i] for i in COEF_ORDER]).reshape(9, 9, pairs, each)
    pos = jnp.stack(
        [
            (slots.reshape(pairs, 2)[:, side, None] * 6 + edge_ends[side].reshape(pairs, each)).astype(F32)
            for side in range(2)
        ],
        axis=0,
    )
    pos = jnp.broadcast_to(pos[:, None], (2, 9, pairs, each))
    by_j = jnp.transpose(turned, (1, 0, 2, 3))
    gap5 = jnp.zeros((5, 9, pairs, each), F32)
    gap7 = jnp.zeros((7, 9, pairs, each), F32)
    table = jnp.concatenate([by_j, pos, gap5, by_j, gap7], axis=0)
    ra = jnp.transpose(table, (2, 1, 3, 0)).reshape(pairs, 9 * each, 32)
    ra = jnp.pad(ra, ((0, 0), (0, 224 - 9 * each), (0, 0)))
    rb = jnp.transpose(table, (2, 0, 1, 3)).reshape(pairs, 32, 9 * each)
    rb = jnp.pad(rb, ((0, 0), (0, 0), (0, 256 - 9 * each)))
    turns = build_turns(ra, rb)

    weights = (
        first_m0, widen_pair(first_m1), widen_pair(first_m2),
        second_m0, widen_pair(second_m1), widen_pair(second_m2),
    )
    picked_c = pick_rows(asked, eye, jnp.transpose(cotangent, (1, 0, 2)))
    picked_c, turns, weights = lax.optimization_barrier((picked_c, turns, weights))
    got_c = exchange(picked_c)
    back_m, *kept = forward(owners, got_f, turns, weights, 2 * edges)
    got_m = exchange(back_m)
    scale = float((2.0 * edges * peers) ** (-0.5))
    back_g, grads = backward(owners, got_c, turns, weights, kept, scale)
    core = (lax.axis_index("atoms") % 2).astype(jnp.int32)
    cores = jnp.stack([core, core])
    half = WEIGHT_ROWS // 2
    sent = lax.dynamic_slice_in_dim(grads, (1 - core) * half, half, axis=0)
    w_rows = add_pair(cores, grads, swapped(sent))
    both = jnp.concatenate([w_rows, back_g], axis=1)
    both, got_m = lax.optimization_barrier((both, got_m))
    messages = add_rows(asked_rows, got_m, BF16)
    got_g, messages = lax.optimization_barrier((exchange(both), messages))
    same_core = [list(range(c, peers, 2)) for c in range(2)]
    w_mine = lax.all_to_all(
        add_peers(got_g).reshape(peers // 2, 2 * WR, 128), "atoms",
        split_axis=0, concat_axis=0, tiled=True, axis_index_groups=same_core,
    ).reshape(peers // 2, 2, WR, 128)
    grad_features = add_rows(asked_rows, got_g, F32)
    w_mine, grad_features = lax.optimization_barrier((w_mine, grad_features))
    messages = jnp.transpose(messages, (1, 0, 2))
    grad_features = jnp.transpose(grad_features, (1, 0, 2))
    w = unpack(cores, w_mine, swapped(w_mine))
    return (messages, grad_features, w[0][0], w[1], w[2], w[3][0], w[4], w[5])


def solution(mesh):
    rows = P("atoms", None, None)
    in_specs = (
        rows, rows, P(None, None, "atoms"), P("atoms", None), P(None, None, "atoms"), P(None, "atoms"),
        P(), P(), P(), P(), P(), P(),
    )
    out_specs = (rows, rows, P(), P(), P(), P(), P(), P())
    return jax.shard_map(local, mesh=mesh, in_specs=in_specs, out_specs=out_specs, check_vma=False)
```

```python
import jax
import jax.numpy as jnp
import numpy as np
from jax import lax
from jax.experimental import pallas as pl
from jax.experimental.pallas import tpu as pltpu
from jax.sharding import PartitionSpec as P

COEF_ORDER = (0, 2, 6, 3, 7, 1, 5, 8, 4)
F32 = jnp.float32
BF16 = jnp.bfloat16
CH = 112
GROUPS = 27
WEIGHT_ROWS = 8192
WR = 32
PICK = 64
VMEM_LIMIT = 58 * 1024 * 1024


def chunk_maps():
    coef = np.full((CH,), -1)
    row = np.full((CH,), -1)
    for line in range(CH):
        tile, at = divmod(line, 16)
        if at < 12:
            coef[line], row[line] = tile, at
        elif tile < 6:
            coef[line], row[line] = 7 + tile // 3, 4 * (tile % 3) + at - 12
    return coef, row


def spread_tables():
    coef, row = chunk_maps()
    spread = np.zeros((32, 256), np.float32)
    rows = np.full((256,), -1.0, np.float32)
    for half in range(2):
        for line in range(CH):
            if coef[line] >= 0:
                spread[16 * half + coef[line], CH * half + line] = 1.0
                rows[CH * half + line] = row[line]
    return spread, rows


def request_columns():
    cols = np.full((64,), -1)
    cols[:12] = np.arange(12)
    for j in range(3):
        cols[16 * (j + 1) + 12 : 16 * (j + 2)] = 4 * j + np.arange(4)
    return cols


def dot(a, b):
    return jnp.dot(a, b, preferred_element_type=F32)


def dot_nt(a, b):
    return lax.dot_general(a, b, (((1,), (1,)), ((), ())), preferred_element_type=F32)


def dot_tn(a, b):
    return lax.dot_general(a, b, (((0,), (0,)), ((), ())), preferred_element_type=F32)


def whole(shape):
    return pl.BlockSpec(shape, lambda *_: (0,) * len(shape))


VM = pl.BlockSpec(memory_space=pltpu.VMEM)
SM = pl.BlockSpec(memory_space=pltpu.SMEM)


def gather_body(idx_ref, eye_ref, feat_ref, out_ref):
    turned = dot_nt(eye_ref[...], idx_ref[...].astype(F32).astype(BF16))
    lane = lax.broadcasted_iota(jnp.int32, (64, 128), 1).astype(F32)
    picks = []
    for q in range(PICK):
        col = jnp.broadcast_to(turned[:, q : q + 1], (64, 128))
        picks.append(jnp.where(col == lane, 1.0, 0.0).astype(BF16))
    kinds = [jnp.concatenate([x[16 * v : 16 * v + 16] for x in picks], axis=0) for v in range(4)]
    for j in range(3):
        left = jnp.concatenate([kinds[0], kinds[j + 1]], axis=1)
        right = jnp.concatenate(
            [
                jnp.concatenate([feat_ref[j], feat_ref[j + 3]], axis=1),
                jnp.concatenate([feat_ref[7], feat_ref[8]], axis=1),
            ],
            axis=0,
        )
        got = dot(left, right).astype(BF16)
        out_ref[:, 4 * j : 4 * j + 4] = got[:, :128].reshape(PICK, 4, 4, 128)
        out_ref[:, 4 * (j + 3) : 4 * (j + 4)] = got[:, 128:].reshape(PICK, 4, 4, 128)
    last = dot(kinds[0], feat_ref[6]).astype(BF16)
    out_ref[:, 24:27] = last.reshape(PICK, 4, 4, 128)[:, :3]


def request_body(blocks_ref, rows_ref, cols_ref, out_ref, seen_ref):
    peers, ends = out_ref.shape[0], 2 * blocks_ref.shape[0]
    out_ref[...] = jnp.full(out_ref.shape, -1, jnp.int32)

    def clear(o, carry):
        seen_ref[o] = 0
        return carry

    lax.fori_loop(0, peers, clear, 0, unroll=8)
    cols = cols_ref[...]
    for end in range(ends):
        pair, side = divmod(end, 2)
        owner = blocks_ref[pair, side]
        slot = seen_ref[owner]
        seen_ref[owner] = slot + 1
        line = out_ref[owner]
        for k in range(6):
            line = jnp.where(cols == 6 * slot + k, rows_ref[side, k, pair], line)
        out_ref[owner] = line


def request_rows(blocks, rows, peers):
    cols = jnp.asarray(request_columns()[None], jnp.int32)
    return pl.pallas_call(
        request_body,
        in_specs=[SM, SM, VM],
        out_specs=VM,
        out_shape=jax.ShapeDtypeStruct((peers, 1, 64), jnp.int32),
        scratch_shapes=[pltpu.SMEM((peers,), jnp.int32)],
        name="request_rows",
    )(blocks, rows, cols)


def pick_rows(idx, eye, feat):
    peers = idx.shape[0]
    return pl.pallas_call(
        gather_body,
        grid=(peers // PICK,),
        in_specs=[
            pl.BlockSpec((PICK, 64), lambda c: (c, 0)),
            whole((64, 64)),
            whole((9, 128, 128)),
        ],
        out_specs=pl.BlockSpec((PICK, GROUPS, 4, 128), lambda c: (c, 0, 0, 0)),
        out_shape=jax.ShapeDtypeStruct((peers, GROUPS, 4, 128), BF16),
        compiler_params=pltpu.CompilerParams(vmem_limit_bytes=VMEM_LIMIT // 2),
        cost_estimate=pl.CostEstimate(flops=2 * 10**9, transcendentals=0, bytes_accessed=4 * 10**6),
        name="pick_rows",
    )(idx, eye, feat)


def prep_body(ra_ref, rb_ref, sp_ref, spt_ref, rows_ref, rowst_ref, wt_ref, ws_ref, vt_ref, vs_ref):
    a = ra_ref[0]
    a_hi = a.astype(BF16)
    a_lo = (a - a_hi.astype(F32)).astype(BF16)
    lane = lax.broadcasted_iota(jnp.int32, (224, 32), 1)
    a_both = jnp.where(lane < 16, a_hi.astype(F32), a_lo.astype(F32)).astype(BF16)
    x = dot(a_both, sp_ref[...])
    rows = jnp.broadcast_to(rows_ref[0:1, :], (224, 256))
    for at, out in ((9, wt_ref), (10, ws_ref)):
        mine = jnp.broadcast_to(a[:, at : at + 1], (224, 256))
        out[0] = jnp.where(mine == rows, x, 0.0).astype(BF16)
    b = rb_ref[0]
    b_hi = b.astype(BF16)
    b_lo = (b - b_hi.astype(F32)).astype(BF16)
    line = lax.broadcasted_iota(jnp.int32, (32, 256), 0)
    b_both = jnp.where(line < 16, b_hi.astype(F32), b_lo.astype(F32)).astype(BF16)
    y = dot(spt_ref[...], b_both)
    rowst = jnp.broadcast_to(rowst_ref[:, 0:1], (224, 256))
    for at, out in ((9, vt_ref), (10, vs_ref)):
        mine = jnp.broadcast_to(b[at : at + 1, :], (224, 256))
        out[0] = jnp.where(mine == rowst, y, 0.0).astype(BF16)


def build_turns(ra, rb):
    pairs = ra.shape[0]
    spread, rows = spread_tables()
    sp = jnp.asarray(spread, BF16)
    spt = jnp.asarray(spread[:, :224].T, BF16)
    rows8 = jnp.asarray(np.tile(rows[None], (8, 1)), F32)
    rowst = jnp.asarray(np.tile(rows[:224, None], (1, 128)), F32)
    one = jax.ShapeDtypeStruct((pairs, 224, 256), BF16)
    block = pl.BlockSpec((1, 224, 256), lambda p: (p, 0, 0))
    return pl.pallas_call(
        prep_body,
        grid=(pairs,),
        in_specs=[
            pl.BlockSpec((1, 224, 32), lambda p: (p, 0, 0)),
            pl.BlockSpec((1, 32, 256), lambda p: (p, 0, 0)),
            whole((32, 256)),
            whole((224, 32)),
            whole((8, 256)),
            whole((224, 128)),
        ],
        out_specs=[block] * 4,
        out_shape=[one] * 4,
        cost_estimate=pl.CostEstimate(flops=10**9, transcendentals=0, bytes_accessed=10**7),
        name="build_turns",
    )(ra, rb, sp, spt, rows8, rowst)


def turn(w_ref, r_ref, pair, owner):
    groups = r_ref[owner]
    last = jnp.concatenate([groups[24:27], jnp.zeros((1, 4, 128), BF16)], axis=0).reshape(16, 128)
    chunk = jnp.concatenate([groups[:24].reshape(96, 128), last], axis=0)
    right = jnp.concatenate([chunk, chunk, jnp.zeros((32, 128), BF16)], axis=0)
    return dot(w_ref[pair], right)


def turn_back(v_ref, pair, src_ref, base):
    parts = [src_ref[pl.ds(base, 24), 128 * k : 128 * k + 128] for k in range(9)]
    x = jnp.concatenate(parts + [jnp.zeros((40, 128), F32)], axis=0)
    hi = x.astype(BF16)
    lo = (x - hi.astype(F32)).astype(BF16)
    y = dot(v_ref[pair], jnp.concatenate([hi, lo], axis=1))
    y = y[:, :128] + y[:, 128:]
    y = (y[:CH] + y[CH:]).astype(BF16)
    return y.reshape(GROUPS + 1, 4, 128)[:GROUPS]


def forward_body(
    own_ref, r_ref, wt_ref, ws_ref, vt_ref, vs_ref, a0_ref, a1_ref, a2_ref, b0_ref, b1_ref, b2_ref,
    out_ref, z_ref, hid_ref, gate_ref, act_ref, mix_ref,
):
    half = z_ref.shape[0] // 2
    pairs = wt_ref.shape[0]

    def lift(d, carry):
        turned = []
        for p in (2 * d, 2 * d + 1):
            turned.append((turn(ws_ref, r_ref, p, own_ref[2 * p + 1]), turn(wt_ref, r_ref, p, own_ref[2 * p])))
        (s0, t0), (s1, t1) = turned
        at = pl.multiple_of(d * 48, 16)
        for k in range(9):
            lines = slice(24 * k, 24 * k + 24)
            s = jnp.concatenate([s0[lines], s1[lines]], axis=0).astype(BF16)
            t = jnp.concatenate([t0[lines], t1[lines]], axis=0).astype(BF16)
            z_ref[pl.ds(at, 48), 256 * k : 256 * k + 128] = s
            z_ref[pl.ds(at, 48), 256 * k + 128 : 256 * k + 256] = t
            z_ref[pl.ds(half + at, 48), 256 * k : 256 * k + 128] = t
            z_ref[pl.ds(half + at, 48), 256 * k + 128 : 256 * k + 256] = s
        return carry

    lax.fori_loop(0, pairs // 2, lift, 0)

    def layer(b, carry):
        at = pl.multiple_of(b * 256, 256)
        here = pl.ds(at, 256)
        o = dot(z_ref[here, 0:768], a0_ref[...])
        gate = jax.nn.sigmoid(o[:, 384:512])
        gate_ref[here, :] = gate
        h0 = o[:, 0:128]
        hid_ref[here, 0:384] = o[:, 0:384]
        act_ref[here, 0:128] = (h0 * jax.nn.sigmoid(h0)).astype(BF16)
        for k in range(1, 3):
            cols = slice(128 * k, 128 * k + 128)
            act_ref[here, cols] = (o[:, cols] * gate).astype(BF16)
        h1 = dot(z_ref[here, 768:1792], a1_ref[...])
        hid_ref[here, 384:896] = h1
        for k in range(4):
            act_ref[here, 384 + 128 * k : 512 + 128 * k] = (h1[:, 128 * k : 128 * k + 128] * gate).astype(BF16)
        h2 = dot(z_ref[here, 1792:2304], a2_ref[...])
        hid_ref[here, 896:1152] = h2
        for k in range(2):
            act_ref[here, 896 + 128 * k : 1024 + 128 * k] = (h2[:, 128 * k : 128 * k + 128] * gate).astype(BF16)
        mix_ref[here, 0:384] = dot(act_ref[here, 0:384], b0_ref[...])
        mix_ref[here, 384:896] = dot(act_ref[here, 384:896], b1_ref[...])
        mix_ref[here, 896:1152] = dot(act_ref[here, 896:1152], b2_ref[...])
        return carry

    lax.fori_loop(0, z_ref.shape[0] // 256, layer, 0)
    out_ref[...] = jnp.zeros(out_ref.shape, BF16)

    def unlift(p, carry):
        at = pl.multiple_of(p * 24, 8)
        t = own_ref[2 * p]
        out_ref[t] = out_ref[t] + turn_back(vt_ref, p, mix_ref, at)
        s = own_ref[2 * p + 1]
        out_ref[s] = out_ref[s] + turn_back(vs_ref, p, mix_ref, half + at)
        return carry

    lax.fori_loop(0, pairs, unlift, 0)


def forward(owners, got, turns, weights, rows):
    peers = got.shape[0]
    return pl.pallas_call(
        forward_body,
        in_specs=[SM] + [VM] * 11,
        out_specs=[VM] * 5,
        out_shape=[
            jax.ShapeDtypeStruct((peers, GROUPS, 4, 128), BF16),
            jax.ShapeDtypeStruct((rows, 2304), BF16),
            jax.ShapeDtypeStruct((rows, 1152), F32),
            jax.ShapeDtypeStruct((rows, 128), F32),
            jax.ShapeDtypeStruct((rows, 1152), BF16),
        ],
        scratch_shapes=[pltpu.VMEM((rows, 1152), F32)],
        compiler_params=pltpu.CompilerParams(vmem_limit_bytes=VMEM_LIMIT),
        cost_estimate=pl.CostEstimate(flops=10**10, transcendentals=10**6, bytes_accessed=3 * 10**7),
        name="forward",
    )(owners, got, *turns, *weights)


def backward_body(
    own_ref, r_ref, wt_ref, ws_ref, vt_ref, vs_ref, a0_ref, a1_ref, a2_ref, b0_ref, b1_ref, b2_ref,
    z_ref, hid_ref, gate_ref, act_ref, out_ref, wg_ref, dmix_ref, dd_ref, gs_ref, gt_ref, *, scale,
):
    half = z_ref.shape[0] // 2
    pairs = wt_ref.shape[0]

    def lift(d, carry):
        turned = []
        for p in (2 * d, 2 * d + 1):
            turned.append((turn(wt_ref, r_ref, p, own_ref[2 * p]), turn(ws_ref, r_ref, p, own_ref[2 * p + 1])))
        (t0, s0), (t1, s1) = turned
        at = pl.multiple_of(d * 48, 16)
        for k in range(9):
            lines = slice(24 * k, 24 * k + 24)
            cols = slice(128 * k, 128 * k + 128)
            dmix_ref[pl.ds(at, 48), cols] = jnp.concatenate([t0[lines], t1[lines]], axis=0).astype(BF16)
            dmix_ref[pl.ds(half + at, 48), cols] = jnp.concatenate([s0[lines], s1[lines]], axis=0).astype(BF16)
        return carry

    lax.fori_loop(0, pairs // 2, lift, 0)

    def layer(b, carry):
        at = pl.multiple_of(b * 128, 128)
        spots = (pl.ds(at, 128), pl.ds(half + at, 128))

        def rows_of(ref, cols):
            return jnp.concatenate([ref[spot, cols] for spot in spots], axis=0)

        def put(col, value):
            value = value.astype(BF16)
            for i, spot in enumerate(spots):
                dd_ref[spot, col : col + 128] = value[128 * i : 128 * i + 128]

        gate = rows_of(gate_ref, slice(0, 128))
        dact0 = dot_nt(rows_of(dmix_ref, slice(0, 384)), b0_ref[...])
        h0 = rows_of(hid_ref, slice(0, 128))
        head = jax.nn.sigmoid(h0)
        put(0, dact0[:, 0:128] * head * (1.0 + h0 * (1.0 - head)))
        total = None

        def gated(k, piece, col):
            put(col, piece * gate)
            return piece * rows_of(hid_ref, slice(128 * k, 128 * k + 128))

        total = gated(1, dact0[:, 128:256], 128) + gated(2, dact0[:, 256:384], 256)
        dact1 = dot_nt(rows_of(dmix_ref, slice(384, 896)), b1_ref[...])
        for k in range(4):
            total = total + gated(3 + k, dact1[:, 128 * k : 128 * k + 128], 512 + 128 * k)
        dact2 = dot_nt(rows_of(dmix_ref, slice(896, 1152)), b2_ref[...])
        for k in range(2):
            total = total + gated(7 + k, dact2[:, 128 * k : 128 * k + 128], 1024 + 128 * k)
        put(384, total * gate * (1.0 - gate))

        first = 0
        for cols, w_ref, count in ((slice(0, 512), a0_ref, 3), (slice(512, 1024), a1_ref, 4), (slice(1024, 1280), a2_ref, 2)):
            dz = dot_nt(rows_of(dd_ref, cols), w_ref[...])
            for k in range(count):
                lo = dz[:, 256 * k : 256 * k + 128]
                hi = dz[:, 256 * k + 128 : 256 * k + 256]
                to = slice(128 * (first + k), 128 * (first + k) + 128)
                gs_ref[spots[0], to] = lo[:128] + hi[128:]
                gt_ref[spots[0], to] = hi[:128] + lo[128:]
            first += count
        return carry

    lax.fori_loop(0, half // 128, layer, 0)
    out_ref[...] = jnp.zeros(out_ref.shape, BF16)

    def unlift(p, carry):
        at = pl.multiple_of(p * 24, 8)
        s = own_ref[2 * p + 1]
        out_ref[s] = out_ref[s] + turn_back(vs_ref, p, gs_ref, at)
        t = own_ref[2 * p]
        out_ref[t] = out_ref[t] + turn_back(vt_ref, p, gt_ref, at)
        return carry

    lax.fori_loop(0, pairs, unlift, 0)

    def put_rows(row, value):
        wg_ref[row : row + value.shape[0], :] = (value * scale).astype(BF16)

    wg_ref[8064:8192, :] = jnp.zeros((128, 128), BF16)

    def plain(left_ref, left_at, height, right_ref, right_cols, row):
        for c in range(height // 128):
            g = dot_tn(left_ref[:, left_at + 128 * c : left_at + 128 * c + 128], right_ref[:, right_cols])
            for n in range(g.shape[1] // 128):
                put_rows(row + n * height + 128 * c, g[:, 128 * n : 128 * n + 128])

    def folded(left_ref, left_at, height, right_ref, right_cols, row):
        width = (right_cols.stop - right_cols.start) // 2
        blocks = width // 128
        for c in range(height // 128):
            low = left_at + 128 * c
            top = dot_tn(left_ref[:, low : low + 128], right_ref[:, right_cols])
            bot = dot_tn(left_ref[:, low + height : low + height + 128], right_ref[:, right_cols])
            same = top[:, :width] + bot[:, width:]
            cross = top[:, width:] - bot[:, :width]
            for n in range(blocks):
                cols = slice(128 * n, 128 * n + 128)
                put_rows(row + n * height + 128 * c, same[:, cols])
                put_rows(row + (blocks + n) * height + 128 * c, cross[:, cols])

    plain(z_ref, 0, 768, dd_ref, slice(0, 512), 0)
    folded(z_ref, 768, 512, dd_ref, slice(512, 1024), 3072)
    folded(z_ref, 1792, 256, dd_ref, slice(1024, 1280), 5120)
    plain(act_ref, 0, 384, dmix_ref, slice(0, 384), 5632)
    folded(act_ref, 384, 256, dmix_ref, slice(384, 896), 6784)
    folded(act_ref, 896, 128, dmix_ref, slice(896, 1152), 7808)


def backward(owners, got, turns, weights, kept, scale):
    peers = got.shape[0]
    rows = kept[0].shape[0]

    def body(*refs):
        backward_body(*refs, scale=scale)

    return pl.pallas_call(
        body,
        in_specs=[SM] + [VM] * 15,
        out_specs=[VM, VM],
        out_shape=[
            jax.ShapeDtypeStruct((peers, GROUPS, 4, 128), BF16),
            jax.ShapeDtypeStruct((WEIGHT_ROWS, 128), BF16),
        ],
        scratch_shapes=[
            pltpu.VMEM((rows, 1152), BF16),
            pltpu.VMEM((rows, 1280), BF16),
            pltpu.VMEM((rows // 2, 1152), F32),
            pltpu.VMEM((rows // 2, 1152), F32),
        ],
        compiler_params=pltpu.CompilerParams(vmem_limit_bytes=VMEM_LIMIT),
        cost_estimate=pl.CostEstimate(flops=2 * 10**10, transcendentals=10**6, bytes_accessed=3 * 10**7),
        name="backward",
    )(owners, got, *turns, *weights, *kept)


def scatter_body(idx_ref, got_ref, out_ref, acc_ref, last_ref, *, first):
    @pl.when(pl.program_id(0) == 0)
    def _():
        acc_ref[...] = jnp.zeros(acc_ref.shape, F32)
        last_ref[...] = jnp.zeros(last_ref.shape, F32)

    atom = lax.broadcasted_iota(jnp.int32, (128, 256), 0)
    kinds = [
        jnp.where(jnp.broadcast_to(idx_ref[v : v + 1, :], (128, 256)) == atom, 1.0, 0.0).astype(BF16)
        for v in range(4)
    ]
    tiles = [got_ref[:, first + 4 * t : first + 4 * t + 4].reshape(256, 128) for t in range(6)]
    last = got_ref[:, first + 24 : first + 27]
    tiles.append(jnp.concatenate([last, jnp.zeros((16, 1, 4, 128), BF16)], axis=1).reshape(256, 128))
    acc_ref[...] += dot(kinds[0], jnp.concatenate(tiles, axis=1))
    spare = jnp.concatenate([jnp.concatenate([tiles[j], tiles[j + 3]], axis=1) for j in range(3)], axis=0)
    last_ref[...] += dot(jnp.concatenate(kinds[1:], axis=1), spare)

    @pl.when(pl.program_id(0) == pl.num_programs(0) - 1)
    def _():
        for k in range(7):
            out_ref[k] = acc_ref[:, 128 * k : 128 * k + 128].astype(out_ref.dtype)
        for k in range(2):
            out_ref[7 + k] = last_ref[:, 128 * k : 128 * k + 128].astype(out_ref.dtype)


def add_rows(idx_rows, got, dtype):
    peers, groups = got.shape[:2]

    def body(*refs):
        scatter_body(*refs, first=groups - GROUPS)

    return pl.pallas_call(
        body,
        grid=(peers // 16,),
        in_specs=[
            pl.BlockSpec((8, 256), lambda c: (0, c)),
            pl.BlockSpec((16, groups, 4, 128), lambda c: (c, 0, 0, 0)),
        ],
        out_specs=whole((9, 128, 128)),
        out_shape=jax.ShapeDtypeStruct((9, 128, 128), dtype),
        scratch_shapes=[pltpu.VMEM((128, 896), F32), pltpu.VMEM((128, 256), F32)],
        cost_estimate=pl.CostEstimate(flops=10**9, transcendentals=0, bytes_accessed=6 * 10**6),
        name="add_rows",
    )(idx_rows, got)


def swapped(x):
    return lax.ppermute(x, "atoms", [(i, i ^ 1) for i in range(lax.axis_size("atoms"))])


def add_pair(core, grads, other):
    half = other.shape[0]

    def body(core_ref, grads_ref, other_ref, out_ref):
        mine = grads_ref[pl.ds(pl.multiple_of(core_ref[0] * half, 16), half), :]
        total = mine.astype(F32) + other_ref[...].astype(F32)
        out_ref[...] = total.astype(BF16).reshape(half // WR, WR // 4, 4, 128)

    return pl.pallas_call(
        body,
        in_specs=[SM, VM, VM],
        out_specs=VM,
        out_shape=jax.ShapeDtypeStruct((half // WR, WR // 4, 4, 128), BF16),
        cost_estimate=pl.CostEstimate(flops=10**6, transcendentals=0, bytes_accessed=4 * 10**6),
        name="add_pair",
    )(core, grads, other)


def add_peers(got):
    peers = got.shape[0]
    chips = peers // 2

    def body(got_ref, out_ref):
        x = got_ref[...].reshape(peers, 16, 128).astype(F32).reshape(chips, 2, 16, 128)
        total = jnp.sum(x, axis=0).astype(BF16)
        out_ref[...] = jnp.broadcast_to(total[None], (chips, 2, 16, 128))

    return pl.pallas_call(
        body,
        grid=(WR // 16,),
        in_specs=[pl.BlockSpec((peers, 4, 4, 128), lambda i: (0, i, 0, 0))],
        out_specs=pl.BlockSpec((chips, 2, 16, 128), lambda i: (0, 0, i, 0)),
        out_shape=jax.ShapeDtypeStruct((chips, 2, WR, 128), BF16),
        compiler_params=pltpu.CompilerParams(vmem_limit_bytes=VMEM_LIMIT // 2),
        cost_estimate=pl.CostEstimate(flops=10**6, transcendentals=0, bytes_accessed=3 * 10**6),
        name="add_peers",
    )(got)


WEIGHT_PARTS = (
    (0, 1, 768, 4), (3072, 2, 512, 2), (5120, 2, 256, 1), (5632, 1, 384, 3), (6784, 2, 256, 2), (7808, 2, 128, 1),
)


def unpack(core, mine, other):
    chips = mine.shape[0]

    def body(core_ref, mine_ref, other_ref, *outs):
        for out, (row, parts, height, blocks) in zip(outs, WEIGHT_PARTS):
            for p in range(parts):
                for n in range(blocks):
                    cols = slice(128 * n, 128 * n + 128)
                    for at in range(0, height, 2 * WR):
                        half, chip = divmod((row + (p * blocks + n) * height + at) // (2 * WR), chips)
                        low = pl.multiple_of(at + WR * core_ref[0], WR)
                        out[p, pl.ds(low, WR), cols] = mine_ref[chip, half].astype(F32)
                        low = pl.multiple_of(at + WR * (1 - core_ref[0]), WR)
                        out[p, pl.ds(low, WR), cols] = other_ref[chip, half].astype(F32)

    return pl.pallas_call(
        body,
        in_specs=[SM, VM, VM],
        out_specs=[VM] * 6,
        out_shape=[jax.ShapeDtypeStruct((parts, height, 128 * blocks), F32) for _, parts, height, blocks in WEIGHT_PARTS],
        compiler_params=pltpu.CompilerParams(vmem_limit_bytes=VMEM_LIMIT // 2),
        cost_estimate=pl.CostEstimate(flops=10**6, transcendentals=0, bytes_accessed=6 * 10**6),
        name="unpack",
    )(core, mine, other)


def widen_pair(w):
    upper = jnp.concatenate([w[0], w[1]], axis=1)
    lower = jnp.concatenate([-w[1], w[0]], axis=1)
    return jnp.concatenate([upper, lower], axis=0)


def exchange(x):
    return lax.all_to_all(x, "atoms", split_axis=0, concat_axis=0, tiled=True)


def local(
    features, cotangent, wigner, pair_blocks, pair_rows, edge_ends,
    first_m0, first_m1, first_m2, second_m0, second_m1, second_m2,
):
    peers = lax.axis_size("atoms")
    pairs = pair_blocks.shape[0]
    edges = edge_ends.shape[1]
    each = edges // pairs
    owners = pair_blocks.reshape(2 * pairs)
    ends = jnp.arange(2 * pairs, dtype=jnp.int32)
    slots = jnp.sum(
        jnp.logical_and(owners[:, None] == owners[None, :], ends[:, None] > ends[None, :]), axis=1
    ).astype(jnp.int32)

    asked = exchange(request_rows(pair_blocks, pair_rows, peers)).reshape(peers, 64)
    asked_rows = jnp.transpose(asked.reshape(peers, 4, 16), (1, 0, 2)).reshape(4, peers * 16)
    asked_rows = jnp.concatenate([asked_rows, asked_rows], axis=0)
    eye = jnp.eye(64, dtype=BF16)

    got_f = exchange(pick_rows(asked, eye, jnp.transpose(features, (1, 0, 2))))

    turned = jnp.stack([wigner[i] for i in COEF_ORDER]).reshape(9, 9, pairs, each)
    pos = jnp.stack(
        [
            (slots.reshape(pairs, 2)[:, side, None] * 6 + edge_ends[side].reshape(pairs, each)).astype(F32)
            for side in range(2)
        ],
        axis=0,
    )
    pos = jnp.broadcast_to(pos[:, None], (2, 9, pairs, each))
    by_j = jnp.transpose(turned, (1, 0, 2, 3))
    gap5 = jnp.zeros((5, 9, pairs, each), F32)
    gap7 = jnp.zeros((7, 9, pairs, each), F32)
    table = jnp.concatenate([by_j, pos, gap5, by_j, gap7], axis=0)
    ra = jnp.transpose(table, (2, 1, 3, 0)).reshape(pairs, 9 * each, 32)
    ra = jnp.pad(ra, ((0, 0), (0, 224 - 9 * each), (0, 0)))
    rb = jnp.transpose(table, (2, 0, 1, 3)).reshape(pairs, 32, 9 * each)
    rb = jnp.pad(rb, ((0, 0), (0, 0), (0, 256 - 9 * each)))
    turns = build_turns(ra, rb)

    weights = (
        first_m0, widen_pair(first_m1), widen_pair(first_m2),
        second_m0, widen_pair(second_m1), widen_pair(second_m2),
    )
    picked_c = pick_rows(asked, eye, jnp.transpose(cotangent, (1, 0, 2)))
    picked_c, turns, weights = lax.optimization_barrier((picked_c, turns, weights))
    got_c = exchange(picked_c)
    back_m, *kept = forward(owners, got_f, turns, weights, 2 * edges)
    got_m = exchange(back_m)
    scale = float((2.0 * edges * peers) ** (-0.5))
    back_g, grads = backward(owners, got_c, turns, weights, kept, scale)
    core = (lax.axis_index("atoms") % 2).astype(jnp.int32)
    cores = jnp.stack([core, core])
    half = WEIGHT_ROWS // 2
    sent = lax.dynamic_slice_in_dim(grads, (1 - core) * half, half, axis=0)
    w_rows = add_pair(cores, grads, swapped(sent))
    both = jnp.concatenate([w_rows, back_g], axis=1)
    both, got_m = lax.optimization_barrier((both, got_m))
    messages = add_rows(asked_rows, got_m, BF16)
    got_g, messages = lax.optimization_barrier((exchange(both), messages))
    same_core = [list(range(c, peers, 2)) for c in range(2)]
    w_mine = lax.all_to_all(
        add_peers(got_g).reshape(peers // 2, 2 * WR, 128), "atoms",
        split_axis=0, concat_axis=0, tiled=True, axis_index_groups=same_core,
    ).reshape(peers // 2, 2, WR, 128)
    grad_features = add_rows(asked_rows, got_g, F32)
    w_mine, grad_features = lax.optimization_barrier((w_mine, grad_features))
    messages = jnp.transpose(messages, (1, 0, 2))
    grad_features = jnp.transpose(grad_features, (1, 0, 2))
    w = unpack(cores, w_mine, swapped(w_mine))
    return (messages, grad_features, w[0][0], w[1], w[2], w[3][0], w[4], w[5])


def solution(mesh):
    rows = P("atoms", None, None)
    in_specs = (
        rows, rows, P(None, None, "atoms"), P("atoms", None), P(None, None, "atoms"), P(None, "atoms"),
        P(), P(), P(), P(), P(), P(),
    )
    out_specs = (rows, rows, P(), P(), P(), P(), P(), P())
    return jax.shard_map(local, mesh=mesh, in_specs=in_specs, out_specs=out_specs, check_vma=False)
```

```python
import jax
import jax.numpy as jnp
import numpy as np
from jax import lax
from jax.experimental import pallas as pl
from jax.experimental.pallas import tpu as pltpu
from jax.sharding import PartitionSpec as P

COEF_ORDER = (0, 2, 6, 3, 7, 1, 5, 8, 4)
F32 = jnp.float32
BF16 = jnp.bfloat16
CH = 112
GROUPS = 27
WEIGHT_ROWS = 8192
WR = 32
PICK = 64
VMEM_LIMIT = 58 * 1024 * 1024


def chunk_maps():
    coef = np.full((CH,), -1)
    row = np.full((CH,), -1)
    for line in range(CH):
        tile, at = divmod(line, 16)
        if at < 12:
            coef[line], row[line] = tile, at
        elif tile < 6:
            coef[line], row[line] = 7 + tile // 3, 4 * (tile % 3) + at - 12
    return coef, row


def spread_tables():
    coef, row = chunk_maps()
    spread = np.zeros((32, 256), np.float32)
    rows = np.full((256,), -1.0, np.float32)
    for half in range(2):
        for line in range(CH):
            if coef[line] >= 0:
                spread[16 * half + coef[line], CH * half + line] = 1.0
                rows[CH * half + line] = row[line]
    return spread, rows


def request_columns():
    cols = np.full((64,), -1)
    cols[:12] = np.arange(12)
    for j in range(3):
        cols[16 * (j + 1) + 12 : 16 * (j + 2)] = 4 * j + np.arange(4)
    return cols


def dot(a, b):
    return jnp.dot(a, b, preferred_element_type=F32)


def dot_nt(a, b):
    return lax.dot_general(a, b, (((1,), (1,)), ((), ())), preferred_element_type=F32)


def dot_tn(a, b):
    return lax.dot_general(a, b, (((0,), (0,)), ((), ())), preferred_element_type=F32)


def whole(shape):
    return pl.BlockSpec(shape, lambda *_: (0,) * len(shape))


VM = pl.BlockSpec(memory_space=pltpu.VMEM)
SM = pl.BlockSpec(memory_space=pltpu.SMEM)


def gather_body(idx_ref, eye_ref, feat_ref, out_ref):
    turned = dot_nt(eye_ref[...], idx_ref[...].astype(F32).astype(BF16))
    lane = lax.broadcasted_iota(jnp.int32, (64, 128), 1).astype(F32)
    picks = []
    for q in range(PICK):
        col = jnp.broadcast_to(turned[:, q : q + 1], (64, 128))
        picks.append(jnp.where(col == lane, 1.0, 0.0).astype(BF16))
    kinds = [jnp.concatenate([x[16 * v : 16 * v + 16] for x in picks], axis=0) for v in range(4)]
    for j in range(3):
        left = jnp.concatenate([kinds[0], kinds[j + 1]], axis=1)
        right = jnp.concatenate(
            [
                jnp.concatenate([feat_ref[j], feat_ref[j + 3]], axis=1),
                jnp.concatenate([feat_ref[7], feat_ref[8]], axis=1),
            ],
            axis=0,
        )
        got = dot(left, right).astype(BF16)
        out_ref[:, 4 * j : 4 * j + 4] = got[:, :128].reshape(PICK, 4, 4, 128)
        out_ref[:, 4 * (j + 3) : 4 * (j + 4)] = got[:, 128:].reshape(PICK, 4, 4, 128)
    last = dot(kinds[0], feat_ref[6]).astype(BF16)
    out_ref[:, 24:27] = last.reshape(PICK, 4, 4, 128)[:, :3]


def request_body(blocks_ref, rows_ref, cols_ref, out_ref, seen_ref):
    peers, ends = out_ref.shape[0], 2 * blocks_ref.shape[1]
    out_ref[...] = jnp.full(out_ref.shape, -1, jnp.int32)

    def clear(o, carry):
        seen_ref[o] = 0
        return carry

    lax.fori_loop(0, peers, clear, 0, unroll=8)
    cols = cols_ref[...]
    for end in range(ends):
        pair, side = divmod(end, 2)
        owner = blocks_ref[side, pair]
        slot = seen_ref[owner]
        seen_ref[owner] = slot + 1
        line = out_ref[owner]
        for k in range(6):
            line = jnp.where(cols == 6 * slot + k, rows_ref[k, side, pair], line)
        out_ref[owner] = line


def request_rows(blocks, rows, peers):
    cols = jnp.asarray(request_columns()[None], jnp.int32)
    return pl.pallas_call(
        request_body,
        in_specs=[SM, SM, VM],
        out_specs=VM,
        out_shape=jax.ShapeDtypeStruct((peers, 1, 64), jnp.int32),
        scratch_shapes=[pltpu.SMEM((peers,), jnp.int32)],
        name="request_rows",
    )(blocks, rows, cols)


def pick_rows(idx, eye, feat):
    peers = idx.shape[0]
    return pl.pallas_call(
        gather_body,
        grid=(peers // PICK,),
        in_specs=[
            pl.BlockSpec((PICK, 64), lambda c: (c, 0)),
            whole((64, 64)),
            whole((9, 128, 128)),
        ],
        out_specs=pl.BlockSpec((PICK, GROUPS, 4, 128), lambda c: (c, 0, 0, 0)),
        out_shape=jax.ShapeDtypeStruct((peers, GROUPS, 4, 128), BF16),
        compiler_params=pltpu.CompilerParams(vmem_limit_bytes=VMEM_LIMIT // 2),
        cost_estimate=pl.CostEstimate(flops=2 * 10**9, transcendentals=0, bytes_accessed=4 * 10**6),
        name="pick_rows",
    )(idx, eye, feat)


def prep_body(ra_ref, rb_ref, sp_ref, spt_ref, rows_ref, rowst_ref, wt_ref, ws_ref, vt_ref, vs_ref):
    a = ra_ref[0]
    a_hi = a.astype(BF16)
    a_lo = (a - a_hi.astype(F32)).astype(BF16)
    lane = lax.broadcasted_iota(jnp.int32, (224, 32), 1)
    a_both = jnp.where(lane < 16, a_hi.astype(F32), a_lo.astype(F32)).astype(BF16)
    x = dot(a_both, sp_ref[...])
    rows = jnp.broadcast_to(rows_ref[0:1, :], (224, 256))
    for at, out in ((9, wt_ref), (10, ws_ref)):
        mine = jnp.broadcast_to(a[:, at : at + 1], (224, 256))
        out[0] = jnp.where(mine == rows, x, 0.0).astype(BF16)
    b = rb_ref[0]
    b_hi = b.astype(BF16)
    b_lo = (b - b_hi.astype(F32)).astype(BF16)
    line = lax.broadcasted_iota(jnp.int32, (32, 256), 0)
    b_both = jnp.where(line < 16, b_hi.astype(F32), b_lo.astype(F32)).astype(BF16)
    y = dot(spt_ref[...], b_both)
    rowst = jnp.broadcast_to(rowst_ref[:, 0:1], (224, 256))
    for at, out in ((9, vt_ref), (10, vs_ref)):
        mine = jnp.broadcast_to(b[at : at + 1, :], (224, 256))
        out[0] = jnp.where(mine == rowst, y, 0.0).astype(BF16)


def build_turns(ra, rb):
    pairs = ra.shape[0]
    spread, rows = spread_tables()
    sp = jnp.asarray(spread, BF16)
    spt = jnp.asarray(spread[:, :224].T, BF16)
    rows8 = jnp.asarray(np.tile(rows[None], (8, 1)), F32)
    rowst = jnp.asarray(np.tile(rows[:224, None], (1, 128)), F32)
    one = jax.ShapeDtypeStruct((pairs, 224, 256), BF16)
    block = pl.BlockSpec((1, 224, 256), lambda p: (p, 0, 0))
    return pl.pallas_call(
        prep_body,
        grid=(pairs,),
        in_specs=[
            pl.BlockSpec((1, 224, 32), lambda p: (p, 0, 0)),
            pl.BlockSpec((1, 32, 256), lambda p: (p, 0, 0)),
            whole((32, 256)),
            whole((224, 32)),
            whole((8, 256)),
            whole((224, 128)),
        ],
        out_specs=[block] * 4,
        out_shape=[one] * 4,
        cost_estimate=pl.CostEstimate(flops=10**9, transcendentals=0, bytes_accessed=10**7),
        name="build_turns",
    )(ra, rb, sp, spt, rows8, rowst)


def turn(w_ref, r_ref, pair, owner):
    groups = r_ref[owner]
    last = jnp.concatenate([groups[24:27], jnp.zeros((1, 4, 128), BF16)], axis=0).reshape(16, 128)
    chunk = jnp.concatenate([groups[:24].reshape(96, 128), last], axis=0)
    right = jnp.concatenate([chunk, chunk, jnp.zeros((32, 128), BF16)], axis=0)
    return dot(w_ref[pair], right)


def turn_back(v_ref, pair, src_ref, base):
    parts = [src_ref[pl.ds(base, 24), 128 * k : 128 * k + 128] for k in range(9)]
    x = jnp.concatenate(parts + [jnp.zeros((40, 128), F32)], axis=0)
    hi = x.astype(BF16)
    lo = (x - hi.astype(F32)).astype(BF16)
    y = dot(v_ref[pair], jnp.concatenate([hi, lo], axis=1))
    y = y[:, :128] + y[:, 128:]
    y = (y[:CH] + y[CH:]).astype(BF16)
    return y.reshape(GROUPS + 1, 4, 128)[:GROUPS]


def forward_body(
    own_ref, r_ref, wt_ref, ws_ref, vt_ref, vs_ref, a0_ref, a1_ref, a2_ref, b0_ref, b1_ref, b2_ref,
    out_ref, z_ref, hid_ref, gate_ref, act_ref, mix_ref,
):
    half = z_ref.shape[0] // 2
    pairs = wt_ref.shape[0]

    def lift(d, carry):
        turned = []
        for p in (2 * d, 2 * d + 1):
            turned.append((turn(ws_ref, r_ref, p, own_ref[2 * p + 1]), turn(wt_ref, r_ref, p, own_ref[2 * p])))
        (s0, t0), (s1, t1) = turned
        at = pl.multiple_of(d * 48, 16)
        for k in range(9):
            lines = slice(24 * k, 24 * k + 24)
            s = jnp.concatenate([s0[lines], s1[lines]], axis=0).astype(BF16)
            t = jnp.concatenate([t0[lines], t1[lines]], axis=0).astype(BF16)
            z_ref[pl.ds(at, 48), 256 * k : 256 * k + 128] = s
            z_ref[pl.ds(at, 48), 256 * k + 128 : 256 * k + 256] = t
            z_ref[pl.ds(half + at, 48), 256 * k : 256 * k + 128] = t
            z_ref[pl.ds(half + at, 48), 256 * k + 128 : 256 * k + 256] = s
        return carry

    lax.fori_loop(0, pairs // 2, lift, 0)

    def layer(b, carry):
        at = pl.multiple_of(b * 256, 256)
        here = pl.ds(at, 256)
        o = dot(z_ref[here, 0:768], a0_ref[...])
        gate = jax.nn.sigmoid(o[:, 384:512])
        gate_ref[here, :] = gate
        h0 = o[:, 0:128]
        hid_ref[here, 0:384] = o[:, 0:384]
        act_ref[here, 0:128] = (h0 * jax.nn.sigmoid(h0)).astype(BF16)
        for k in range(1, 3):
            cols = slice(128 * k, 128 * k + 128)
            act_ref[here, cols] = (o[:, cols] * gate).astype(BF16)
        h1 = dot(z_ref[here, 768:1792], a1_ref[...])
        hid_ref[here, 384:896] = h1
        for k in range(4):
            act_ref[here, 384 + 128 * k : 512 + 128 * k] = (h1[:, 128 * k : 128 * k + 128] * gate).astype(BF16)
        h2 = dot(z_ref[here, 1792:2304], a2_ref[...])
        hid_ref[here, 896:1152] = h2
        for k in range(2):
            act_ref[here, 896 + 128 * k : 1024 + 128 * k] = (h2[:, 128 * k : 128 * k + 128] * gate).astype(BF16)
        mix_ref[here, 0:384] = dot(act_ref[here, 0:384], b0_ref[...])
        mix_ref[here, 384:896] = dot(act_ref[here, 384:896], b1_ref[...])
        mix_ref[here, 896:1152] = dot(act_ref[here, 896:1152], b2_ref[...])
        return carry

    lax.fori_loop(0, z_ref.shape[0] // 256, layer, 0)
    out_ref[...] = jnp.zeros(out_ref.shape, BF16)

    def unlift(p, carry):
        at = pl.multiple_of(p * 24, 8)
        t = own_ref[2 * p]
        out_ref[t] = out_ref[t] + turn_back(vt_ref, p, mix_ref, at)
        s = own_ref[2 * p + 1]
        out_ref[s] = out_ref[s] + turn_back(vs_ref, p, mix_ref, half + at)
        return carry

    lax.fori_loop(0, pairs, unlift, 0)


def forward(owners, got, turns, weights, rows):
    peers = got.shape[0]
    return pl.pallas_call(
        forward_body,
        in_specs=[SM] + [VM] * 11,
        out_specs=[VM] * 5,
        out_shape=[
            jax.ShapeDtypeStruct((peers, GROUPS, 4, 128), BF16),
            jax.ShapeDtypeStruct((rows, 2304), BF16),
            jax.ShapeDtypeStruct((rows, 1152), F32),
            jax.ShapeDtypeStruct((rows, 128), F32),
            jax.ShapeDtypeStruct((rows, 1152), BF16),
        ],
        scratch_shapes=[pltpu.VMEM((rows, 1152), F32)],
        compiler_params=pltpu.CompilerParams(vmem_limit_bytes=VMEM_LIMIT),
        cost_estimate=pl.CostEstimate(flops=10**10, transcendentals=10**6, bytes_accessed=3 * 10**7),
        name="forward",
    )(owners, got, *turns, *weights)


def backward_body(
    own_ref, r_ref, wt_ref, ws_ref, vt_ref, vs_ref, a0_ref, a1_ref, a2_ref, b0_ref, b1_ref, b2_ref,
    z_ref, hid_ref, gate_ref, act_ref, out_ref, wg_ref, dmix_ref, dd_ref, gs_ref, gt_ref, *, scale,
):
    half = z_ref.shape[0] // 2
    pairs = wt_ref.shape[0]

    def lift(d, carry):
        turned = []
        for p in (2 * d, 2 * d + 1):
            turned.append((turn(wt_ref, r_ref, p, own_ref[2 * p]), turn(ws_ref, r_ref, p, own_ref[2 * p + 1])))
        (t0, s0), (t1, s1) = turned
        at = pl.multiple_of(d * 48, 16)
        for k in range(9):
            lines = slice(24 * k, 24 * k + 24)
            cols = slice(128 * k, 128 * k + 128)
            dmix_ref[pl.ds(at, 48), cols] = jnp.concatenate([t0[lines], t1[lines]], axis=0).astype(BF16)
            dmix_ref[pl.ds(half + at, 48), cols] = jnp.concatenate([s0[lines], s1[lines]], axis=0).astype(BF16)
        return carry

    lax.fori_loop(0, pairs // 2, lift, 0)

    def layer(b, carry):
        at = pl.multiple_of(b * 128, 128)
        spots = (pl.ds(at, 128), pl.ds(half + at, 128))

        def rows_of(ref, cols):
            return jnp.concatenate([ref[spot, cols] for spot in spots], axis=0)

        def put(col, value):
            value = value.astype(BF16)
            for i, spot in enumerate(spots):
                dd_ref[spot, col : col + 128] = value[128 * i : 128 * i + 128]

        gate = rows_of(gate_ref, slice(0, 128))
        dact0 = dot_nt(rows_of(dmix_ref, slice(0, 384)), b0_ref[...])
        h0 = rows_of(hid_ref, slice(0, 128))
        head = jax.nn.sigmoid(h0)
        put(0, dact0[:, 0:128] * head * (1.0 + h0 * (1.0 - head)))
        total = None

        def gated(k, piece, col):
            put(col, piece * gate)
            return piece * rows_of(hid_ref, slice(128 * k, 128 * k + 128))

        total = gated(1, dact0[:, 128:256], 128) + gated(2, dact0[:, 256:384], 256)
        dact1 = dot_nt(rows_of(dmix_ref, slice(384, 896)), b1_ref[...])
        for k in range(4):
            total = total + gated(3 + k, dact1[:, 128 * k : 128 * k + 128], 512 + 128 * k)
        dact2 = dot_nt(rows_of(dmix_ref, slice(896, 1152)), b2_ref[...])
        for k in range(2):
            total = total + gated(7 + k, dact2[:, 128 * k : 128 * k + 128], 1024 + 128 * k)
        put(384, total * gate * (1.0 - gate))

        first = 0
        for cols, w_ref, count in ((slice(0, 512), a0_ref, 3), (slice(512, 1024), a1_ref, 4), (slice(1024, 1280), a2_ref, 2)):
            dz = dot_nt(rows_of(dd_ref, cols), w_ref[...])
            for k in range(count):
                lo = dz[:, 256 * k : 256 * k + 128]
                hi = dz[:, 256 * k + 128 : 256 * k + 256]
                to = slice(128 * (first + k), 128 * (first + k) + 128)
                gs_ref[spots[0], to] = lo[:128] + hi[128:]
                gt_ref[spots[0], to] = hi[:128] + lo[128:]
            first += count
        return carry

    lax.fori_loop(0, half // 128, layer, 0)
    out_ref[...] = jnp.zeros(out_ref.shape, BF16)

    def unlift(p, carry):
        at = pl.multiple_of(p * 24, 8)
        s = own_ref[2 * p + 1]
        out_ref[s] = out_ref[s] + turn_back(vs_ref, p, gs_ref, at)
        t = own_ref[2 * p]
        out_ref[t] = out_ref[t] + turn_back(vt_ref, p, gt_ref, at)
        return carry

    lax.fori_loop(0, pairs, unlift, 0)

    def put_rows(row, value):
        wg_ref[row : row + value.shape[0], :] = (value * scale).astype(BF16)

    wg_ref[8064:8192, :] = jnp.zeros((128, 128), BF16)

    def plain(left_ref, left_at, height, right_ref, right_cols, row):
        for c in range(height // 128):
            g = dot_tn(left_ref[:, left_at + 128 * c : left_at + 128 * c + 128], right_ref[:, right_cols])
            for n in range(g.shape[1] // 128):
                put_rows(row + n * height + 128 * c, g[:, 128 * n : 128 * n + 128])

    def folded(left_ref, left_at, height, right_ref, right_cols, row):
        width = (right_cols.stop - right_cols.start) // 2
        blocks = width // 128
        for c in range(height // 128):
            low = left_at + 128 * c
            top = dot_tn(left_ref[:, low : low + 128], right_ref[:, right_cols])
            bot = dot_tn(left_ref[:, low + height : low + height + 128], right_ref[:, right_cols])
            same = top[:, :width] + bot[:, width:]
            cross = top[:, width:] - bot[:, :width]
            for n in range(blocks):
                cols = slice(128 * n, 128 * n + 128)
                put_rows(row + n * height + 128 * c, same[:, cols])
                put_rows(row + (blocks + n) * height + 128 * c, cross[:, cols])

    plain(z_ref, 0, 768, dd_ref, slice(0, 512), 0)
    folded(z_ref, 768, 512, dd_ref, slice(512, 1024), 3072)
    folded(z_ref, 1792, 256, dd_ref, slice(1024, 1280), 5120)
    plain(act_ref, 0, 384, dmix_ref, slice(0, 384), 5632)
    folded(act_ref, 384, 256, dmix_ref, slice(384, 896), 6784)
    folded(act_ref, 896, 128, dmix_ref, slice(896, 1152), 7808)


def backward(owners, got, turns, weights, kept, scale):
    peers = got.shape[0]
    rows = kept[0].shape[0]

    def body(*refs):
        backward_body(*refs, scale=scale)

    return pl.pallas_call(
        body,
        in_specs=[SM] + [VM] * 15,
        out_specs=[VM, VM],
        out_shape=[
            jax.ShapeDtypeStruct((peers, GROUPS, 4, 128), BF16),
            jax.ShapeDtypeStruct((WEIGHT_ROWS, 128), BF16),
        ],
        scratch_shapes=[
            pltpu.VMEM((rows, 1152), BF16),
            pltpu.VMEM((rows, 1280), BF16),
            pltpu.VMEM((rows // 2, 1152), F32),
            pltpu.VMEM((rows // 2, 1152), F32),
        ],
        compiler_params=pltpu.CompilerParams(vmem_limit_bytes=VMEM_LIMIT),
        cost_estimate=pl.CostEstimate(flops=2 * 10**10, transcendentals=10**6, bytes_accessed=3 * 10**7),
        name="backward",
    )(owners, got, *turns, *weights, *kept)


def scatter_body(idx_ref, got_ref, out_ref, acc_ref, last_ref, *, first):
    @pl.when(pl.program_id(0) == 0)
    def _():
        acc_ref[...] = jnp.zeros(acc_ref.shape, F32)
        last_ref[...] = jnp.zeros(last_ref.shape, F32)

    atom = lax.broadcasted_iota(jnp.int32, (128, 256), 0)
    kinds = [
        jnp.where(jnp.broadcast_to(idx_ref[v : v + 1, :], (128, 256)) == atom, 1.0, 0.0).astype(BF16)
        for v in range(4)
    ]
    tiles = [got_ref[:, first + 4 * t : first + 4 * t + 4].reshape(256, 128) for t in range(6)]
    last = got_ref[:, first + 24 : first + 27]
    tiles.append(jnp.concatenate([last, jnp.zeros((16, 1, 4, 128), BF16)], axis=1).reshape(256, 128))
    acc_ref[...] += dot(kinds[0], jnp.concatenate(tiles, axis=1))
    spare = jnp.concatenate([jnp.concatenate([tiles[j], tiles[j + 3]], axis=1) for j in range(3)], axis=0)
    last_ref[...] += dot(jnp.concatenate(kinds[1:], axis=1), spare)

    @pl.when(pl.program_id(0) == pl.num_programs(0) - 1)
    def _():
        for k in range(7):
            out_ref[k] = acc_ref[:, 128 * k : 128 * k + 128].astype(out_ref.dtype)
        for k in range(2):
            out_ref[7 + k] = last_ref[:, 128 * k : 128 * k + 128].astype(out_ref.dtype)


def add_rows(idx_rows, got, dtype):
    peers, groups = got.shape[:2]

    def body(*refs):
        scatter_body(*refs, first=groups - GROUPS)

    return pl.pallas_call(
        body,
        grid=(peers // 16,),
        in_specs=[
            pl.BlockSpec((8, 256), lambda c: (0, c)),
            pl.BlockSpec((16, groups, 4, 128), lambda c: (c, 0, 0, 0)),
        ],
        out_specs=whole((9, 128, 128)),
        out_shape=jax.ShapeDtypeStruct((9, 128, 128), dtype),
        scratch_shapes=[pltpu.VMEM((128, 896), F32), pltpu.VMEM((128, 256), F32)],
        cost_estimate=pl.CostEstimate(flops=10**9, transcendentals=0, bytes_accessed=6 * 10**6),
        name="add_rows",
    )(idx_rows, got)


def swapped(x):
    return lax.ppermute(x, "atoms", [(i, i ^ 1) for i in range(lax.axis_size("atoms"))])


def add_pair(core, grads, other):
    half = other.shape[0]

    def body(core_ref, grads_ref, other_ref, out_ref):
        mine = grads_ref[pl.ds(pl.multiple_of(core_ref[0] * half, 16), half), :]
        total = mine.astype(F32) + other_ref[...].astype(F32)
        out_ref[...] = total.astype(BF16).reshape(half // WR, WR // 4, 4, 128)

    return pl.pallas_call(
        body,
        in_specs=[SM, VM, VM],
        out_specs=VM,
        out_shape=jax.ShapeDtypeStruct((half // WR, WR // 4, 4, 128), BF16),
        cost_estimate=pl.CostEstimate(flops=10**6, transcendentals=0, bytes_accessed=4 * 10**6),
        name="add_pair",
    )(core, grads, other)


def add_peers(got):
    peers = got.shape[0]
    chips = peers // 2

    def body(got_ref, out_ref):
        x = got_ref[...].reshape(peers, 16, 128).astype(F32).reshape(chips, 2, 16, 128)
        total = jnp.sum(x, axis=0).astype(BF16)
        out_ref[...] = jnp.broadcast_to(total[None], (chips, 2, 16, 128))

    return pl.pallas_call(
        body,
        grid=(WR // 16,),
        in_specs=[pl.BlockSpec((peers, 4, 4, 128), lambda i: (0, i, 0, 0))],
        out_specs=pl.BlockSpec((chips, 2, 16, 128), lambda i: (0, 0, i, 0)),
        out_shape=jax.ShapeDtypeStruct((chips, 2, WR, 128), BF16),
        compiler_params=pltpu.CompilerParams(vmem_limit_bytes=VMEM_LIMIT // 2),
        cost_estimate=pl.CostEstimate(flops=10**6, transcendentals=0, bytes_accessed=3 * 10**6),
        name="add_peers",
    )(got)


WEIGHT_PARTS = (
    (0, 1, 768, 4), (3072, 2, 512, 2), (5120, 2, 256, 1), (5632, 1, 384, 3), (6784, 2, 256, 2), (7808, 2, 128, 1),
)


def unpack(core, mine, other):
    chips = mine.shape[0]

    shapes = [(parts, height, 128 * blocks) for _, parts, height, blocks in WEIGHT_PARTS]

    def body(core_ref, mine_ref, other_ref, *refs):
        outs, held, sem = refs[:6], refs[6:12], refs[12]
        copies = []
        for i, (row, parts, height, blocks) in enumerate(WEIGHT_PARTS):
            for p in range(parts):
                for n in range(blocks):
                    cols = slice(128 * n, 128 * n + 128)
                    for at in range(0, height, 2 * WR):
                        half, chip = divmod((row + (p * blocks + n) * height + at) // (2 * WR), chips)
                        low = pl.multiple_of(at + WR * core_ref[0], WR)
                        held[i][p, pl.ds(low, WR), cols] = mine_ref[chip, half].astype(F32)
                        low = pl.multiple_of(at + WR * (1 - core_ref[0]), WR)
                        held[i][p, pl.ds(low, WR), cols] = other_ref[chip, half].astype(F32)
            copies.append(pltpu.make_async_copy(held[i], outs[i], sem.at[i]))
            copies[-1].start()
        for copy in copies:
            copy.wait()

    return pl.pallas_call(
        body,
        in_specs=[SM, VM, VM],
        out_specs=[pl.BlockSpec(memory_space=pl.ANY)] * 6,
        out_shape=[jax.ShapeDtypeStruct(shape, F32) for shape in shapes],
        scratch_shapes=[pltpu.VMEM(shape, F32) for shape in shapes] + [pltpu.SemaphoreType.DMA((6,))],
        compiler_params=pltpu.CompilerParams(vmem_limit_bytes=VMEM_LIMIT // 2),
        cost_estimate=pl.CostEstimate(flops=10**6, transcendentals=0, bytes_accessed=6 * 10**6),
        name="unpack",
    )(core, mine, other)


def widen_pair(w):
    upper = jnp.concatenate([w[0], w[1]], axis=1)
    lower = jnp.concatenate([-w[1], w[0]], axis=1)
    return jnp.concatenate([upper, lower], axis=0)


def exchange(x):
    return lax.all_to_all(x, "atoms", split_axis=0, concat_axis=0, tiled=True)


def local(
    features, cotangent, wigner, pair_blocks, pair_rows, edge_ends,
    first_m0, first_m1, first_m2, second_m0, second_m1, second_m2,
):
    peers = lax.axis_size("atoms")
    pairs = pair_blocks.shape[0]
    edges = edge_ends.shape[1]
    each = edges // pairs
    owners = pair_blocks.reshape(2 * pairs)
    ends = jnp.arange(2 * pairs, dtype=jnp.int32)
    slots = jnp.sum(
        jnp.logical_and(owners[:, None] == owners[None, :], ends[:, None] > ends[None, :]), axis=1
    ).astype(jnp.int32)

    asked = exchange(
        request_rows(jnp.transpose(pair_blocks), jnp.transpose(pair_rows, (1, 0, 2)), peers)
    ).reshape(peers, 64)
    asked_rows = jnp.transpose(asked.reshape(peers, 4, 16), (1, 0, 2)).reshape(4, peers * 16)
    asked_rows = jnp.concatenate([asked_rows, asked_rows], axis=0)
    eye = jnp.eye(64, dtype=BF16)

    got_f = exchange(pick_rows(asked, eye, jnp.transpose(features, (1, 0, 2))))

    turned = jnp.stack([wigner[i] for i in COEF_ORDER]).reshape(9, 9, pairs, each)
    pos = jnp.stack(
        [
            (slots.reshape(pairs, 2)[:, side, None] * 6 + edge_ends[side].reshape(pairs, each)).astype(F32)
            for side in range(2)
        ],
        axis=0,
    )
    pos = jnp.broadcast_to(pos[:, None], (2, 9, pairs, each))
    by_j = jnp.transpose(turned, (1, 0, 2, 3))
    gap5 = jnp.zeros((5, 9, pairs, each), F32)
    gap7 = jnp.zeros((7, 9, pairs, each), F32)
    table = jnp.concatenate([by_j, pos, gap5, by_j, gap7], axis=0)
    ra = jnp.transpose(table, (2, 1, 3, 0)).reshape(pairs, 9 * each, 32)
    ra = jnp.pad(ra, ((0, 0), (0, 224 - 9 * each), (0, 0)))
    rb = jnp.transpose(table, (2, 0, 1, 3)).reshape(pairs, 32, 9 * each)
    rb = jnp.pad(rb, ((0, 0), (0, 0), (0, 256 - 9 * each)))
    turns = build_turns(ra, rb)

    weights = (
        first_m0, widen_pair(first_m1), widen_pair(first_m2),
        second_m0, widen_pair(second_m1), widen_pair(second_m2),
    )
    picked_c = pick_rows(asked, eye, jnp.transpose(cotangent, (1, 0, 2)))
    picked_c, turns, weights = lax.optimization_barrier((picked_c, turns, weights))
    got_c = exchange(picked_c)
    back_m, *kept = forward(owners, got_f, turns, weights, 2 * edges)
    got_m = exchange(back_m)
    scale = float((2.0 * edges * peers) ** (-0.5))
    back_g, grads = backward(owners, got_c, turns, weights, kept, scale)
    core = (lax.axis_index("atoms") % 2).astype(jnp.int32)
    cores = jnp.stack([core, core])
    half = WEIGHT_ROWS // 2
    sent = lax.dynamic_slice_in_dim(grads, (1 - core) * half, half, axis=0)
    w_rows = add_pair(cores, grads, swapped(sent))
    both = jnp.concatenate([w_rows, back_g], axis=1)
    both, got_m = lax.optimization_barrier((both, got_m))
    messages = add_rows(asked_rows, got_m, BF16)
    got_g, messages = lax.optimization_barrier((exchange(both), messages))
    same_core = [list(range(c, peers, 2)) for c in range(2)]
    w_mine = lax.all_to_all(
        add_peers(got_g).reshape(peers // 2, 2 * WR, 128), "atoms",
        split_axis=0, concat_axis=0, tiled=True, axis_index_groups=same_core,
    ).reshape(peers // 2, 2, WR, 128)
    grad_features = add_rows(asked_rows, got_g, F32)
    w_mine, grad_features = lax.optimization_barrier((w_mine, grad_features))
    messages = jnp.transpose(messages, (1, 0, 2))
    grad_features = jnp.transpose(grad_features, (1, 0, 2))
    w = unpack(cores, w_mine, swapped(w_mine))
    return (messages, grad_features, w[0][0], w[1], w[2], w[3][0], w[4], w[5])


def solution(mesh):
    rows = P("atoms", None, None)
    in_specs = (
        rows, rows, P(None, None, "atoms"), P("atoms", None), P(None, None, "atoms"), P(None, "atoms"),
        P(), P(), P(), P(), P(), P(),
    )
    out_specs = (rows, rows, P(), P(), P(), P(), P(), P())
    return jax.shard_map(local, mesh=mesh, in_specs=in_specs, out_specs=out_specs, check_vma=False)
```

```python
import jax
import jax.numpy as jnp
import numpy as np
from jax import lax
from jax.experimental import pallas as pl
from jax.experimental.pallas import tpu as pltpu
from jax.sharding import PartitionSpec as P

COEF_ORDER = (0, 2, 6, 3, 7, 1, 5, 8, 4)
F32 = jnp.float32
BF16 = jnp.bfloat16
CH = 112
GROUPS = 27
WEIGHT_ROWS = 8192
WR = 32
PICK = 64
VMEM_LIMIT = 58 * 1024 * 1024


def chunk_maps():
    coef = np.full((CH,), -1)
    row = np.full((CH,), -1)
    for line in range(CH):
        tile, at = divmod(line, 16)
        if at < 12:
            coef[line], row[line] = tile, at
        elif tile < 6:
            coef[line], row[line] = 7 + tile // 3, 4 * (tile % 3) + at - 12
    return coef, row


def spread_tables():
    coef, row = chunk_maps()
    spread = np.zeros((32, 256), np.float32)
    rows = np.full((256,), -1.0, np.float32)
    for half in range(2):
        for line in range(CH):
            if coef[line] >= 0:
                spread[16 * half + coef[line], CH * half + line] = 1.0
                rows[CH * half + line] = row[line]
    return spread, rows


def request_columns():
    cols = np.full((64,), -1)
    cols[:12] = np.arange(12)
    for j in range(3):
        cols[16 * (j + 1) + 12 : 16 * (j + 2)] = 4 * j + np.arange(4)
    return cols


def dot(a, b):
    return jnp.dot(a, b, preferred_element_type=F32)


def dot_nt(a, b):
    return lax.dot_general(a, b, (((1,), (1,)), ((), ())), preferred_element_type=F32)


def dot_tn(a, b):
    return lax.dot_general(a, b, (((0,), (0,)), ((), ())), preferred_element_type=F32)


def whole(shape):
    return pl.BlockSpec(shape, lambda *_: (0,) * len(shape))


VM = pl.BlockSpec(memory_space=pltpu.VMEM)
SM = pl.BlockSpec(memory_space=pltpu.SMEM)


def gather_body(idx_ref, eye_ref, right_ref, six_ref, out_ref):
    turned = dot_nt(eye_ref[...], idx_ref[...].astype(F32).astype(BF16))
    lane = lax.broadcasted_iota(jnp.int32, (64, 128), 1).astype(F32)
    picks = []
    for q in range(PICK):
        col = jnp.broadcast_to(turned[:, q : q + 1], (64, 128))
        picks.append(jnp.where(col == lane, 1.0, 0.0).astype(BF16))
    kinds = [jnp.concatenate([x[16 * v : 16 * v + 16] for x in picks], axis=0) for v in range(4)]
    for j in range(3):
        left = jnp.concatenate([kinds[0], kinds[j + 1]], axis=1)
        got = dot(left, right_ref[j]).astype(BF16)
        out_ref[:, 4 * j : 4 * j + 4] = got[:, :128].reshape(PICK, 4, 4, 128)
        out_ref[:, 4 * (j + 3) : 4 * (j + 4)] = got[:, 128:].reshape(PICK, 4, 4, 128)
    last = dot(kinds[0], six_ref[...]).astype(BF16)
    out_ref[:, 24:27] = last.reshape(PICK, 4, 4, 128)[:, :3]


def request_body(blocks_ref, rows_ref, cols_ref, out_ref, seen_ref):
    peers, ends = out_ref.shape[0], 2 * blocks_ref.shape[1]
    out_ref[...] = jnp.full(out_ref.shape, -1, jnp.int32)

    def clear(o, carry):
        seen_ref[o] = 0
        return carry

    lax.fori_loop(0, peers, clear, 0, unroll=8)
    cols = cols_ref[...]
    for end in range(ends):
        pair, side = divmod(end, 2)
        owner = blocks_ref[side, pair]
        slot = seen_ref[owner]
        seen_ref[owner] = slot + 1
        line = out_ref[owner]
        for k in range(6):
            line = jnp.where(cols == 6 * slot + k, rows_ref[k, side, pair], line)
        out_ref[owner] = line


def request_rows(blocks, rows, peers):
    cols = jnp.asarray(request_columns()[None], jnp.int32)
    return pl.pallas_call(
        request_body,
        in_specs=[SM, SM, VM],
        out_specs=VM,
        out_shape=jax.ShapeDtypeStruct((peers, 1, 64), jnp.int32),
        scratch_shapes=[pltpu.SMEM((peers,), jnp.int32)],
        name="request_rows",
    )(blocks, rows, cols)


def stacked(block):
    feat = jnp.transpose(block, (1, 0, 2))
    upper = jnp.concatenate([feat[0:3], feat[3:6]], axis=2)
    lower = jnp.broadcast_to(jnp.concatenate([feat[7:8], feat[8:9]], axis=2), upper.shape)
    return jnp.concatenate([upper, lower], axis=1), feat[6]


def pick_rows(idx, eye, right, six):
    peers = idx.shape[0]
    return pl.pallas_call(
        gather_body,
        grid=(peers // PICK,),
        in_specs=[
            pl.BlockSpec((PICK, 64), lambda c: (c, 0)),
            whole((64, 64)),
            whole((3, 256, 256)),
            whole((128, 128)),
        ],
        out_specs=pl.BlockSpec((PICK, GROUPS, 4, 128), lambda c: (c, 0, 0, 0)),
        out_shape=jax.ShapeDtypeStruct((peers, GROUPS, 4, 128), BF16),
        compiler_params=pltpu.CompilerParams(vmem_limit_bytes=VMEM_LIMIT // 2),
        cost_estimate=pl.CostEstimate(flops=2 * 10**9, transcendentals=0, bytes_accessed=4 * 10**6),
        name="pick_rows",
    )(idx, eye, right, six)


def prep_body(ra_ref, rb_ref, sp_ref, spt_ref, rows_ref, rowst_ref, wt_ref, ws_ref, vt_ref, vs_ref):
    a = ra_ref[0]
    a_hi = a.astype(BF16)
    a_lo = (a - a_hi.astype(F32)).astype(BF16)
    lane = lax.broadcasted_iota(jnp.int32, (224, 32), 1)
    a_both = jnp.where(lane < 16, a_hi.astype(F32), a_lo.astype(F32)).astype(BF16)
    x = dot(a_both, sp_ref[...])
    rows = jnp.broadcast_to(rows_ref[0:1, :], (224, 256))
    for at, out in ((9, wt_ref), (10, ws_ref)):
        mine = jnp.broadcast_to(a[:, at : at + 1], (224, 256))
        out[0] = jnp.where(mine == rows, x, 0.0).astype(BF16)
    b = rb_ref[0]
    b_hi = b.astype(BF16)
    b_lo = (b - b_hi.astype(F32)).astype(BF16)
    line = lax.broadcasted_iota(jnp.int32, (32, 256), 0)
    b_both = jnp.where(line < 16, b_hi.astype(F32), b_lo.astype(F32)).astype(BF16)
    y = dot(spt_ref[...], b_both)
    rowst = jnp.broadcast_to(rowst_ref[:, 0:1], (224, 256))
    for at, out in ((9, vt_ref), (10, vs_ref)):
        mine = jnp.broadcast_to(b[at : at + 1, :], (224, 256))
        out[0] = jnp.where(mine == rowst, y, 0.0).astype(BF16)


def build_turns(ra, rb):
    pairs = ra.shape[0]
    spread, rows = spread_tables()
    sp = jnp.asarray(spread, BF16)
    spt = jnp.asarray(spread[:, :224].T, BF16)
    rows8 = jnp.asarray(np.tile(rows[None], (8, 1)), F32)
    rowst = jnp.asarray(np.tile(rows[:224, None], (1, 128)), F32)
    one = jax.ShapeDtypeStruct((pairs, 224, 256), BF16)
    block = pl.BlockSpec((1, 224, 256), lambda p: (p, 0, 0))
    return pl.pallas_call(
        prep_body,
        grid=(pairs,),
        in_specs=[
            pl.BlockSpec((1, 224, 32), lambda p: (p, 0, 0)),
            pl.BlockSpec((1, 32, 256), lambda p: (p, 0, 0)),
            whole((32, 256)),
            whole((224, 32)),
            whole((8, 256)),
            whole((224, 128)),
        ],
        out_specs=[block] * 4,
        out_shape=[one] * 4,
        cost_estimate=pl.CostEstimate(flops=10**9, transcendentals=0, bytes_accessed=10**7),
        name="build_turns",
    )(ra, rb, sp, spt, rows8, rowst)


def turn(w_ref, r_ref, pair, owner):
    groups = r_ref[owner]
    last = jnp.concatenate([groups[24:27], jnp.zeros((1, 4, 128), BF16)], axis=0).reshape(16, 128)
    chunk = jnp.concatenate([groups[:24].reshape(96, 128), last], axis=0)
    right = jnp.concatenate([chunk, chunk, jnp.zeros((32, 128), BF16)], axis=0)
    return dot(w_ref[pair], right)


def turn_back(v_ref, pair, src_ref, base):
    parts = [src_ref[pl.ds(base, 24), 128 * k : 128 * k + 128] for k in range(9)]
    x = jnp.concatenate(parts + [jnp.zeros((40, 128), F32)], axis=0)
    hi = x.astype(BF16)
    lo = (x - hi.astype(F32)).astype(BF16)
    y = dot(v_ref[pair], jnp.concatenate([hi, lo], axis=1))
    y = y[:, :128] + y[:, 128:]
    y = (y[:CH] + y[CH:]).astype(BF16)
    return y.reshape(GROUPS + 1, 4, 128)[:GROUPS]


def forward_body(
    own_ref, r_ref, wt_ref, ws_ref, vt_ref, vs_ref, a0_ref, a1_ref, a2_ref, b0_ref, b1_ref, b2_ref,
    out_ref, z_ref, hid_ref, gate_ref, act_ref, mix_ref,
):
    half = z_ref.shape[0] // 2
    pairs = wt_ref.shape[0]

    def lift(d, carry):
        turned = []
        for p in (2 * d, 2 * d + 1):
            turned.append((turn(ws_ref, r_ref, p, own_ref[2 * p + 1]), turn(wt_ref, r_ref, p, own_ref[2 * p])))
        (s0, t0), (s1, t1) = turned
        at = pl.multiple_of(d * 48, 16)
        for k in range(9):
            lines = slice(24 * k, 24 * k + 24)
            s = jnp.concatenate([s0[lines], s1[lines]], axis=0).astype(BF16)
            t = jnp.concatenate([t0[lines], t1[lines]], axis=0).astype(BF16)
            z_ref[pl.ds(at, 48), 256 * k : 256 * k + 128] = s
            z_ref[pl.ds(at, 48), 256 * k + 128 : 256 * k + 256] = t
            z_ref[pl.ds(half + at, 48), 256 * k : 256 * k + 128] = t
            z_ref[pl.ds(half + at, 48), 256 * k + 128 : 256 * k + 256] = s
        return carry

    lax.fori_loop(0, pairs // 2, lift, 0)

    def layer(b, carry):
        at = pl.multiple_of(b * 256, 256)
        here = pl.ds(at, 256)
        o = dot(z_ref[here, 0:768], a0_ref[...])
        gate = jax.nn.sigmoid(o[:, 384:512])
        gate_ref[here, :] = gate
        h0 = o[:, 0:128]
        hid_ref[here, 0:384] = o[:, 0:384]
        act_ref[here, 0:128] = (h0 * jax.nn.sigmoid(h0)).astype(BF16)
        for k in range(1, 3):
            cols = slice(128 * k, 128 * k + 128)
            act_ref[here, cols] = (o[:, cols] * gate).astype(BF16)
        h1 = dot(z_ref[here, 768:1792], a1_ref[...])
        hid_ref[here, 384:896] = h1
        for k in range(4):
            act_ref[here, 384 + 128 * k : 512 + 128 * k] = (h1[:, 128 * k : 128 * k + 128] * gate).astype(BF16)
        h2 = dot(z_ref[here, 1792:2304], a2_ref[...])
        hid_ref[here, 896:1152] = h2
        for k in range(2):
            act_ref[here, 896 + 128 * k : 1024 + 128 * k] = (h2[:, 128 * k : 128 * k + 128] * gate).astype(BF16)
        mix_ref[here, 0:384] = dot(act_ref[here, 0:384], b0_ref[...])
        mix_ref[here, 384:896] = dot(act_ref[here, 384:896], b1_ref[...])
        mix_ref[here, 896:1152] = dot(act_ref[here, 896:1152], b2_ref[...])
        return carry

    lax.fori_loop(0, z_ref.shape[0] // 256, layer, 0)
    out_ref[...] = jnp.zeros(out_ref.shape, BF16)

    def unlift(p, carry):
        at = pl.multiple_of(p * 24, 8)
        t = own_ref[2 * p]
        out_ref[t] = out_ref[t] + turn_back(vt_ref, p, mix_ref, at)
        s = own_ref[2 * p + 1]
        out_ref[s] = out_ref[s] + turn_back(vs_ref, p, mix_ref, half + at)
        return carry

    lax.fori_loop(0, pairs, unlift, 0)


def forward(owners, got, turns, weights, rows):
    peers = got.shape[0]
    return pl.pallas_call(
        forward_body,
        in_specs=[SM] + [VM] * 11,
        out_specs=[VM] * 5,
        out_shape=[
            jax.ShapeDtypeStruct((peers, GROUPS, 4, 128), BF16),
            jax.ShapeDtypeStruct((rows, 2304), BF16),
            jax.ShapeDtypeStruct((rows, 1152), F32),
            jax.ShapeDtypeStruct((rows, 128), F32),
            jax.ShapeDtypeStruct((rows, 1152), BF16),
        ],
        scratch_shapes=[pltpu.VMEM((rows, 1152), F32)],
        compiler_params=pltpu.CompilerParams(vmem_limit_bytes=VMEM_LIMIT),
        cost_estimate=pl.CostEstimate(flops=10**10, transcendentals=10**6, bytes_accessed=3 * 10**7),
        name="forward",
    )(owners, got, *turns, *weights)


def backward_body(
    own_ref, r_ref, wt_ref, ws_ref, vt_ref, vs_ref, a0_ref, a1_ref, a2_ref, b0_ref, b1_ref, b2_ref,
    z_ref, hid_ref, gate_ref, act_ref, out_ref, wg_ref, dmix_ref, dd_ref, gs_ref, gt_ref, *, scale,
):
    half = z_ref.shape[0] // 2
    pairs = wt_ref.shape[0]

    def lift(d, carry):
        turned = []
        for p in (2 * d, 2 * d + 1):
            turned.append((turn(wt_ref, r_ref, p, own_ref[2 * p]), turn(ws_ref, r_ref, p, own_ref[2 * p + 1])))
        (t0, s0), (t1, s1) = turned
        at = pl.multiple_of(d * 48, 16)
        for k in range(9):
            lines = slice(24 * k, 24 * k + 24)
            cols = slice(128 * k, 128 * k + 128)
            dmix_ref[pl.ds(at, 48), cols] = jnp.concatenate([t0[lines], t1[lines]], axis=0).astype(BF16)
            dmix_ref[pl.ds(half + at, 48), cols] = jnp.concatenate([s0[lines], s1[lines]], axis=0).astype(BF16)
        return carry

    lax.fori_loop(0, pairs // 2, lift, 0)

    def layer(b, carry):
        at = pl.multiple_of(b * 128, 128)
        spots = (pl.ds(at, 128), pl.ds(half + at, 128))

        def rows_of(ref, cols):
            return jnp.concatenate([ref[spot, cols] for spot in spots], axis=0)

        def put(col, value):
            value = value.astype(BF16)
            for i, spot in enumerate(spots):
                dd_ref[spot, col : col + 128] = value[128 * i : 128 * i + 128]

        gate = rows_of(gate_ref, slice(0, 128))
        dact0 = dot_nt(rows_of(dmix_ref, slice(0, 384)), b0_ref[...])
        h0 = rows_of(hid_ref, slice(0, 128))
        head = jax.nn.sigmoid(h0)
        put(0, dact0[:, 0:128] * head * (1.0 + h0 * (1.0 - head)))
        total = None

        def gated(k, piece, col):
            put(col, piece * gate)
            return piece * rows_of(hid_ref, slice(128 * k, 128 * k + 128))

        total = gated(1, dact0[:, 128:256], 128) + gated(2, dact0[:, 256:384], 256)
        dact1 = dot_nt(rows_of(dmix_ref, slice(384, 896)), b1_ref[...])
        for k in range(4):
            total = total + gated(3 + k, dact1[:, 128 * k : 128 * k + 128], 512 + 128 * k)
        dact2 = dot_nt(rows_of(dmix_ref, slice(896, 1152)), b2_ref[...])
        for k in range(2):
            total = total + gated(7 + k, dact2[:, 128 * k : 128 * k + 128], 1024 + 128 * k)
        put(384, total * gate * (1.0 - gate))

        first = 0
        for cols, w_ref, count in ((slice(0, 512), a0_ref, 3), (slice(512, 1024), a1_ref, 4), (slice(1024, 1280), a2_ref, 2)):
            dz = dot_nt(rows_of(dd_ref, cols), w_ref[...])
            for k in range(count):
                lo = dz[:, 256 * k : 256 * k + 128]
                hi = dz[:, 256 * k + 128 : 256 * k + 256]
                to = slice(128 * (first + k), 128 * (first + k) + 128)
                gs_ref[spots[0], to] = lo[:128] + hi[128:]
                gt_ref[spots[0], to] = hi[:128] + lo[128:]
            first += count
        return carry

    lax.fori_loop(0, half // 128, layer, 0)
    out_ref[...] = jnp.zeros(out_ref.shape, BF16)

    def unlift(p, carry):
        at = pl.multiple_of(p * 24, 8)
        s = own_ref[2 * p + 1]
        out_ref[s] = out_ref[s] + turn_back(vs_ref, p, gs_ref, at)
        t = own_ref[2 * p]
        out_ref[t] = out_ref[t] + turn_back(vt_ref, p, gt_ref, at)
        return carry

    lax.fori_loop(0, pairs, unlift, 0)

    def put_rows(row, value):
        wg_ref[row : row + value.shape[0], :] = (value * scale).astype(BF16)

    wg_ref[8064:8192, :] = jnp.zeros((128, 128), BF16)

    def plain(left_ref, left_at, height, right_ref, right_cols, row):
        for c in range(height // 128):
            g = dot_tn(left_ref[:, left_at + 128 * c : left_at + 128 * c + 128], right_ref[:, right_cols])
            for n in range(g.shape[1] // 128):
                put_rows(row + n * height + 128 * c, g[:, 128 * n : 128 * n + 128])

    def folded(left_ref, left_at, height, right_ref, right_cols, row):
        width = (right_cols.stop - right_cols.start) // 2
        blocks = width // 128
        for c in range(height // 128):
            low = left_at + 128 * c
            top = dot_tn(left_ref[:, low : low + 128], right_ref[:, right_cols])
            bot = dot_tn(left_ref[:, low + height : low + height + 128], right_ref[:, right_cols])
            same = top[:, :width] + bot[:, width:]
            cross = top[:, width:] - bot[:, :width]
            for n in range(blocks):
                cols = slice(128 * n, 128 * n + 128)
                put_rows(row + n * height + 128 * c, same[:, cols])
                put_rows(row + (blocks + n) * height + 128 * c, cross[:, cols])

    plain(z_ref, 0, 768, dd_ref, slice(0, 512), 0)
    folded(z_ref, 768, 512, dd_ref, slice(512, 1024), 3072)
    folded(z_ref, 1792, 256, dd_ref, slice(1024, 1280), 5120)
    plain(act_ref, 0, 384, dmix_ref, slice(0, 384), 5632)
    folded(act_ref, 384, 256, dmix_ref, slice(384, 896), 6784)
    folded(act_ref, 896, 128, dmix_ref, slice(896, 1152), 7808)


def backward(owners, got, turns, weights, kept, scale):
    peers = got.shape[0]
    rows = kept[0].shape[0]

    def body(*refs):
        backward_body(*refs, scale=scale)

    return pl.pallas_call(
        body,
        in_specs=[SM] + [VM] * 15,
        out_specs=[VM, VM],
        out_shape=[
            jax.ShapeDtypeStruct((peers, GROUPS, 4, 128), BF16),
            jax.ShapeDtypeStruct((WEIGHT_ROWS, 128), BF16),
        ],
        scratch_shapes=[
            pltpu.VMEM((rows, 1152), BF16),
            pltpu.VMEM((rows, 1280), BF16),
            pltpu.VMEM((rows // 2, 1152), F32),
            pltpu.VMEM((rows // 2, 1152), F32),
        ],
        compiler_params=pltpu.CompilerParams(vmem_limit_bytes=VMEM_LIMIT),
        cost_estimate=pl.CostEstimate(flops=2 * 10**10, transcendentals=10**6, bytes_accessed=3 * 10**7),
        name="backward",
    )(owners, got, *turns, *weights, *kept)


def scatter_body(idx_ref, got_ref, out_ref, acc_ref, last_ref, *, first):
    @pl.when(pl.program_id(0) == 0)
    def _():
        acc_ref[...] = jnp.zeros(acc_ref.shape, F32)
        last_ref[...] = jnp.zeros(last_ref.shape, F32)

    atom = lax.broadcasted_iota(jnp.int32, (128, 256), 0)
    kinds = [
        jnp.where(jnp.broadcast_to(idx_ref[v : v + 1, :], (128, 256)) == atom, 1.0, 0.0).astype(BF16)
        for v in range(4)
    ]
    tiles = [got_ref[:, first + 4 * t : first + 4 * t + 4].reshape(256, 128) for t in range(6)]
    last = got_ref[:, first + 24 : first + 27]
    tiles.append(jnp.concatenate([last, jnp.zeros((16, 1, 4, 128), BF16)], axis=1).reshape(256, 128))
    acc_ref[...] += dot(kinds[0], jnp.concatenate(tiles, axis=1))
    spare = jnp.concatenate([jnp.concatenate([tiles[j], tiles[j + 3]], axis=1) for j in range(3)], axis=0)
    last_ref[...] += dot(jnp.concatenate(kinds[1:], axis=1), spare)

    @pl.when(pl.program_id(0) == pl.num_programs(0) - 1)
    def _():
        for k in range(7):
            out_ref[k] = acc_ref[:, 128 * k : 128 * k + 128].astype(out_ref.dtype)
        for k in range(2):
            out_ref[7 + k] = last_ref[:, 128 * k : 128 * k + 128].astype(out_ref.dtype)


def add_rows(idx_rows, got, dtype):
    peers, groups = got.shape[:2]

    def body(*refs):
        scatter_body(*refs, first=groups - GROUPS)

    return pl.pallas_call(
        body,
        grid=(peers // 16,),
        in_specs=[
            pl.BlockSpec((8, 256), lambda c: (0, c)),
            pl.BlockSpec((16, groups, 4, 128), lambda c: (c, 0, 0, 0)),
        ],
        out_specs=whole((9, 128, 128)),
        out_shape=jax.ShapeDtypeStruct((9, 128, 128), dtype),
        scratch_shapes=[pltpu.VMEM((128, 896), F32), pltpu.VMEM((128, 256), F32)],
        cost_estimate=pl.CostEstimate(flops=10**9, transcendentals=0, bytes_accessed=6 * 10**6),
        name="add_rows",
    )(idx_rows, got)


def swapped(x):
    return lax.ppermute(x, "atoms", [(i, i ^ 1) for i in range(lax.axis_size("atoms"))])


def add_pair(core, grads, other):
    half = other.shape[0]

    def body(core_ref, grads_ref, other_ref, out_ref):
        mine = grads_ref[pl.ds(pl.multiple_of(core_ref[0] * half, 16), half), :]
        total = mine.astype(F32) + other_ref[...].astype(F32)
        out_ref[...] = total.astype(BF16).reshape(half // WR, WR // 4, 4, 128)

    return pl.pallas_call(
        body,
        in_specs=[SM, VM, VM],
        out_specs=VM,
        out_shape=jax.ShapeDtypeStruct((half // WR, WR // 4, 4, 128), BF16),
        cost_estimate=pl.CostEstimate(flops=10**6, transcendentals=0, bytes_accessed=4 * 10**6),
        name="add_pair",
    )(core, grads, other)


def add_peers(got):
    peers = got.shape[0]
    chips = peers // 2

    def body(got_ref, out_ref):
        x = got_ref[...].reshape(peers, 16, 128).astype(F32).reshape(chips, 2, 16, 128)
        total = jnp.sum(x, axis=0).astype(BF16)
        out_ref[...] = jnp.broadcast_to(total[None], (chips, 2, 16, 128))

    return pl.pallas_call(
        body,
        grid=(WR // 16,),
        in_specs=[pl.BlockSpec((peers, 4, 4, 128), lambda i: (0, i, 0, 0))],
        out_specs=pl.BlockSpec((chips, 2, 16, 128), lambda i: (0, 0, i, 0)),
        out_shape=jax.ShapeDtypeStruct((chips, 2, WR, 128), BF16),
        compiler_params=pltpu.CompilerParams(vmem_limit_bytes=VMEM_LIMIT // 2),
        cost_estimate=pl.CostEstimate(flops=10**6, transcendentals=0, bytes_accessed=3 * 10**6),
        name="add_peers",
    )(got)


WEIGHT_PARTS = (
    (0, 1, 768, 4), (3072, 2, 512, 2), (5120, 2, 256, 1), (5632, 1, 384, 3), (6784, 2, 256, 2), (7808, 2, 128, 1),
)


def unpack(core, mine, other):
    chips = mine.shape[0]

    shapes = [(parts, height, 128 * blocks) for _, parts, height, blocks in WEIGHT_PARTS]

    def body(core_ref, mine_ref, other_ref, *refs):
        outs, held, sem = refs[:6], refs[6:12], refs[12]
        copies = []
        for i, (row, parts, height, blocks) in enumerate(WEIGHT_PARTS):
            for p in range(parts):
                for n in range(blocks):
                    cols = slice(128 * n, 128 * n + 128)
                    for at in range(0, height, 2 * WR):
                        half, chip = divmod((row + (p * blocks + n) * height + at) // (2 * WR), chips)
                        low = pl.multiple_of(at + WR * core_ref[0], WR)
                        held[i][p, pl.ds(low, WR), cols] = mine_ref[chip, half].astype(F32)
                        low = pl.multiple_of(at + WR * (1 - core_ref[0]), WR)
                        held[i][p, pl.ds(low, WR), cols] = other_ref[chip, half].astype(F32)
            copies.append(pltpu.make_async_copy(held[i], outs[i], sem.at[i]))
            copies[-1].start()
        for copy in copies:
            copy.wait()

    return pl.pallas_call(
        body,
        in_specs=[SM, VM, VM],
        out_specs=[pl.BlockSpec(memory_space=pl.ANY)] * 6,
        out_shape=[jax.ShapeDtypeStruct(shape, F32) for shape in shapes],
        scratch_shapes=[pltpu.VMEM(shape, F32) for shape in shapes] + [pltpu.SemaphoreType.DMA((6,))],
        compiler_params=pltpu.CompilerParams(vmem_limit_bytes=VMEM_LIMIT // 2),
        cost_estimate=pl.CostEstimate(flops=10**6, transcendentals=0, bytes_accessed=6 * 10**6),
        name="unpack",
    )(core, mine, other)


def widen_pair(w):
    upper = jnp.concatenate([w[0], w[1]], axis=1)
    lower = jnp.concatenate([-w[1], w[0]], axis=1)
    return jnp.concatenate([upper, lower], axis=0)


def exchange(x):
    return lax.all_to_all(x, "atoms", split_axis=0, concat_axis=0, tiled=True)


def local(
    features, cotangent, wigner, pair_blocks, pair_rows, edge_ends,
    first_m0, first_m1, first_m2, second_m0, second_m1, second_m2,
):
    peers = lax.axis_size("atoms")
    pairs = pair_blocks.shape[0]
    edges = edge_ends.shape[1]
    each = edges // pairs
    owners = pair_blocks.reshape(2 * pairs)
    ends = jnp.arange(2 * pairs, dtype=jnp.int32)
    slots = jnp.sum(
        jnp.logical_and(owners[:, None] == owners[None, :], ends[:, None] > ends[None, :]), axis=1
    ).astype(jnp.int32)

    asked = exchange(
        request_rows(jnp.transpose(pair_blocks), jnp.transpose(pair_rows, (1, 0, 2)), peers)
    ).reshape(peers, 64)
    asked_rows = jnp.transpose(asked.reshape(peers, 4, 16), (1, 0, 2)).reshape(4, peers * 16)
    asked_rows = jnp.concatenate([asked_rows, asked_rows], axis=0)
    eye = jnp.eye(64, dtype=BF16)

    got_f = exchange(pick_rows(asked, eye, *stacked(features)))

    turned = jnp.stack([wigner[i] for i in COEF_ORDER]).reshape(9, 9, pairs, each)
    pos = jnp.stack(
        [
            (slots.reshape(pairs, 2)[:, side, None] * 6 + edge_ends[side].reshape(pairs, each)).astype(F32)
            for side in range(2)
        ],
        axis=0,
    )
    pos = jnp.broadcast_to(pos[:, None], (2, 9, pairs, each))
    by_j = jnp.transpose(turned, (1, 0, 2, 3))
    gap5 = jnp.zeros((5, 9, pairs, each), F32)
    gap7 = jnp.zeros((7, 9, pairs, each), F32)
    table = jnp.concatenate([by_j, pos, gap5, by_j, gap7], axis=0)
    ra = jnp.transpose(table, (2, 1, 3, 0)).reshape(pairs, 9 * each, 32)
    ra = jnp.pad(ra, ((0, 0), (0, 224 - 9 * each), (0, 0)))
    rb = jnp.transpose(table, (2, 0, 1, 3)).reshape(pairs, 32, 9 * each)
    rb = jnp.pad(rb, ((0, 0), (0, 0), (0, 256 - 9 * each)))
    turns = build_turns(ra, rb)

    weights = (
        first_m0, widen_pair(first_m1), widen_pair(first_m2),
        second_m0, widen_pair(second_m1), widen_pair(second_m2),
    )
    picked_c = pick_rows(asked, eye, *stacked(cotangent))
    picked_c, turns, weights = lax.optimization_barrier((picked_c, turns, weights))
    got_c = exchange(picked_c)
    back_m, *kept = forward(owners, got_f, turns, weights, 2 * edges)
    got_m = exchange(back_m)
    scale = float((2.0 * edges * peers) ** (-0.5))
    back_g, grads = backward(owners, got_c, turns, weights, kept, scale)
    core = (lax.axis_index("atoms") % 2).astype(jnp.int32)
    cores = jnp.stack([core, core])
    half = WEIGHT_ROWS // 2
    sent = lax.dynamic_slice_in_dim(grads, (1 - core) * half, half, axis=0)
    w_rows = add_pair(cores, grads, swapped(sent))
    both = jnp.concatenate([w_rows, back_g], axis=1)
    both, got_m = lax.optimization_barrier((both, got_m))
    messages = add_rows(asked_rows, got_m, BF16)
    got_g, messages = lax.optimization_barrier((exchange(both), messages))
    same_core = [list(range(c, peers, 2)) for c in range(2)]
    w_mine = lax.all_to_all(
        add_peers(got_g).reshape(peers // 2, 2 * WR, 128), "atoms",
        split_axis=0, concat_axis=0, tiled=True, axis_index_groups=same_core,
    ).reshape(peers // 2, 2, WR, 128)
    grad_features = add_rows(asked_rows, got_g, F32)
    w_mine, grad_features = lax.optimization_barrier((w_mine, grad_features))
    messages = jnp.transpose(messages, (1, 0, 2))
    grad_features = jnp.transpose(grad_features, (1, 0, 2))
    w = unpack(cores, w_mine, swapped(w_mine))
    return (messages, grad_features, w[0][0], w[1], w[2], w[3][0], w[4], w[5])


def solution(mesh):
    rows = P("atoms", None, None)
    in_specs = (
        rows, rows, P(None, None, "atoms"), P("atoms", None), P(None, None, "atoms"), P(None, "atoms"),
        P(), P(), P(), P(), P(), P(),
    )
    out_specs = (rows, rows, P(), P(), P(), P(), P(), P())
    return jax.shard_map(local, mesh=mesh, in_specs=in_specs, out_specs=out_specs, check_vma=False)
```
